32 devices in a mesh: blk: 8 (over z, x), ulysses: 4 (over y, core).
Axes of the slice: x: 2, y: 2, z: 4, core: 2. Of those that a mesh axis runs over, the one named last changes fastest.
Arguments:
- tokens: bfloat16 [2, 2048, 768], P(None, ('blk', 'ulysses')), may hold values from -6 to 6
- attn_gain: bfloat16 [768], P(('blk', 'ulysses')), may hold values from 0.25 to 1.75
- qkv_weight: bfloat16 [768, 2304], P(('blk', 'ulysses')), may hold values from -0.3125 to 0.3125
- attn_out_weight: bfloat16 [768, 768], P(('blk', 'ulysses')), may hold values from -1.25 to 1.25
- mlp_gain: bfloat16 [768], P(('blk', 'ulysses')), may hold values from 0.25 to 1.75
- in_weight: bfloat16 [768, 2304], P(('blk', 'ulysses')), may hold values from -0.21875 to 0.21875
- out_weight: bfloat16 [1152, 768], P(None, ('blk', 'ulysses')), may hold values from -0.1875 to 0.1875
- cotangent: bfloat16 [2, 2048, 768], P(None, ('blk', 'ulysses')), may hold values from -6 to 6
Outputs:
- layer_output: bfloat16 [2, 2048, 768], P(None, ('blk', 'ulysses'))
- input_grad: bfloat16 [2, 2048, 768], P(None, ('blk', 'ulysses'))
- attn_gain_grad: float32 [768], P(('blk', 'ulysses'))
- qkv_weight_grad: float32 [768, 2304], P(('blk', 'ulysses'))
- attn_out_weight_grad: float32 [768, 768], P(('blk', 'ulysses'))
- mlp_gain_grad: float32 [768], P(('blk', 'ulysses'))
- in_weight_grad: float32 [768, 2304], P(('blk', 'ulysses'))
- out_weight_grad: float32 [1152, 768], P(None, ('blk', 'ulysses'))
The draws below stay inside these ranges and needn't reach their ends.
All inputs are finite; a program needn't handle non-finite values.
Results may differ from the reference program's by a relative error of at most 0.018.
The reference program's roundings to bfloat16 on the way count: a program that leaves them out, or rounds other values in their place, can miss the bound.
Values may be sent and summed in bfloat16 or wider, within the bound.
No kernel may reach another device: no remote copies, remote signals or barrier semaphores. Data moves between devices by JAX's collectives and lax.ppermute only.
A program may use at most 256 MiB of HBM per device.

```python
import jax
import jax.numpy as jnp
from jax import lax

D = 768
HEADS = 12
HEAD = 64
FF = 1152
SEQS = 2
LEN = 2048


def spiked(array, rng, source, target, parts, factor):
    def block_of(dim):
        return (jnp.arange(array.shape[dim]) // (array.shape[dim] // parts)).reshape((-1,) + (1,) * (array.ndim - 1 - dim))

    near = jax.random.permutation(rng, parts)[block_of(target)]
    far = (block_of(target) + parts // 2) % parts
    return jnp.where((block_of(source) == near) | (block_of(source) == far), factor * array, array)


def block_levels(own_key, dims, shards, smallest, largest):
    def one(dim, shards_of):
        draws = jax.random.uniform(jax.random.fold_in(jax.random.fold_in(own_key, 6), dim), (shards_of,), jnp.float32, smallest / len(shards), largest / len(shards))
        return jnp.repeat(jnp.exp(draws), dims[dim] // shards_of).reshape((-1,) + (1,) * (len(dims) - dim - 1))

    level = one(*shards[0])
    for cut in shards[1:]:
        level = level * one(*cut)
    return level


def gaussian(key, dims, deviation, bound, cuts=(), kind=jnp.bfloat16):
    entries = jax.random.normal(key, dims, jnp.float32) * deviation
    if len(cuts) > 0:
        entries = block_levels(key, dims, cuts, -0.22, 0.18) * entries
    return jnp.clip(entries, min=-bound, max=bound).astype(kind)


def heavy_noise(own_key, shape, width, most, pieces, heavy, kind=jnp.bfloat16):
    array = width * jax.random.normal(own_key, shape, jnp.float32)
    if pieces:
        array = array * block_levels(own_key, shape, pieces, -0.22, 0.18)
    return jnp.clip(spiked(array, jax.random.fold_in(own_key, 3), *heavy), -most, most).astype(kind)


def setup_inputs(seed: int = 0) -> dict:
    key_of = jax.random.split(jax.random.key(seed), 9)
    return {
        "tokens": gaussian(key_of[0], (SEQS, LEN, D), 1.0, 6.0, ((1, 32),)),
        "attn_gain": jnp.clip(1.0 + 0.15 * jax.random.normal(key_of[1], (D,), jnp.float32), 0.25, 1.75).astype(jnp.bfloat16),
        "qkv_weight": gaussian(key_of[2], (D, 3 * D), (D // 2) ** -0.5, 0.3125, ((0, 32),)),
        "attn_out_weight": gaussian(key_of[3], (D, D), (max(1, 55 * D // LEN)) ** -0.5, 1.25, ((0, 32),)),
        "mlp_gain": jnp.clip(1.0 + 0.15 * jax.random.normal(key_of[4], (D,), jnp.float32), 0.25, 1.75).astype(jnp.bfloat16),
        "in_weight": gaussian(key_of[5], (D, 2 * FF), D ** -0.5, 0.21875, ((0, 32),)),
        "out_weight": gaussian(key_of[6], (FF, D), FF ** -0.5, 0.1875, ((1, 32),)),
        "cotangent": heavy_noise(key_of[7], (SEQS, LEN, D), 1.0, 6.0, ((1, 32),), (1, 2, 32, 2.75)),
    }


EPSILON = 1e-05
THETA = 160000.0

@jax.custom_vjp
def low(v):
    return lax.optimization_barrier(v.astype(jnp.bfloat16)).astype(jnp.float32)

@jax.custom_vjp
def low_back(v):
    return v

def low_keep(v):
    return (low(v), None)

def low_pass(kept, grad):
    return (grad,)

def back_keep(v):
    return (v, None)

def back_low(kept, grad):
    return (low(grad),)
low.defvjp(low_keep, low_pass)
low_back.defvjp(back_keep, back_low)

def product(left, right):
    return jnp.dot(left, right, precision=lax.Precision.HIGHEST, preferred_element_type=jnp.float32)

def normalize(values):
    center = values - lax.optimization_barrier(jnp.mean(values, axis=-1, keepdims=True))
    inverse = lax.rsqrt(lax.optimization_barrier(jnp.mean(center * center, axis=-1, keepdims=True)) + EPSILON)
    return center * inverse

def rotation(first_row, row_count, head_width):
    half_width = head_width // 2
    frequency = THETA ** (-(jnp.arange(half_width, dtype=jnp.float32) * 2.0) / head_width)
    positions = (first_row + jnp.arange(row_count, dtype=jnp.int32)).astype(jnp.float32)
    angles = positions[:, None] * frequency[None, :]
    cosine_table = jnp.concatenate([jnp.cos(angles), jnp.cos(angles)], axis=-1)
    sine_table = jnp.concatenate([jnp.sin(angles), jnp.sin(angles)], axis=-1)
    return (cosine_table, sine_table)

def rotate(values, cosine_table, sine_table, direction):
    half_width = values.shape[-1] // 2
    turned = jnp.concatenate([-values[..., half_width:], values[..., :half_width]], axis=-1)
    return values * cosine_table[:, None, :] + direction * turned * sine_table[:, None, :]

def attention(queries, key_rows, value_rows):
    length = queries.shape[0]
    block_rows = min(512, length)
    blocks = queries.reshape(length // block_rows, block_rows, HEADS, HEAD)

    def one_block(query_block):
        scores = low_back(HEAD ** (-0.5) * jnp.einsum('qhd,khd->hqk', query_block, key_rows, precision=lax.Precision.HIGHEST))
        row_top = lax.optimization_barrier(jnp.max(scores, axis=-1, keepdims=True))
        weights = jnp.exp(scores - row_top)
        row_total = lax.optimization_barrier(jnp.sum(weights, axis=-1))
        mixed_rows = jnp.einsum('hqk,khd->qhd', low(weights), value_rows, precision=lax.Precision.HIGHEST)
        return mixed_rows / jnp.transpose(row_total)[:, :, None]
    return lax.map(jax.checkpoint(one_block), blocks).reshape(length, HEADS, HEAD)

def layer(sequence, gain_one, qkv_full, attn_full, gain_two, in_full, out_full):
    length = sequence.shape[0]
    hidden_one = low(normalize(sequence) * gain_one)
    qkv = low_back(low(product(hidden_one, qkv_full))).reshape(length, 3, HEADS, HEAD)
    cosine_table, sine_table = rotation(0, length, HEAD)
    queries = low(rotate(qkv[:, 0], cosine_table, sine_table, 1.0))
    key_rows = low(rotate(qkv[:, 1], cosine_table, sine_table, 1.0))
    attn = low_back(low(attention(queries, key_rows, qkv[:, 2]))).reshape(length, HEADS * HEAD)
    middle = sequence + low_back(product(attn, attn_full))
    hidden_two = low(normalize(middle) * gain_two)
    joint = low_back(product(hidden_two, in_full))
    activation = low(jax.nn.gelu(joint[:, :FF], approximate=False) * joint[:, FF:])
    return middle + product(activation, out_full)

def reference(tokens, attn_gain, qkv_weight, attn_out_weight, mlp_gain, in_weight, out_weight, cotangent):
    params = tuple((weight.astype(jnp.float32) for weight in (attn_gain, qkv_weight, attn_out_weight, mlp_gain, in_weight, out_weight)))

    def per_sequence(totals, inputs):
        sequence, incoming = inputs
        result, pullback = jax.vjp(layer, sequence.astype(jnp.float32), *params)
        grads = pullback(incoming.astype(jnp.float32))
        totals = tuple((left + right for left, right in zip(totals, grads[1:])))
        return (totals, (result.astype(jnp.bfloat16), grads[0].astype(jnp.bfloat16)))
    starting = tuple((jnp.zeros_like(weight) for weight in params))
    totals, (results, input_grads) = lax.scan(per_sequence, starting, (tokens, cotangent))
    return (results, input_grads, totals[0], totals[1], totals[2], totals[3], totals[4], totals[5])
```

```python
import jax
import jax.numpy as jnp
from jax import lax
from jax.experimental import pallas as pl
from jax.experimental.pallas import tpu as pltpu
from jax.sharding import PartitionSpec as P

HEAD = 64


EPSILON = 1e-05
THETA = 160000.0


def from_behind(value, axis, by):
    size = lax.axis_size(axis)
    return lax.ppermute(value, axis, [(i, (i + by) % size) for i in range(size)])


def normalize(values):
    center = values - jnp.mean(values, axis=-1, keepdims=True)
    inverse = lax.rsqrt(jnp.mean(center * center, axis=-1, keepdims=True) + EPSILON)
    return (center * inverse, inverse)


def norm_back(grad_normed, normed, inverse):
    first_mean = jnp.mean(grad_normed, axis=-1, keepdims=True)
    second_mean = jnp.mean(grad_normed * normed, axis=-1, keepdims=True)
    return inverse * (grad_normed - first_mean - normed * second_mean)


def rotation(first_row, row_count, head_width):
    half_width = head_width // 2
    frequency = THETA ** (-(jnp.arange(half_width, dtype=jnp.float32) * 2.0) / head_width)
    positions = (first_row + jnp.arange(row_count, dtype=jnp.int32)).astype(jnp.float32)
    angles = positions[:, None] * frequency[None, :]
    cosine_table = jnp.concatenate([jnp.cos(angles), jnp.cos(angles)], axis=-1)
    sine_table = jnp.concatenate([jnp.sin(angles), jnp.sin(angles)], axis=-1)
    return (cosine_table, sine_table)


def rotate(values, cosine_table, sine_table, direction):
    half_width = values.shape[-1] // 2
    turned = jnp.concatenate([-values[..., half_width:], values[..., :half_width]], axis=-1)
    return values * cosine_table[:, None, :] + direction * turned * sine_table[:, None, :]


def block_grads(
    query_part,
    key_part,
    value_part,
    grad_part,
    log_part,
    dots_part,
    top_part,
    total_part,
    score_scale,
):
    scores = (
        jnp.einsum("sqhd,skhd->shqk", query_part, key_part, preferred_element_type=jnp.float32)
        * score_scale
    )
    probs = jnp.exp(scores - log_part[..., None])
    grad_probs = jnp.einsum(
        "sqhd,skhd->shqk", grad_part, value_part, preferred_element_type=jnp.float32
    )
    grad_scores = (probs * (grad_probs - dots_part[..., None])).astype(jnp.bfloat16)
    weights_low = jnp.exp(scores - top_part[..., None]).astype(jnp.bfloat16)
    grad_scaled = grad_part.astype(jnp.float32) / jnp.transpose(total_part, (0, 2, 1))[..., None]
    value_term = jnp.einsum("shqk,sqhd->skhd", weights_low.astype(jnp.float32), grad_scaled)
    return (value_term, grad_scores)


def ring_body(
    tokens, attn_gain, qkv_weight, attn_out_weight, mlp_gain, in_weight, out_weight, cotangent
):
    sequences, per_device, model_width = tokens.shape
    groups = lax.axis_size("ulysses")
    cycle_size = lax.axis_size("blk")
    group_width = model_width // groups
    heads_here = group_width // HEAD
    group_rows = per_device * groups
    score_scale = HEAD ** (-0.5)
    qkv_full, attn_full, in_full, out_full, gain_one, gain_two = (
        lax.all_gather(qkv_weight, ("blk", "ulysses"), axis=0, tiled=True),
        lax.all_gather(attn_out_weight, ("blk", "ulysses"), axis=0, tiled=True),
        lax.all_gather(in_weight, ("blk", "ulysses"), axis=0, tiled=True),
        lax.all_gather(out_weight, ("blk", "ulysses"), axis=1, tiled=True),
        lax.all_gather(attn_gain, ("blk", "ulysses"), axis=0, tiled=True),
        lax.all_gather(mlp_gain, ("blk", "ulysses"), axis=0, tiled=True),
    )
    gain_one = gain_one.astype(jnp.float32)
    gain_two = gain_two.astype(jnp.float32)
    hidden_units = out_full.shape[0]
    inputs_wide = tokens.astype(jnp.float32).reshape(sequences * per_device, model_width)
    normed_one, inverse_one = normalize(inputs_wide)
    hidden_one = (normed_one * gain_one).astype(jnp.bfloat16)
    qkv = jnp.dot(hidden_one, qkv_full, preferred_element_type=jnp.float32).astype(jnp.bfloat16)
    packed = qkv.reshape(sequences, per_device, 3, groups, group_width)
    headwise = lax.all_to_all(packed, "ulysses", split_axis=3, concat_axis=1, tiled=True)
    headwise = headwise.reshape(sequences, group_rows, 3, heads_here, HEAD)
    cosine_table, sine_table = rotation(lax.axis_index("blk") * group_rows, group_rows, HEAD)
    queries = rotate(headwise[:, :, 0].astype(jnp.float32), cosine_table, sine_table, 1.0).astype(
        jnp.bfloat16
    )
    key_rows = rotate(headwise[:, :, 1].astype(jnp.float32), cosine_table, sine_table, 1.0).astype(
        jnp.bfloat16
    )
    value_rows = headwise[:, :, 2]
    start_top = jnp.full((sequences, heads_here, group_rows), -1e30, jnp.float32)
    zeros_rows = jnp.zeros((sequences, group_rows, heads_here, HEAD), jnp.float32)
    key_piece = lax.all_gather(key_rows, "blk", axis=1, tiled=True)
    value_piece = lax.all_gather(value_rows, "blk", axis=1, tiled=True)
    scores = (
        jnp.einsum("sqhd,skhd->shqk", queries, key_piece, preferred_element_type=jnp.float32)
        * score_scale
    )
    new_top = jnp.maximum(start_top, jnp.max(scores, axis=-1))
    weights = jnp.exp(scores - new_top[..., None])
    attend_row_total = jnp.sum(weights, axis=-1)
    update = jnp.einsum(
        "shqk,skhd->sqhd",
        weights.astype(jnp.bfloat16),
        value_piece,
        preferred_element_type=jnp.float32,
    )
    weighted = update
    row_top, row_total, weighted = (new_top, attend_row_total, weighted)
    log_total = row_top + jnp.log(row_total)
    attn_wide = weighted / jnp.transpose(row_total, (0, 2, 1))[..., None]
    attn_low = attn_wide.astype(jnp.bfloat16).reshape(sequences, group_rows, 1, group_width)
    token_rows = lax.all_to_all(attn_low, "ulysses", split_axis=1, concat_axis=2, tiled=True)
    attn_cat = token_rows.reshape(sequences * per_device, model_width)
    middle = inputs_wide + jnp.dot(attn_cat, attn_full, preferred_element_type=jnp.float32)
    normed_two, inverse_two = normalize(middle)
    hidden_two = (normed_two * gain_two).astype(jnp.bfloat16)
    joint = jnp.dot(hidden_two, in_full, preferred_element_type=jnp.float32)

    def geglu(joint_pre):
        return (
            jax.nn.gelu(joint_pre[:, :hidden_units], approximate=False)
            * joint_pre[:, hidden_units:]
        )

    act_wide, geglu_back = jax.vjp(geglu, joint)
    activation = act_wide.astype(jnp.bfloat16)
    result = middle + jnp.dot(activation, out_full, preferred_element_type=jnp.float32)
    layer_output = result.astype(jnp.bfloat16).reshape(sequences, per_device, model_width)
    grad_out = cotangent.reshape(sequences * per_device, model_width)
    grad_wout = jnp.einsum("tf,td->fd", activation, grad_out, preferred_element_type=jnp.float32)
    grad_act = jnp.einsum("td,fd->tf", grad_out, out_full, preferred_element_type=jnp.float32)
    grad_joint = geglu_back(grad_act)[0].astype(jnp.bfloat16)
    grad_win = jnp.einsum("tc,tf->cf", hidden_two, grad_joint, preferred_element_type=jnp.float32)
    grad_hidden_two = jnp.einsum(
        "tf,cf->tc", grad_joint, in_full, preferred_element_type=jnp.float32
    )
    grad_gain_two = jnp.sum(grad_hidden_two * normed_two, axis=0)
    grad_middle = grad_out.astype(jnp.float32) + norm_back(
        grad_hidden_two * gain_two, normed_two, inverse_two
    )
    grad_branch = grad_middle.astype(jnp.bfloat16)
    grad_wattn = jnp.einsum("tc,td->cd", attn_cat, grad_branch, preferred_element_type=jnp.float32)
    grad_cat = jnp.einsum(
        "td,cd->tc", grad_branch, attn_full, preferred_element_type=jnp.float32
    ).astype(jnp.bfloat16)
    grad_heads_in = lax.all_to_all(
        grad_cat.reshape(sequences, per_device, groups, group_width),
        "ulysses",
        split_axis=2,
        concat_axis=1,
        tiled=True,
    )
    grad_attn = grad_heads_in.reshape(sequences, group_rows, heads_here, HEAD)
    row_dots = jnp.transpose(jnp.sum(grad_attn.astype(jnp.float32) * attn_wide, axis=-1), (0, 2, 1))

    def cycle_step(step_index, state_now):
        key_now, value_now, grad_key, grad_value, grad_query = state_now
        value_term, grad_scores = block_grads(
            queries,
            key_now,
            value_now,
            grad_attn,
            log_total,
            row_dots,
            row_top,
            row_total,
            score_scale,
        )
        grad_value = grad_value + value_term
        grad_key = grad_key + score_scale * jnp.einsum(
            "shqk,sqhd->skhd", grad_scores, queries, preferred_element_type=jnp.float32
        )
        grad_query = grad_query + score_scale * jnp.einsum(
            "shqk,skhd->sqhd", grad_scores, key_now, preferred_element_type=jnp.float32
        )
        key_now, value_now = from_behind((key_now, value_now), "blk", 1)
        grad_key, grad_value = (
            from_behind(grad_key.astype(jnp.bfloat16), "blk", 1).astype(grad_key.dtype),
            from_behind(grad_value.astype(jnp.bfloat16), "blk", 1).astype(grad_value.dtype),
        )
        return (key_now, value_now, grad_key, grad_value, grad_query)

    final_state = lax.fori_loop(
        0, cycle_size, cycle_step, (key_rows, value_rows, zeros_rows, zeros_rows, zeros_rows)
    )
    grad_key, grad_value, grad_query = (final_state[2], final_state[3], final_state[4])
    grad_query = rotate(grad_query, cosine_table, sine_table, -1.0)
    grad_key = rotate(grad_key, cosine_table, sine_table, -1.0)
    grad_stack = jnp.stack([grad_query, grad_key, grad_value], axis=2).astype(jnp.bfloat16)
    grad_stack = grad_stack.reshape(sequences, group_rows, 3, 1, group_width)
    grad_tokens = lax.all_to_all(grad_stack, "ulysses", split_axis=1, concat_axis=3, tiled=True)
    grad_qkv = grad_tokens.reshape(sequences * per_device, 3 * model_width)
    grad_wqkv = jnp.einsum("tc,tf->cf", hidden_one, grad_qkv, preferred_element_type=jnp.float32)
    grad_hidden_one = jnp.einsum(
        "tf,cf->tc", grad_qkv, qkv_full, preferred_element_type=jnp.float32
    )
    grad_gain_one = jnp.sum(grad_hidden_one * normed_one, axis=0)
    grad_input = grad_middle + norm_back(grad_hidden_one * gain_one, normed_one, inverse_one)
    input_grad = grad_input.astype(jnp.bfloat16).reshape(sequences, per_device, model_width)
    shard_qkv, shard_attn, shard_in, shard_out, shard_one, shard_two = (
        lax.psum_scatter(grad_wqkv, ("blk", "ulysses"), scatter_dimension=0, tiled=True),
        lax.psum_scatter(grad_wattn, ("blk", "ulysses"), scatter_dimension=0, tiled=True),
        lax.psum_scatter(grad_win, ("blk", "ulysses"), scatter_dimension=0, tiled=True),
        lax.psum_scatter(grad_wout, ("blk", "ulysses"), scatter_dimension=1, tiled=True),
        lax.psum_scatter(grad_gain_one, ("blk", "ulysses"), scatter_dimension=0, tiled=True),
        lax.psum_scatter(grad_gain_two, ("blk", "ulysses"), scatter_dimension=0, tiled=True),
    )
    return (
        layer_output,
        input_grad,
        shard_one,
        shard_qkv,
        shard_attn,
        shard_two,
        shard_in,
        shard_out,
    )


AXES = ("blk", "ulysses")
BF = jnp.bfloat16
F32 = jnp.float32
HEADS = 12
SHARE = 3
BLOCK = 256


def swap(value, axis, bit):
    size = lax.axis_size(axis)
    return lax.ppermute(value, axis, [(i, i ^ bit) for i in range(size)])


def my_bit(axis, bit):
    return (lax.axis_index(axis) // bit) % 2


def join(mine, other, side, axis):
    first = jnp.stack([mine, other], axis=axis)
    second = jnp.stack([other, mine], axis=axis)
    return jnp.where(side == 0, first, second)


def gather_sequence(tokens):
    sequences, rows, width = tokens.shape
    z2, z1, x = my_bit("blk", 4), my_bit("blk", 2), my_bit("blk", 1)
    y, core = my_bit("ulysses", 2), my_bit("ulysses", 1)
    keep = lax.dynamic_index_in_dim(tokens, z2, 0, keepdims=False)
    give = lax.dynamic_index_in_dim(tokens, 1 - z2, 0, keepdims=False)
    wide = join(keep, swap(give, "blk", 4), z2, 0)
    wide = join(wide, swap(wide, "blk", 2), z1, 1)
    wide = wide.reshape(2, 2, 2, rows // 2, width)
    part_a, part_b = wide[:, :, 0], wide[:, :, 1]
    from_a, from_b = swap(part_a, "blk", 1), swap(part_b, "ulysses", 2)
    part_a = join(part_a, from_a, x, 2)
    part_b = join(part_b, from_b, y, 2)
    from_a, from_b = swap(part_a, "ulysses", 2), swap(part_b, "blk", 1)
    part_a = join(part_a, from_a, y, 3)
    part_b = join(part_b, from_b, x, 2)
    wide = jnp.stack([part_a, part_b], axis=4)
    wide = join(wide, swap(wide, "ulysses", 1), core, 4)
    return wide.reshape(32 * rows, width)


def halve(value, axis, bit, dim):
    side = my_bit(axis, bit)
    keep = lax.dynamic_index_in_dim(value, side, dim, keepdims=False)
    give = lax.dynamic_index_in_dim(value, 1 - side, dim, keepdims=False)
    got = swap(give, axis, bit)
    return (keep.astype(F32) + got.astype(F32)).astype(BF)


def scatter_rows(grads):
    rows, columns = grads.shape
    view = grads.reshape(2, 2, 2, 2, 2, rows // 32, columns)
    view = halve(view, "ulysses", 1, 4)
    half = columns // 256 * 128
    part_a, part_b = view[..., :half], view[..., half:]
    part_a = halve(part_a, "blk", 1, 2)
    part_b = halve(part_b, "ulysses", 2, 3)
    part_a = halve(part_a, "ulysses", 2, 2)
    part_b = halve(part_b, "blk", 1, 2)
    part_a, part_b = halve(part_a, "blk", 2, 1), halve(part_b, "blk", 2, 1)
    part_a, part_b = halve(part_a, "blk", 4, 0), halve(part_b, "blk", 4, 0)
    return jnp.concatenate([part_a, part_b], axis=-1)


def exchange(value):
    return lax.all_to_all(value, AXES, split_axis=0, concat_axis=0, tiled=True)


def to_owners(by_pair):
    sequences, heads = by_pair.shape[:2]
    tail = by_pair.shape[2:]
    grouped = by_pair.reshape(sequences, heads // SHARE, SHARE, *tail)
    grouped = jnp.concatenate([grouped, grouped[:, :, -1:]], axis=2)
    return grouped.reshape(sequences * heads // SHARE * (SHARE + 1), *tail)


def from_owners(blocks):
    tail = blocks.shape[1:]
    grouped = blocks.reshape(2, HEADS // SHARE, SHARE + 1, *tail)[:, :, :SHARE]
    return grouped.reshape(2, HEADS, *tail)


def turn(values):
    lane = lax.broadcasted_iota(jnp.int32, values.shape, 1) % HEAD
    return jnp.where(
        lane < HEAD // 2, -pltpu.roll(values, 3 * HEAD // 2, 1), pltpu.roll(values, HEAD // 2, 1)
    )


def project_kernel(tokens, gain, weight, cosine, sine, hidden, queries, key_rows, value_rows):
    normed, inverse = normalize(tokens[...].astype(F32))
    low = (normed * gain[...]).astype(BF)
    hidden[...] = low
    qkv = jnp.dot(low, weight[...], preferred_element_type=F32).astype(BF)
    both = qkv[:, : 2 * HEAD].astype(F32)
    both = both * cosine[...] + turn(both) * sine[...]
    both = both.astype(BF)
    queries[...] = both[:, :HEAD] * BF(HEAD**-0.5)
    key_rows[...] = both[:, HEAD:]
    value_rows[...] = qkv[:, 2 * HEAD :]


def project(tokens, gain, weight, cosine, sine):
    length, width = tokens.shape
    by_row = lambda columns: pl.BlockSpec((BLOCK, columns), lambda i: (i, 0))
    whole = lambda shape: pl.BlockSpec(shape, lambda i: (0, 0))
    return pl.pallas_call(
        project_kernel,
        grid=(length // BLOCK,),
        in_specs=[
            by_row(width),
            whole((1, width)),
            whole(weight.shape),
            by_row(2 * HEAD),
            by_row(2 * HEAD),
        ],
        out_specs=[by_row(width), by_row(HEAD), by_row(HEAD), by_row(HEAD)],
        out_shape=[jax.ShapeDtypeStruct((length, width), BF)]
        + [jax.ShapeDtypeStruct((length, HEAD), BF)] * 3,
        name="project",
    )(tokens, gain, weight, cosine, sine)


def attend_kernel(queries, key_rows, value_rows, weights, attn32, total):
    scores = lax.dot_general(
        queries[...], key_rows[...], (((1,), (1,)), ((), ())), preferred_element_type=F32
    )
    top = jnp.max(scores, axis=-1, keepdims=True)
    expo = jnp.exp(scores - top)
    row_total = jnp.sum(expo, axis=-1, keepdims=True)
    low = expo.astype(BF)
    weights[...] = low
    mixed = jnp.dot(low, value_rows[...], preferred_element_type=F32)
    attn32[...] = mixed / row_total
    total[...] = row_total


def attend(queries, key_rows, value_rows):
    length = queries.shape[0]
    by_row = lambda columns: pl.BlockSpec((BLOCK, columns), lambda i: (i, 0))
    whole = pl.BlockSpec((length, HEAD), lambda i: (0, 0))
    return pl.pallas_call(
        attend_kernel,
        grid=(length // BLOCK,),
        in_specs=[by_row(HEAD), whole, whole],
        out_specs=[by_row(length), by_row(HEAD), by_row(1)],
        out_shape=[
            jax.ShapeDtypeStruct((length, length), BF),
            jax.ShapeDtypeStruct((length, HEAD), F32),
            jax.ShapeDtypeStruct((length, 1), F32),
        ],
        name="attend",
    )(queries, key_rows, value_rows)


def attend_back_kernel(
    grad, attn32, total, weights, queries, key_rows, value_rows, grad_query, grad_key, grad_value
):
    @pl.when(pl.program_id(0) == 0)
    def _():
        grad_key[...] = jnp.zeros_like(grad_key)
        grad_value[...] = jnp.zeros_like(grad_value)

    wide = grad[...].astype(F32)
    dots = jnp.sum(wide * attn32[...], axis=-1, keepdims=True)
    grad_probs = lax.dot_general(
        grad[...], value_rows[...], (((1,), (1,)), ((), ())), preferred_element_type=F32
    )
    inverse = 1.0 / total[...]
    low = weights[...]
    grad_scores = ((low.astype(F32) * inverse) * (grad_probs - dots)).astype(BF)
    grad_query[...] = HEAD**-0.5 * jnp.dot(
        grad_scores, key_rows[...], preferred_element_type=F32
    )
    over_rows = (((0,), (0,)), ((), ()))
    grad_value[...] += lax.dot_general(
        low, (wide * inverse).astype(BF), over_rows, preferred_element_type=F32
    )
    grad_key[...] += lax.dot_general(
        grad_scores, queries[...], over_rows, preferred_element_type=F32
    )


def attend_back(grad, attn32, total, weights, queries, key_rows, value_rows):
    length = queries.shape[0]
    by_row = lambda columns: pl.BlockSpec((BLOCK, columns), lambda i: (i, 0))
    whole = pl.BlockSpec((length, HEAD), lambda i: (0, 0))
    return pl.pallas_call(
        attend_back_kernel,
        grid=(length // BLOCK,),
        in_specs=[
            by_row(HEAD),
            by_row(HEAD),
            by_row(1),
            by_row(length),
            by_row(HEAD),
            whole,
            whole,
        ],
        out_specs=[by_row(HEAD), whole, whole],
        out_shape=[jax.ShapeDtypeStruct((length, HEAD), F32)] * 3,
        name="attend_back",
    )(grad, attn32, total, weights, queries, key_rows, value_rows)


def unturn(values, cosine_table, sine_table):
    half_width = HEAD // 2
    turned = jnp.concatenate([-values[:, half_width:], values[:, :half_width]], axis=-1)
    return values * cosine_table - turned * sine_table


def owner_body(
    tokens, attn_gain, qkv_weight, attn_out_weight, mlp_gain, in_weight, out_weight, cotangent
):
    sequences, per_device, model_width = tokens.shape
    hidden_units = out_weight.shape[0]
    rows_here = qkv_weight.shape[0]
    length = per_device * 32
    late = jnp.concatenate(
        [in_weight, attn_out_weight, jnp.transpose(out_weight)], axis=1
    )
    late_full = lax.all_gather(late, AXES, axis=0, tiled=True)
    in_full = late_full[:, : 2 * hidden_units]
    attn_full = late_full[:, 2 * hidden_units : 2 * hidden_units + model_width]
    out_turned = late_full[:, 2 * hidden_units + model_width :]
    by_head = qkv_weight.reshape(rows_here, 3, HEADS, HEAD).transpose(2, 0, 1, 3)
    by_head = by_head.reshape(HEADS, rows_here, 3 * HEAD)
    gains = jnp.concatenate([attn_gain, mlp_gain, jnp.zeros((3 * HEAD - 2 * rows_here,), BF)])
    gain_rows = jnp.broadcast_to(gains, (HEADS, 8, 3 * HEAD))
    packed = jnp.concatenate([by_head, gain_rows], axis=1)
    packed = to_owners(jnp.stack([packed, packed]))
    got = exchange(packed)
    weight_here = got[:, :rows_here].reshape(model_width, 3 * HEAD)
    gain_one = got[:, rows_here, :rows_here].reshape(1, model_width).astype(F32)
    gain_two = got[:, rows_here, rows_here : 2 * rows_here].reshape(1, model_width).astype(F32)
    sequence = gather_sequence(tokens)
    cosine_table, sine_table = rotation(0, length, HEAD)
    cosine_two = jnp.concatenate([cosine_table, cosine_table], axis=1)
    sine_two = jnp.concatenate([sine_table, sine_table], axis=1)
    hidden_one, queries, key_rows, value_rows = project(
        sequence, gain_one, weight_here, cosine_two, sine_two
    )
    weights_low, attn32, row_total = attend(queries, key_rows, value_rows)
    back = exchange(attn32.astype(BF).reshape(32, per_device, HEAD))
    attn_cat = from_owners(back).transpose(0, 2, 1, 3)
    attn_cat = attn_cat.reshape(sequences * per_device, model_width)
    inputs_wide = tokens.astype(F32).reshape(sequences * per_device, model_width)
    middle = inputs_wide + jnp.dot(attn_cat, attn_full, preferred_element_type=F32)
    normed_two, inverse_two = normalize(middle)
    hidden_two = (normed_two * gain_two).astype(BF)
    joint = jnp.dot(hidden_two, in_full, preferred_element_type=F32)

    def geglu(joint_pre):
        return (
            jax.nn.gelu(joint_pre[:, :hidden_units], approximate=False)
            * joint_pre[:, hidden_units:]
        )

    act_wide, geglu_back = jax.vjp(geglu, joint)
    activation = act_wide.astype(BF)
    result = middle + jnp.einsum("tf,df->td", activation, out_turned, preferred_element_type=F32)
    layer_output = result.astype(BF).reshape(sequences, per_device, model_width)
    grad_out = cotangent.reshape(sequences * per_device, model_width)
    grad_act = jnp.dot(grad_out, out_turned, preferred_element_type=F32)
    grad_joint = geglu_back(grad_act)[0].astype(BF)
    grad_hidden_two = jnp.einsum("tf,cf->tc", grad_joint, in_full, preferred_element_type=F32)
    grad_middle = grad_out.astype(F32) + norm_back(
        grad_hidden_two * gain_two, normed_two, inverse_two
    )
    grad_branch = grad_middle.astype(BF)
    grad_cat = jnp.einsum(
        "td,cd->tc", grad_branch, attn_full, preferred_element_type=F32
    ).astype(BF)
    by_pair = grad_cat.reshape(sequences, per_device, HEADS, HEAD).transpose(0, 2, 1, 3)
    grad_attn = exchange(to_owners(by_pair)).reshape(length, HEAD)
    grad_wout = jnp.einsum("td,tf->df", grad_out, activation, preferred_element_type=F32)
    grad_win = jnp.einsum("tc,tf->cf", hidden_two, grad_joint, preferred_element_type=F32)
    grad_wattn = jnp.einsum("tc,td->cd", attn_cat, grad_branch, preferred_element_type=F32)
    late_grads = jnp.concatenate(
        [grad_win.astype(BF), grad_wattn.astype(BF), grad_wout.astype(BF)], axis=1
    )
    shards = scatter_rows(late_grads).astype(F32)
    shard_in = shards[:, : 2 * hidden_units]
    shard_attn = shards[:, 2 * hidden_units : 2 * hidden_units + model_width]
    shard_out = jnp.transpose(shards[:, 2 * hidden_units + model_width :])
    shard_two = jnp.sum(shard_in * in_weight.astype(F32), axis=1) / mlp_gain.astype(F32)
    qkv_full = lax.all_gather(qkv_weight, AXES, axis=0, tiled=True)
    grad_query, grad_key, grad_value = attend_back(
        grad_attn, attn32, row_total, weights_low, queries, key_rows, value_rows
    )
    grad_query = unturn(grad_query, cosine_table, sine_table)
    grad_key = unturn(grad_key, cosine_table, sine_table)
    grad_stack = jnp.concatenate([grad_query, grad_key, grad_value], axis=1).astype(BF)
    grad_tokens = exchange(grad_stack.reshape(32, per_device, 3 * HEAD))
    grad_whead = jnp.einsum("tc,tf->cf", hidden_one, grad_stack, preferred_element_type=F32)
    grad_rows = from_owners(exchange(grad_whead.astype(BF).reshape(32, rows_here, 3 * HEAD)))
    grad_rows = jnp.sum(grad_rows.astype(F32), axis=0).reshape(HEADS, rows_here, 3, HEAD)
    shard_qkv = grad_rows.transpose(1, 2, 0, 3).reshape(rows_here, 3 * model_width)
    shard_one = jnp.sum(shard_qkv * qkv_weight.astype(F32), axis=1) / attn_gain.astype(F32)
    grad_qkv = from_owners(grad_tokens).reshape(sequences, HEADS, per_device, 3, HEAD)
    grad_qkv = grad_qkv.transpose(0, 2, 3, 1, 4).reshape(sequences * per_device, 3 * model_width)
    grad_hidden_one = jnp.einsum("tf,cf->tc", grad_qkv, qkv_full, preferred_element_type=F32)
    normed_one, inverse_one = normalize(inputs_wide)
    grad_input = grad_middle + norm_back(grad_hidden_one * gain_one, normed_one, inverse_one)
    input_grad = grad_input.astype(BF).reshape(sequences, per_device, model_width)
    return (
        layer_output,
        input_grad,
        shard_one,
        shard_qkv,
        shard_attn,
        shard_two,
        shard_in,
        shard_out,
    )


def solution(mesh):
    placed = (
        P(None, ("blk", "ulysses"), None),
        P(("blk", "ulysses")),
        P(("blk", "ulysses"), None),
        P(("blk", "ulysses"), None),
        P(("blk", "ulysses")),
        P(("blk", "ulysses"), None),
        P(None, ("blk", "ulysses")),
        P(None, ("blk", "ulysses"), None),
    )
    sizes = (mesh.shape["blk"], mesh.shape["ulysses"])
    return jax.shard_map(
        owner_body if sizes == (8, 4) else ring_body,
        mesh=mesh,
        in_specs=placed,
        out_specs=(
            P(None, ("blk", "ulysses"), None),
            P(None, ("blk", "ulysses"), None),
            P(("blk", "ulysses")),
            P(("blk", "ulysses"), None),
            P(("blk", "ulysses"), None),
            P(("blk", "ulysses")),
            P(("blk", "ulysses"), None),
            P(None, ("blk", "ulysses")),
        ),
        check_vma=False,
    )
```

```python
import functools

import jax
import jax.numpy as jnp
from jax import lax
from jax.experimental import pallas as pl
from jax.experimental.pallas import tpu as pltpu
from jax.sharding import PartitionSpec as P

HEAD = 64


EPSILON = 1e-05
THETA = 160000.0


def from_behind(value, axis, by):
    size = lax.axis_size(axis)
    return lax.ppermute(value, axis, [(i, (i + by) % size) for i in range(size)])


def normalize(values):
    center = values - jnp.mean(values, axis=-1, keepdims=True)
    inverse = lax.rsqrt(jnp.mean(center * center, axis=-1, keepdims=True) + EPSILON)
    return (center * inverse, inverse)


def norm_back(grad_normed, normed, inverse):
    first_mean = jnp.mean(grad_normed, axis=-1, keepdims=True)
    second_mean = jnp.mean(grad_normed * normed, axis=-1, keepdims=True)
    return inverse * (grad_normed - first_mean - normed * second_mean)


def rotation(first_row, row_count, head_width):
    half_width = head_width // 2
    frequency = THETA ** (-(jnp.arange(half_width, dtype=jnp.float32) * 2.0) / head_width)
    positions = (first_row + jnp.arange(row_count, dtype=jnp.int32)).astype(jnp.float32)
    angles = positions[:, None] * frequency[None, :]
    cosine_table = jnp.concatenate([jnp.cos(angles), jnp.cos(angles)], axis=-1)
    sine_table = jnp.concatenate([jnp.sin(angles), jnp.sin(angles)], axis=-1)
    return (cosine_table, sine_table)


def rotate(values, cosine_table, sine_table, direction):
    half_width = values.shape[-1] // 2
    turned = jnp.concatenate([-values[..., half_width:], values[..., :half_width]], axis=-1)
    return values * cosine_table[:, None, :] + direction * turned * sine_table[:, None, :]


def block_grads(
    query_part,
    key_part,
    value_part,
    grad_part,
    log_part,
    dots_part,
    top_part,
    total_part,
    score_scale,
):
    scores = (
        jnp.einsum("sqhd,skhd->shqk", query_part, key_part, preferred_element_type=jnp.float32)
        * score_scale
    )
    probs = jnp.exp(scores - log_part[..., None])
    grad_probs = jnp.einsum(
        "sqhd,skhd->shqk", grad_part, value_part, preferred_element_type=jnp.float32
    )
    grad_scores = (probs * (grad_probs - dots_part[..., None])).astype(jnp.bfloat16)
    weights_low = jnp.exp(scores - top_part[..., None]).astype(jnp.bfloat16)
    grad_scaled = grad_part.astype(jnp.float32) / jnp.transpose(total_part, (0, 2, 1))[..., None]
    value_term = jnp.einsum("shqk,sqhd->skhd", weights_low.astype(jnp.float32), grad_scaled)
    return (value_term, grad_scores)


def ring_body(
    tokens, attn_gain, qkv_weight, attn_out_weight, mlp_gain, in_weight, out_weight, cotangent
):
    sequences, per_device, model_width = tokens.shape
    groups = lax.axis_size("ulysses")
    cycle_size = lax.axis_size("blk")
    group_width = model_width // groups
    heads_here = group_width // HEAD
    group_rows = per_device * groups
    score_scale = HEAD ** (-0.5)
    qkv_full, attn_full, in_full, out_full, gain_one, gain_two = (
        lax.all_gather(qkv_weight, ("blk", "ulysses"), axis=0, tiled=True),
        lax.all_gather(attn_out_weight, ("blk", "ulysses"), axis=0, tiled=True),
        lax.all_gather(in_weight, ("blk", "ulysses"), axis=0, tiled=True),
        lax.all_gather(out_weight, ("blk", "ulysses"), axis=1, tiled=True),
        lax.all_gather(attn_gain, ("blk", "ulysses"), axis=0, tiled=True),
        lax.all_gather(mlp_gain, ("blk", "ulysses"), axis=0, tiled=True),
    )
    gain_one = gain_one.astype(jnp.float32)
    gain_two = gain_two.astype(jnp.float32)
    hidden_units = out_full.shape[0]
    inputs_wide = tokens.astype(jnp.float32).reshape(sequences * per_device, model_width)
    normed_one, inverse_one = normalize(inputs_wide)
    hidden_one = (normed_one * gain_one).astype(jnp.bfloat16)
    qkv = jnp.dot(hidden_one, qkv_full, preferred_element_type=jnp.float32).astype(jnp.bfloat16)
    packed = qkv.reshape(sequences, per_device, 3, groups, group_width)
    headwise = lax.all_to_all(packed, "ulysses", split_axis=3, concat_axis=1, tiled=True)
    headwise = headwise.reshape(sequences, group_rows, 3, heads_here, HEAD)
    cosine_table, sine_table = rotation(lax.axis_index("blk") * group_rows, group_rows, HEAD)
    queries = rotate(headwise[:, :, 0].astype(jnp.float32), cosine_table, sine_table, 1.0).astype(
        jnp.bfloat16
    )
    key_rows = rotate(headwise[:, :, 1].astype(jnp.float32), cosine_table, sine_table, 1.0).astype(
        jnp.bfloat16
    )
    value_rows = headwise[:, :, 2]
    start_top = jnp.full((sequences, heads_here, group_rows), -1e30, jnp.float32)
    zeros_rows = jnp.zeros((sequences, group_rows, heads_here, HEAD), jnp.float32)
    key_piece = lax.all_gather(key_rows, "blk", axis=1, tiled=True)
    value_piece = lax.all_gather(value_rows, "blk", axis=1, tiled=True)
    scores = (
        jnp.einsum("sqhd,skhd->shqk", queries, key_piece, preferred_element_type=jnp.float32)
        * score_scale
    )
    new_top = jnp.maximum(start_top, jnp.max(scores, axis=-1))
    weights = jnp.exp(scores - new_top[..., None])
    attend_row_total = jnp.sum(weights, axis=-1)
    update = jnp.einsum(
        "shqk,skhd->sqhd",
        weights.astype(jnp.bfloat16),
        value_piece,
        preferred_element_type=jnp.float32,
    )
    weighted = update
    row_top, row_total, weighted = (new_top, attend_row_total, weighted)
    log_total = row_top + jnp.log(row_total)
    attn_wide = weighted / jnp.transpose(row_total, (0, 2, 1))[..., None]
    attn_low = attn_wide.astype(jnp.bfloat16).reshape(sequences, group_rows, 1, group_width)
    token_rows = lax.all_to_all(attn_low, "ulysses", split_axis=1, concat_axis=2, tiled=True)
    attn_cat = token_rows.reshape(sequences * per_device, model_width)
    middle = inputs_wide + jnp.dot(attn_cat, attn_full, preferred_element_type=jnp.float32)
    normed_two, inverse_two = normalize(middle)
    hidden_two = (normed_two * gain_two).astype(jnp.bfloat16)
    joint = jnp.dot(hidden_two, in_full, preferred_element_type=jnp.float32)

    def geglu(joint_pre):
        return (
            jax.nn.gelu(joint_pre[:, :hidden_units], approximate=False)
            * joint_pre[:, hidden_units:]
        )

    act_wide, geglu_back = jax.vjp(geglu, joint)
    activation = act_wide.astype(jnp.bfloat16)
    result = middle + jnp.dot(activation, out_full, preferred_element_type=jnp.float32)
    layer_output = result.astype(jnp.bfloat16).reshape(sequences, per_device, model_width)
    grad_out = cotangent.reshape(sequences * per_device, model_width)
    grad_wout = jnp.einsum("tf,td->fd", activation, grad_out, preferred_element_type=jnp.float32)
    grad_act = jnp.einsum("td,fd->tf", grad_out, out_full, preferred_element_type=jnp.float32)
    grad_joint = geglu_back(grad_act)[0].astype(jnp.bfloat16)
    grad_win = jnp.einsum("tc,tf->cf", hidden_two, grad_joint, preferred_element_type=jnp.float32)
    grad_hidden_two = jnp.einsum(
        "tf,cf->tc", grad_joint, in_full, preferred_element_type=jnp.float32
    )
    grad_gain_two = jnp.sum(grad_hidden_two * normed_two, axis=0)
    grad_middle = grad_out.astype(jnp.float32) + norm_back(
        grad_hidden_two * gain_two, normed_two, inverse_two
    )
    grad_branch = grad_middle.astype(jnp.bfloat16)
    grad_wattn = jnp.einsum("tc,td->cd", attn_cat, grad_branch, preferred_element_type=jnp.float32)
    grad_cat = jnp.einsum(
        "td,cd->tc", grad_branch, attn_full, preferred_element_type=jnp.float32
    ).astype(jnp.bfloat16)
    grad_heads_in = lax.all_to_all(
        grad_cat.reshape(sequences, per_device, groups, group_width),
        "ulysses",
        split_axis=2,
        concat_axis=1,
        tiled=True,
    )
    grad_attn = grad_heads_in.reshape(sequences, group_rows, heads_here, HEAD)
    row_dots = jnp.transpose(jnp.sum(grad_attn.astype(jnp.float32) * attn_wide, axis=-1), (0, 2, 1))

    def cycle_step(step_index, state_now):
        key_now, value_now, grad_key, grad_value, grad_query = state_now
        value_term, grad_scores = block_grads(
            queries,
            key_now,
            value_now,
            grad_attn,
            log_total,
            row_dots,
            row_top,
            row_total,
            score_scale,
        )
        grad_value = grad_value + value_term
        grad_key = grad_key + score_scale * jnp.einsum(
            "shqk,sqhd->skhd", grad_scores, queries, preferred_element_type=jnp.float32
        )
        grad_query = grad_query + score_scale * jnp.einsum(
            "shqk,skhd->sqhd", grad_scores, key_now, preferred_element_type=jnp.float32
        )
        key_now, value_now = from_behind((key_now, value_now), "blk", 1)
        grad_key, grad_value = (
            from_behind(grad_key.astype(jnp.bfloat16), "blk", 1).astype(grad_key.dtype),
            from_behind(grad_value.astype(jnp.bfloat16), "blk", 1).astype(grad_value.dtype),
        )
        return (key_now, value_now, grad_key, grad_value, grad_query)

    final_state = lax.fori_loop(
        0, cycle_size, cycle_step, (key_rows, value_rows, zeros_rows, zeros_rows, zeros_rows)
    )
    grad_key, grad_value, grad_query = (final_state[2], final_state[3], final_state[4])
    grad_query = rotate(grad_query, cosine_table, sine_table, -1.0)
    grad_key = rotate(grad_key, cosine_table, sine_table, -1.0)
    grad_stack = jnp.stack([grad_query, grad_key, grad_value], axis=2).astype(jnp.bfloat16)
    grad_stack = grad_stack.reshape(sequences, group_rows, 3, 1, group_width)
    grad_tokens = lax.all_to_all(grad_stack, "ulysses", split_axis=1, concat_axis=3, tiled=True)
    grad_qkv = grad_tokens.reshape(sequences * per_device, 3 * model_width)
    grad_wqkv = jnp.einsum("tc,tf->cf", hidden_one, grad_qkv, preferred_element_type=jnp.float32)
    grad_hidden_one = jnp.einsum(
        "tf,cf->tc", grad_qkv, qkv_full, preferred_element_type=jnp.float32
    )
    grad_gain_one = jnp.sum(grad_hidden_one * normed_one, axis=0)
    grad_input = grad_middle + norm_back(grad_hidden_one * gain_one, normed_one, inverse_one)
    input_grad = grad_input.astype(jnp.bfloat16).reshape(sequences, per_device, model_width)
    shard_qkv, shard_attn, shard_in, shard_out, shard_one, shard_two = (
        lax.psum_scatter(grad_wqkv, ("blk", "ulysses"), scatter_dimension=0, tiled=True),
        lax.psum_scatter(grad_wattn, ("blk", "ulysses"), scatter_dimension=0, tiled=True),
        lax.psum_scatter(grad_win, ("blk", "ulysses"), scatter_dimension=0, tiled=True),
        lax.psum_scatter(grad_wout, ("blk", "ulysses"), scatter_dimension=1, tiled=True),
        lax.psum_scatter(grad_gain_one, ("blk", "ulysses"), scatter_dimension=0, tiled=True),
        lax.psum_scatter(grad_gain_two, ("blk", "ulysses"), scatter_dimension=0, tiled=True),
    )
    return (
        layer_output,
        input_grad,
        shard_one,
        shard_qkv,
        shard_attn,
        shard_two,
        shard_in,
        shard_out,
    )


AXES = ("blk", "ulysses")
BF = jnp.bfloat16
F32 = jnp.float32
HEADS = 12
SHARE = 3
BLOCK = 256
LANES = 128
TILE = 384
BY_COLUMN = (((1,), (1,)), ((), ()))
BY_ROW = (((0,), (0,)), ((), ()))


def swap(value, axis, bit):
    size = lax.axis_size(axis)
    return lax.ppermute(value, axis, [(i, i ^ bit) for i in range(size)])


def my_bit(axis, bit):
    return (lax.axis_index(axis) // bit) % 2


def join(mine, other, side, axis):
    first = jnp.stack([mine, other], axis=axis)
    second = jnp.stack([other, mine], axis=axis)
    return jnp.where(side == 0, first, second)


def gather_sequence(tokens, also):
    sequences, rows, width = tokens.shape
    z2, z1, x = my_bit("blk", 4), my_bit("blk", 2), my_bit("blk", 1)
    y = my_bit("ulysses", 2)
    keep = lax.dynamic_index_in_dim(tokens, z2, 0, keepdims=False)
    give = lax.dynamic_index_in_dim(tokens, 1 - z2, 0, keepdims=False)
    wide = join(keep, swap(give, "blk", 4), z2, 0)
    wide = join(wide, swap(wide, "blk", 2), z1, 1)
    wide = wide.reshape(2, 2, 2, rows // 2, width)
    part_a, part_b = wide[:, :, 0], wide[:, :, 1]
    from_a, from_b = swap(part_a, "blk", 1), swap(part_b, "ulysses", 2)
    part_a = join(part_a, from_a, x, 2)
    part_b = join(part_b, from_b, y, 2)
    from_a, from_b = swap(part_a, "ulysses", 2), swap(part_b, "blk", 1)
    part_a = join(part_a, from_a, y, 3)
    part_b = join(part_b, from_b, x, 2)
    wide = jnp.stack([part_a, part_b], axis=4).reshape(16 * rows, width)
    wide, also = lax.optimization_barrier((wide, also))
    return wide, swap(wide, "ulysses", 1), also


def halve(keep, got, axis, bit, dim):
    total = (keep.astype(F32) + got.astype(F32)).astype(BF)
    side = my_bit(axis, bit)
    keep = lax.dynamic_index_in_dim(total, side, dim, keepdims=False)
    give = lax.dynamic_index_in_dim(total, 1 - side, dim, keepdims=False)
    return keep, give


def exchange(value):
    return lax.all_to_all(value, AXES, split_axis=0, concat_axis=0, tiled=True)


def owner_slot(sequence, head):
    return sequence * 16 + head // SHARE * (SHARE + 1) + head % SHARE


def turn(values):
    lane = lax.broadcasted_iota(jnp.int32, values.shape, 1) % HEAD
    return jnp.where(
        lane < HEAD // 2,
        -pltpu.roll(values, LANES - HEAD // 2, 1),
        pltpu.roll(values, HEAD // 2, 1),
    )


def side_by_side(left, right):
    return jnp.concatenate([left, right], axis=1)


def smem():
    return pl.BlockSpec(memory_space=pltpu.SMEM)


def project_kernel(
    core, mine, other, gain, weight, cosine, sine, hidden, queries, key_rows, value_rows
):
    def one(tokens, slot):
        normed, inverse = normalize(tokens[...].astype(F32))
        low = (normed * gain[...]).astype(BF)
        hidden[slot] = low
        qkv = jnp.dot(low, weight[:, : 3 * HEAD], preferred_element_type=F32).astype(BF)
        both = qkv[:, :LANES].astype(F32)
        both = (both * cosine[slot] + turn(both) * sine[slot]).astype(BF)
        queries[slot] = both[:, :HEAD] * BF(HEAD**-0.5)
        key_rows[slot] = both[:, HEAD:]
        value_rows[slot] = qkv[:, LANES:]

    one(mine, core[0])
    one(other, 1 - core[0])


def project(core, mine, other, gain, weight, cosine, sine):
    length, width = mine.shape
    by_row = pl.BlockSpec((BLOCK, width), lambda i: (i, 0))
    by_pair = lambda columns: pl.BlockSpec((2, BLOCK, columns), lambda i: (0, i, 0))
    whole = lambda shape: pl.BlockSpec(shape, lambda i: (0, 0))
    return pl.pallas_call(
        project_kernel,
        grid=(length // BLOCK,),
        in_specs=[
            smem(),
            by_row,
            by_row,
            whole((1, width)),
            whole(weight.shape),
            by_pair(LANES),
            by_pair(LANES),
        ],
        out_specs=[by_pair(width), by_pair(HEAD), by_pair(HEAD), by_pair(HEAD)],
        out_shape=[jax.ShapeDtypeStruct((2, length, width), BF)]
        + [jax.ShapeDtypeStruct((2, length, HEAD), BF)] * 3,
        name="project",
    )(core, mine, other, gain, weight, cosine, sine)


def attend_kernel(queries, key_rows, value_rows, weights, attn32, total, send):
    scores = lax.dot_general(
        queries[...], key_rows[...], BY_COLUMN, preferred_element_type=F32
    )
    top = jnp.max(scores, axis=-1, keepdims=True)
    expo = jnp.exp(scores - top)
    row_total = jnp.sum(expo, axis=-1, keepdims=True)
    low = expo.astype(BF)
    weights[...] = low
    mixed = jnp.dot(low, value_rows[...], preferred_element_type=F32) / row_total
    attn32[...] = mixed
    total[...] = row_total
    mixed = mixed.astype(BF)
    for i in range(BLOCK // 64):
        rows = mixed[64 * i : 64 * i + 64]
        send[i, 0] = side_by_side(rows[:32], rows[32:])


def attend(queries, key_rows, value_rows):
    length = queries.shape[0]
    by_row = lambda columns: pl.BlockSpec((BLOCK, columns), lambda i: (i, 0))
    whole = pl.BlockSpec((length, HEAD), lambda i: (0, 0))
    steps = length // BLOCK
    return pl.pallas_call(
        attend_kernel,
        grid=(steps,),
        in_specs=[by_row(HEAD), whole, whole],
        out_specs=[
            by_row(length),
            by_row(HEAD),
            by_row(1),
            pl.BlockSpec(
                (BLOCK // 64, 1, 32, LANES), lambda i: (i % (steps // 2), i // (steps // 2), 0, 0)
            ),
        ],
        out_shape=[
            jax.ShapeDtypeStruct((length, length), BF),
            jax.ShapeDtypeStruct((length, HEAD), F32),
            jax.ShapeDtypeStruct((length, 1), F32),
            jax.ShapeDtypeStruct((length // 128, 2, 32, LANES), BF),
        ],
        name="attend",
    )(queries, key_rows, value_rows)


def middle_kernel(
    got, tokens, late, gain, grad_out, layer_output, send, attn, hidden, grad_joint, activation,
    branch, grad_middle
):
    width = tokens.shape[1]
    hidden_units = activation.shape[1]
    cut = 2 * hidden_units
    for s in range(2):
        for h in range(0, HEADS, 2):
            left, right = got[owner_slot(s, h)], got[owner_slot(s, h + 1)]
            columns = slice(h * HEAD, h * HEAD + LANES)
            attn[64 * s : 64 * s + 32, columns] = side_by_side(left[:, :HEAD], right[:, :HEAD])
            attn[64 * s + 32 : 64 * s + 64, columns] = side_by_side(
                left[:, HEAD:], right[:, HEAD:]
            )
    attn_weight = late[:, cut : cut + width]
    middle = tokens[...].astype(F32) + jnp.dot(
        attn[...], attn_weight, preferred_element_type=F32
    )
    normed, inverse = normalize(middle)
    low = (normed * gain[...]).astype(BF)
    hidden[...] = low
    first = jnp.dot(low, late[:, :hidden_units], preferred_element_type=F32)
    gate = jnp.dot(low, late[:, hidden_units:cut], preferred_element_type=F32)
    cumulative = 0.5 * (1.0 + lax.erf(first * (0.5**0.5)))
    bent = first * cumulative
    active = (bent * gate).astype(BF)
    activation[...] = active
    out_weight = late[:, cut + width :]
    layer_output[...] = (
        middle + lax.dot_general(active, out_weight, BY_COLUMN, preferred_element_type=F32)
    ).astype(BF)
    grad_act = jnp.dot(grad_out[...], out_weight, preferred_element_type=F32)
    density = jnp.exp(-0.5 * first * first) * 0.3989422804014327
    grad_joint[:, :hidden_units] = (grad_act * gate * (cumulative + first * density)).astype(BF)
    grad_joint[:, hidden_units:] = (grad_act * bent).astype(BF)
    grad_hidden = lax.dot_general(
        grad_joint[...], late[:, :cut], BY_COLUMN, preferred_element_type=F32
    )
    total = grad_out[...].astype(F32) + norm_back(grad_hidden * gain[...], normed, inverse)
    grad_middle[...] = total
    branch_low = total.astype(BF)
    branch[...] = branch_low
    grad_cat = lax.dot_general(
        branch_low, attn_weight, BY_COLUMN, preferred_element_type=F32
    ).astype(BF)
    for s in range(2):
        for h in range(HEADS):
            rows = grad_cat[64 * s : 64 * s + 64, h * HEAD : (h + 1) * HEAD]
            block = side_by_side(rows[:32], rows[32:])
            send[owner_slot(s, h)] = block
            if h % SHARE == SHARE - 1:
                send[owner_slot(s, h) + 1] = block


def middle_part(got, tokens, late, gain, grad_out):
    rows, width = tokens.shape
    hidden_units = (late.shape[1] - width) // 3
    shapes = [
        ((rows, width), BF),
        (got.shape, BF),
        ((rows, width), BF),
        ((rows, width), BF),
        ((rows, 2 * hidden_units), BF),
        ((rows, hidden_units), BF),
        ((rows, width), BF),
        ((rows, width), F32),
    ]
    return pl.pallas_call(
        middle_kernel,
        out_shape=[jax.ShapeDtypeStruct(shape, kind) for shape, kind in shapes],
        name="middle_part",
    )(got, tokens, late, gain, grad_out)


def weight_grads_kernel(
    core, hidden, attn, grad_out, joint, branch, active, keep, give, *, in_tiles, attn_tiles
):
    tile = pl.program_id(0)

    def write(left, right):
        total = lax.dot_general(left[...], right[...], BY_ROW, preferred_element_type=F32)
        total = total.reshape(keep.shape[0], 2, *keep.shape[1:])
        first, second = total[:, 0], total[:, 1]
        keep[...] = jnp.where(core[0] == 0, first, second).astype(BF)
        give[...] = jnp.where(core[0] == 0, second, first).astype(BF)

    @pl.when(tile < in_tiles)
    def _():
        write(hidden, joint)

    @pl.when((tile >= in_tiles) & (tile < in_tiles + attn_tiles))
    def _():
        write(attn, branch)

    @pl.when(tile >= in_tiles + attn_tiles)
    def _():
        write(grad_out, active)


def weight_grads(core, hidden, attn, grad_out, joint, branch, active, rows_here):
    rows, width = hidden.shape
    in_tiles, attn_tiles = joint.shape[1] // TILE, width // TILE
    out_tiles = active.shape[1] // TILE
    tiles = in_tiles + attn_tiles + out_tiles
    whole = pl.BlockSpec((rows, width), lambda t: (0, 0))
    part = lambda first, count: pl.BlockSpec(
        (rows, TILE), lambda t: (0, jnp.clip(t - first, 0, count - 1))
    )
    pairs = width // (2 * rows_here)
    result = pl.BlockSpec((pairs, rows_here, TILE), lambda t: (0, 0, t))
    return pl.pallas_call(
        functools.partial(weight_grads_kernel, in_tiles=in_tiles, attn_tiles=attn_tiles),
        grid=(tiles,),
        in_specs=[
            smem(),
            whole,
            whole,
            whole,
            part(0, in_tiles),
            part(in_tiles, attn_tiles),
            part(in_tiles + attn_tiles, out_tiles),
        ],
        out_specs=[result, result],
        out_shape=[jax.ShapeDtypeStruct((pairs, rows_here, tiles * TILE), BF)] * 2,
        name="weight_grads",
    )(core, hidden, attn, grad_out, joint, branch, active)


def attend_back_kernel(
    got, attn32, total, weights, queries, key_rows, value_rows, cosine, sine, send, grad_both,
    grad_low, grad_query, grad_key, grad_value
):
    step = pl.program_id(0)

    @pl.when(step == 0)
    def _():
        grad_key[...] = jnp.zeros_like(grad_key)
        grad_value[...] = jnp.zeros_like(grad_value)

    pieces = []
    for i in range(BLOCK // 64):
        block = got[i, 0]
        pieces += [block[:, :HEAD], block[:, HEAD:]]
    grad = jnp.concatenate(pieces, axis=0)
    wide = grad.astype(F32)
    dots = jnp.sum(wide * attn32[...], axis=-1, keepdims=True)
    grad_probs = lax.dot_general(
        grad, value_rows[...], BY_COLUMN, preferred_element_type=F32
    )
    inverse = 1.0 / total[...]
    low = weights[...]
    grad_scores = ((low.astype(F32) * inverse) * (grad_probs - dots)).astype(BF)
    grad_query[pl.ds(step * BLOCK, BLOCK), :] = HEAD**-0.5 * jnp.dot(
        grad_scores, key_rows[...], preferred_element_type=F32
    )
    grad_value[...] += lax.dot_general(
        low, (wide * inverse).astype(BF), BY_ROW, preferred_element_type=F32
    )
    grad_key[...] += lax.dot_general(
        grad_scores, queries[...], BY_ROW, preferred_element_type=F32
    )

    @pl.when(step == pl.num_programs(0) - 1)
    def _():
        length = grad_key.shape[0]
        both = side_by_side(grad_query[...], grad_key[...])
        both = (both * cosine[...] - turn(both) * sine[...]).astype(BF)
        grad_both[...] = both
        low = grad_value[...].astype(BF)
        grad_low[...] = low
        for i in range(length // 64):
            core, pair = i // (length // 128), i % (length // 128)
            rows = low[64 * i : 64 * i + 64]
            send[pair, core, :64] = both[64 * i : 64 * i + 64]
            send[pair, core, 64:] = side_by_side(rows[:32], rows[32:])


def attend_back(got, attn32, total, weights, queries, key_rows, value_rows, cosine, sine):
    length = queries.shape[0]
    steps = length // BLOCK
    by_row = lambda columns: pl.BlockSpec((BLOCK, columns), lambda i: (i, 0))
    whole = lambda *shape: pl.BlockSpec(shape, lambda i: (0,) * len(shape))
    send = (length // 128, 2, 96, LANES)
    return pl.pallas_call(
        attend_back_kernel,
        grid=(steps,),
        in_specs=[
            pl.BlockSpec(
                (BLOCK // 64, 1, 32, LANES), lambda i: (i % (steps // 2), i // (steps // 2), 0, 0)
            ),
            by_row(HEAD),
            by_row(1),
            by_row(length),
            by_row(HEAD),
            whole(length, HEAD),
            whole(length, HEAD),
            whole(length, LANES),
            whole(length, LANES),
        ],
        out_specs=[whole(*send), whole(length, LANES), whole(length, HEAD)],
        out_shape=[
            jax.ShapeDtypeStruct(send, BF),
            jax.ShapeDtypeStruct((length, LANES), BF),
            jax.ShapeDtypeStruct((length, HEAD), BF),
        ],
        scratch_shapes=[pltpu.VMEM((length, HEAD), F32)] * 3,
        name="attend_back",
    )(got, attn32, total, weights, queries, key_rows, value_rows, cosine, sine)


def head_grads_kernel(hidden, both, low, result):
    @pl.when(pl.program_id(0) == 0)
    def _():
        result[...] = jnp.zeros_like(result)

    result[:, :LANES] += lax.dot_general(
        hidden[...], both[...], BY_ROW, preferred_element_type=F32
    )
    result[:, LANES:] += lax.dot_general(
        hidden[...], low[...], BY_ROW, preferred_element_type=F32
    )


def head_grads(hidden, both, low):
    length, width = hidden.shape
    by_row = lambda columns: pl.BlockSpec((2 * BLOCK, columns), lambda i: (i, 0))
    return pl.pallas_call(
        head_grads_kernel,
        grid=(length // (2 * BLOCK),),
        in_specs=[by_row(width), by_row(LANES), by_row(HEAD)],
        out_specs=pl.BlockSpec((width, 3 * HEAD), lambda i: (0, 0)),
        out_shape=jax.ShapeDtypeStruct((width, 3 * HEAD), F32),
        name="head_grads",
    )(hidden, both, low)


def last_kernel(got, weight, tokens, gain, grad_middle, result, grads):
    width = tokens.shape[1]
    for s in range(2):
        for h in range(0, HEADS, 2):
            left, right = got[owner_slot(s, h)], got[owner_slot(s, h + 1)]
            top, end = slice(64 * s, 64 * s + 64), slice(64 * s + 64, 64 * s + 128)
            place = lambda j: slice(j * width + h * HEAD, j * width + h * HEAD + LANES)
            grads[top, place(0)] = side_by_side(left[:64, :HEAD], right[:64, :HEAD])
            grads[top, place(1)] = side_by_side(left[:64, HEAD:], right[:64, HEAD:])
            grads[64 * s : 64 * s + 32, place(2)] = side_by_side(
                left[64:, :HEAD], right[64:, :HEAD]
            )
            grads[64 * s + 32 : 64 * s + 64, place(2)] = side_by_side(
                left[64:, HEAD:], right[64:, HEAD:]
            )
    grad_hidden = lax.dot_general(
        grads[...], weight[...], BY_COLUMN, preferred_element_type=F32
    )
    normed, inverse = normalize(tokens[...].astype(F32))
    result[...] = (
        grad_middle[...] + norm_back(grad_hidden * gain[...], normed, inverse)
    ).astype(BF)


def last_part(got, weight, tokens, gain, grad_middle):
    return pl.pallas_call(
        last_kernel,
        out_shape=jax.ShapeDtypeStruct(tokens.shape, BF),
        scratch_shapes=[pltpu.VMEM((tokens.shape[0], weight.shape[1]), BF)],
        name="last_part",
    )(got, weight, tokens, gain, grad_middle)


def collect_kernel(got, weight, gain, result, gain_grad):
    width = result.shape[1] // 3
    for h in range(0, HEADS, 2):
        left = got[owner_slot(0, h)].astype(F32) + got[owner_slot(1, h)].astype(F32)
        right = got[owner_slot(0, h + 1)].astype(F32) + got[owner_slot(1, h + 1)].astype(F32)
        for j in range(3):
            columns = slice(j * HEAD, (j + 1) * HEAD)
            place = slice(j * width + h * HEAD, j * width + h * HEAD + LANES)
            result[:, place] = side_by_side(left[:, columns], right[:, columns])
    product = result[...] * weight[...].astype(F32)
    gain_grad[...] = jnp.sum(product, axis=1, keepdims=True) / gain[...]


def collect(got, weight, gain):
    rows, columns = weight.shape
    return pl.pallas_call(
        collect_kernel,
        out_shape=[
            jax.ShapeDtypeStruct((rows, columns), F32),
            jax.ShapeDtypeStruct((rows, 1), F32),
        ],
        name="collect",
    )(got, weight, gain)


def owner_body(
    tokens, attn_gain, qkv_weight, attn_out_weight, mlp_gain, in_weight, out_weight, cotangent
):
    sequences, per_device, model_width = tokens.shape
    hidden_units = out_weight.shape[0]
    rows_here = qkv_weight.shape[0]
    rows = sequences * per_device
    length = per_device * 32
    core = my_bit("ulysses", 1).astype(jnp.int32).reshape(1)
    late = jnp.concatenate([in_weight, attn_out_weight, jnp.transpose(out_weight)], axis=1)
    late_full = lax.all_gather(late, AXES, axis=0, tiled=True)
    by_head = qkv_weight.reshape(rows_here, 3, HEADS, HEAD).transpose(2, 0, 1, 3)
    by_head = by_head.reshape(HEADS, rows_here, 3 * HEAD)
    gains = jnp.stack([attn_gain, mlp_gain], axis=1)
    gains = jnp.broadcast_to(jnp.pad(gains, ((0, 0), (0, HEAD - 2))), (HEADS, rows_here, HEAD))
    packed = jnp.concatenate([by_head, gains], axis=2)
    packed = packed.reshape(HEADS // SHARE, SHARE, rows_here, 4 * HEAD)
    packed = jnp.concatenate([packed, packed[:, -1:]], axis=1)
    packed = jnp.broadcast_to(packed[None], (2,) + packed.shape)
    mixed = exchange(packed.reshape(32, rows_here, 4 * HEAD))
    mine, other, mixed = gather_sequence(tokens, mixed)
    weight_here = mixed.reshape(model_width, 4 * HEAD)
    gain_one = weight_here[:, 3 * HEAD].reshape(1, model_width).astype(F32)
    gain_two = weight_here[:, 3 * HEAD + 1].reshape(1, model_width).astype(F32)
    cosine, sine = rotation(0, length, HEAD)
    by_core = lambda table: jnp.tile(
        table.reshape(length // 128, 2, 64, HEAD).transpose(1, 0, 2, 3).reshape(length, HEAD),
        (1, 2),
    )
    cosine, sine = by_core(cosine), by_core(sine)
    hidden_one, queries, key_rows, value_rows = project(
        core,
        mine,
        other,
        gain_one,
        weight_here,
        cosine.reshape(2, length // 2, LANES),
        sine.reshape(2, length // 2, LANES),
    )
    queries, key_rows, value_rows = (
        value.reshape(length, HEAD) for value in (queries, key_rows, value_rows)
    )
    weights_low, attn32, row_total, send = attend(queries, key_rows, value_rows)
    got = exchange(send.reshape(32, 32, LANES))
    flat_tokens = tokens.reshape(rows, model_width)
    grad_out = cotangent.reshape(rows, model_width)
    layer_output, send, attn_cat, hidden_two, grad_joint, activation, branch, grad_middle = (
        middle_part(got, flat_tokens, late_full, gain_two, grad_out)
    )
    got = exchange(send)
    keep, give = weight_grads(
        core, hidden_two, attn_cat, grad_out, grad_joint, branch, activation, rows_here
    )
    came = swap(give, "ulysses", 1)
    got, keep, came = lax.optimization_barrier((got, keep, came))
    columns = keep.shape[-1]
    half = columns // 256 * 128
    view = (2, 2, 2, 2, rows_here)
    cut = lambda value: (
        value[..., :half].reshape(*view, half),
        value[..., half:].reshape(*view, columns - half),
    )
    (keep_a, keep_b), (came_a, came_b) = cut(keep), cut(came)
    keep_a, give_a = halve(keep_a, came_a, "blk", 1, 2)
    keep_b, give_b = halve(keep_b, came_b, "ulysses", 2, 3)
    came_a, came_b = swap(give_a, "blk", 1), swap(give_b, "ulysses", 2)
    send, grad_both, grad_low = attend_back(
        got.reshape(length // 128, 2, 32, LANES),
        attn32,
        row_total,
        weights_low,
        queries,
        key_rows,
        value_rows,
        cosine,
        sine,
    )
    qkv_full = lax.all_gather(qkv_weight, AXES, axis=0, tiled=True)
    send, came_a, came_b = lax.optimization_barrier((send, came_a, came_b))
    got = exchange(send.reshape(32, 96, LANES))
    keep_a, give_a = halve(keep_a, came_a, "ulysses", 2, 2)
    keep_b, give_b = halve(keep_b, came_b, "blk", 1, 2)
    came_a, came_b = swap(give_a, "ulysses", 2), swap(give_b, "blk", 1)
    head_grad = head_grads(hidden_one.reshape(length, model_width), grad_both, grad_low)
    got, head_grad, came_a, came_b = lax.optimization_barrier((got, head_grad, came_a, came_b))
    got_grads = exchange(head_grad.astype(BF).reshape(32, rows_here, 3 * HEAD))
    keep_a, give_a = halve(keep_a, came_a, "blk", 2, 1)
    keep_b, give_b = halve(keep_b, came_b, "blk", 2, 1)
    came_a, came_b = swap(give_a, "blk", 2), swap(give_b, "blk", 2)
    input_grad = last_part(got, qkv_full, flat_tokens, gain_one, grad_middle)
    input_grad = input_grad.reshape(sequences, per_device, model_width)
    keep_a, give_a = halve(keep_a, came_a, "blk", 4, 0)
    keep_b, give_b = halve(keep_b, came_b, "blk", 4, 0)
    came_a, came_b = swap(give_a, "blk", 4), swap(give_b, "blk", 4)
    shard_qkv, shard_one = collect(
        got_grads, qkv_weight, attn_gain.astype(F32).reshape(rows_here, 1)
    )
    part_a = keep_a.astype(F32) + came_a.astype(F32)
    part_b = keep_b.astype(F32) + came_b.astype(F32)
    shards = jnp.concatenate([part_a, part_b], axis=1)
    shard_in = shards[:, : 2 * hidden_units]
    shard_attn = shards[:, 2 * hidden_units : 2 * hidden_units + model_width]
    shard_out = jnp.transpose(shards[:, 2 * hidden_units + model_width :])
    shard_two = jnp.sum(shard_in * in_weight.astype(F32), axis=1) / mlp_gain.astype(F32)
    return (
        layer_output.reshape(sequences, per_device, model_width),
        input_grad,
        shard_one.reshape(rows_here),
        shard_qkv,
        shard_attn,
        shard_two,
        shard_in,
        shard_out,
    )


def solution(mesh):
    placed = (
        P(None, ("blk", "ulysses"), None),
        P(("blk", "ulysses")),
        P(("blk", "ulysses"), None),
        P(("blk", "ulysses"), None),
        P(("blk", "ulysses")),
        P(("blk", "ulysses"), None),
        P(None, ("blk", "ulysses")),
        P(None, ("blk", "ulysses"), None),
    )
    sizes = (mesh.shape["blk"], mesh.shape["ulysses"])
    return jax.shard_map(
        owner_body if sizes == (8, 4) else ring_body,
        mesh=mesh,
        in_specs=placed,
        out_specs=(
            P(None, ("blk", "ulysses"), None),
            P(None, ("blk", "ulysses"), None),
            P(("blk", "ulysses")),
            P(("blk", "ulysses"), None),
            P(("blk", "ulysses"), None),
            P(("blk", "ulysses")),
            P(("blk", "ulysses"), None),
            P(None, ("blk", "ulysses")),
        ),
        check_vma=False,
    )
```

```python
import functools

import jax
import jax.numpy as jnp
from jax import lax
from jax.experimental import pallas as pl
from jax.experimental.pallas import tpu as pltpu
from jax.sharding import PartitionSpec as P

HEAD = 64


EPSILON = 1e-05
THETA = 160000.0


def from_behind(value, axis, by):
    size = lax.axis_size(axis)
    return lax.ppermute(value, axis, [(i, (i + by) % size) for i in range(size)])


def normalize(values):
    center = values - jnp.mean(values, axis=-1, keepdims=True)
    inverse = lax.rsqrt(jnp.mean(center * center, axis=-1, keepdims=True) + EPSILON)
    return (center * inverse, inverse)


def norm_back(grad_normed, normed, inverse):
    first_mean = jnp.mean(grad_normed, axis=-1, keepdims=True)
    second_mean = jnp.mean(grad_normed * normed, axis=-1, keepdims=True)
    return inverse * (grad_normed - first_mean - normed * second_mean)


def rotation(first_row, row_count, head_width):
    half_width = head_width // 2
    frequency = THETA ** (-(jnp.arange(half_width, dtype=jnp.float32) * 2.0) / head_width)
    positions = (first_row + jnp.arange(row_count, dtype=jnp.int32)).astype(jnp.float32)
    angles = positions[:, None] * frequency[None, :]
    cosine_table = jnp.concatenate([jnp.cos(angles), jnp.cos(angles)], axis=-1)
    sine_table = jnp.concatenate([jnp.sin(angles), jnp.sin(angles)], axis=-1)
    return (cosine_table, sine_table)


def rotate(values, cosine_table, sine_table, direction):
    half_width = values.shape[-1] // 2
    turned = jnp.concatenate([-values[..., half_width:], values[..., :half_width]], axis=-1)
    return values * cosine_table[:, None, :] + direction * turned * sine_table[:, None, :]


def block_grads(
    query_part,
    key_part,
    value_part,
    grad_part,
    log_part,
    dots_part,
    top_part,
    total_part,
    score_scale,
):
    scores = (
        jnp.einsum("sqhd,skhd->shqk", query_part, key_part, preferred_element_type=jnp.float32)
        * score_scale
    )
    probs = jnp.exp(scores - log_part[..., None])
    grad_probs = jnp.einsum(
        "sqhd,skhd->shqk", grad_part, value_part, preferred_element_type=jnp.float32
    )
    grad_scores = (probs * (grad_probs - dots_part[..., None])).astype(jnp.bfloat16)
    weights_low = jnp.exp(scores - top_part[..., None]).astype(jnp.bfloat16)
    grad_scaled = grad_part.astype(jnp.float32) / jnp.transpose(total_part, (0, 2, 1))[..., None]
    value_term = jnp.einsum("shqk,sqhd->skhd", weights_low.astype(jnp.float32), grad_scaled)
    return (value_term, grad_scores)


def ring_body(
    tokens, attn_gain, qkv_weight, attn_out_weight, mlp_gain, in_weight, out_weight, cotangent
):
    sequences, per_device, model_width = tokens.shape
    groups = lax.axis_size("ulysses")
    cycle_size = lax.axis_size("blk")
    group_width = model_width // groups
    heads_here = group_width // HEAD
    group_rows = per_device * groups
    score_scale = HEAD ** (-0.5)
    qkv_full, attn_full, in_full, out_full, gain_one, gain_two = (
        lax.all_gather(qkv_weight, ("blk", "ulysses"), axis=0, tiled=True),
        lax.all_gather(attn_out_weight, ("blk", "ulysses"), axis=0, tiled=True),
        lax.all_gather(in_weight, ("blk", "ulysses"), axis=0, tiled=True),
        lax.all_gather(out_weight, ("blk", "ulysses"), axis=1, tiled=True),
        lax.all_gather(attn_gain, ("blk", "ulysses"), axis=0, tiled=True),
        lax.all_gather(mlp_gain, ("blk", "ulysses"), axis=0, tiled=True),
    )
    gain_one = gain_one.astype(jnp.float32)
    gain_two = gain_two.astype(jnp.float32)
    hidden_units = out_full.shape[0]
    inputs_wide = tokens.astype(jnp.float32).reshape(sequences * per_device, model_width)
    normed_one, inverse_one = normalize(inputs_wide)
    hidden_one = (normed_one * gain_one).astype(jnp.bfloat16)
    qkv = jnp.dot(hidden_one, qkv_full, preferred_element_type=jnp.float32).astype(jnp.bfloat16)
    packed = qkv.reshape(sequences, per_device, 3, groups, group_width)
    headwise = lax.all_to_all(packed, "ulysses", split_axis=3, concat_axis=1, tiled=True)
    headwise = headwise.reshape(sequences, group_rows, 3, heads_here, HEAD)
    cosine_table, sine_table = rotation(lax.axis_index("blk") * group_rows, group_rows, HEAD)
    queries = rotate(headwise[:, :, 0].astype(jnp.float32), cosine_table, sine_table, 1.0).astype(
        jnp.bfloat16
    )
    key_rows = rotate(headwise[:, :, 1].astype(jnp.float32), cosine_table, sine_table, 1.0).astype(
        jnp.bfloat16
    )
    value_rows = headwise[:, :, 2]
    start_top = jnp.full((sequences, heads_here, group_rows), -1e30, jnp.float32)
    zeros_rows = jnp.zeros((sequences, group_rows, heads_here, HEAD), jnp.float32)
    key_piece = lax.all_gather(key_rows, "blk", axis=1, tiled=True)
    value_piece = lax.all_gather(value_rows, "blk", axis=1, tiled=True)
    scores = (
        jnp.einsum("sqhd,skhd->shqk", queries, key_piece, preferred_element_type=jnp.float32)
        * score_scale
    )
    new_top = jnp.maximum(start_top, jnp.max(scores, axis=-1))
    weights = jnp.exp(scores - new_top[..., None])
    attend_row_total = jnp.sum(weights, axis=-1)
    update = jnp.einsum(
        "shqk,skhd->sqhd",
        weights.astype(jnp.bfloat16),
        value_piece,
        preferred_element_type=jnp.float32,
    )
    weighted = update
    row_top, row_total, weighted = (new_top, attend_row_total, weighted)
    log_total = row_top + jnp.log(row_total)
    attn_wide = weighted / jnp.transpose(row_total, (0, 2, 1))[..., None]
    attn_low = attn_wide.astype(jnp.bfloat16).reshape(sequences, group_rows, 1, group_width)
    token_rows = lax.all_to_all(attn_low, "ulysses", split_axis=1, concat_axis=2, tiled=True)
    attn_cat = token_rows.reshape(sequences * per_device, model_width)
    middle = inputs_wide + jnp.dot(attn_cat, attn_full, preferred_element_type=jnp.float32)
    normed_two, inverse_two = normalize(middle)
    hidden_two = (normed_two * gain_two).astype(jnp.bfloat16)
    joint = jnp.dot(hidden_two, in_full, preferred_element_type=jnp.float32)

    def geglu(joint_pre):
        return (
            jax.nn.gelu(joint_pre[:, :hidden_units], approximate=False)
            * joint_pre[:, hidden_units:]
        )

    act_wide, geglu_back = jax.vjp(geglu, joint)
    activation = act_wide.astype(jnp.bfloat16)
    result = middle + jnp.dot(activation, out_full, preferred_element_type=jnp.float32)
    layer_output = result.astype(jnp.bfloat16).reshape(sequences, per_device, model_width)
    grad_out = cotangent.reshape(sequences * per_device, model_width)
    grad_wout = jnp.einsum("tf,td->fd", activation, grad_out, preferred_element_type=jnp.float32)
    grad_act = jnp.einsum("td,fd->tf", grad_out, out_full, preferred_element_type=jnp.float32)
    grad_joint = geglu_back(grad_act)[0].astype(jnp.bfloat16)
    grad_win = jnp.einsum("tc,tf->cf", hidden_two, grad_joint, preferred_element_type=jnp.float32)
    grad_hidden_two = jnp.einsum(
        "tf,cf->tc", grad_joint, in_full, preferred_element_type=jnp.float32
    )
    grad_gain_two = jnp.sum(grad_hidden_two * normed_two, axis=0)
    grad_middle = grad_out.astype(jnp.float32) + norm_back(
        grad_hidden_two * gain_two, normed_two, inverse_two
    )
    grad_branch = grad_middle.astype(jnp.bfloat16)
    grad_wattn = jnp.einsum("tc,td->cd", attn_cat, grad_branch, preferred_element_type=jnp.float32)
    grad_cat = jnp.einsum(
        "td,cd->tc", grad_branch, attn_full, preferred_element_type=jnp.float32
    ).astype(jnp.bfloat16)
    grad_heads_in = lax.all_to_all(
        grad_cat.reshape(sequences, per_device, groups, group_width),
        "ulysses",
        split_axis=2,
        concat_axis=1,
        tiled=True,
    )
    grad_attn = grad_heads_in.reshape(sequences, group_rows, heads_here, HEAD)
    row_dots = jnp.transpose(jnp.sum(grad_attn.astype(jnp.float32) * attn_wide, axis=-1), (0, 2, 1))

    def cycle_step(step_index, state_now):
        key_now, value_now, grad_key, grad_value, grad_query = state_now
        value_term, grad_scores = block_grads(
            queries,
            key_now,
            value_now,
            grad_attn,
            log_total,
            row_dots,
            row_top,
            row_total,
            score_scale,
        )
        grad_value = grad_value + value_term
        grad_key = grad_key + score_scale * jnp.einsum(
            "shqk,sqhd->skhd", grad_scores, queries, preferred_element_type=jnp.float32
        )
        grad_query = grad_query + score_scale * jnp.einsum(
            "shqk,skhd->sqhd", grad_scores, key_now, preferred_element_type=jnp.float32
        )
        key_now, value_now = from_behind((key_now, value_now), "blk", 1)
        grad_key, grad_value = (
            from_behind(grad_key.astype(jnp.bfloat16), "blk", 1).astype(grad_key.dtype),
            from_behind(grad_value.astype(jnp.bfloat16), "blk", 1).astype(grad_value.dtype),
        )
        return (key_now, value_now, grad_key, grad_value, grad_query)

    final_state = lax.fori_loop(
        0, cycle_size, cycle_step, (key_rows, value_rows, zeros_rows, zeros_rows, zeros_rows)
    )
    grad_key, grad_value, grad_query = (final_state[2], final_state[3], final_state[4])
    grad_query = rotate(grad_query, cosine_table, sine_table, -1.0)
    grad_key = rotate(grad_key, cosine_table, sine_table, -1.0)
    grad_stack = jnp.stack([grad_query, grad_key, grad_value], axis=2).astype(jnp.bfloat16)
    grad_stack = grad_stack.reshape(sequences, group_rows, 3, 1, group_width)
    grad_tokens = lax.all_to_all(grad_stack, "ulysses", split_axis=1, concat_axis=3, tiled=True)
    grad_qkv = grad_tokens.reshape(sequences * per_device, 3 * model_width)
    grad_wqkv = jnp.einsum("tc,tf->cf", hidden_one, grad_qkv, preferred_element_type=jnp.float32)
    grad_hidden_one = jnp.einsum(
        "tf,cf->tc", grad_qkv, qkv_full, preferred_element_type=jnp.float32
    )
    grad_gain_one = jnp.sum(grad_hidden_one * normed_one, axis=0)
    grad_input = grad_middle + norm_back(grad_hidden_one * gain_one, normed_one, inverse_one)
    input_grad = grad_input.astype(jnp.bfloat16).reshape(sequences, per_device, model_width)
    shard_qkv, shard_attn, shard_in, shard_out, shard_one, shard_two = (
        lax.psum_scatter(grad_wqkv, ("blk", "ulysses"), scatter_dimension=0, tiled=True),
        lax.psum_scatter(grad_wattn, ("blk", "ulysses"), scatter_dimension=0, tiled=True),
        lax.psum_scatter(grad_win, ("blk", "ulysses"), scatter_dimension=0, tiled=True),
        lax.psum_scatter(grad_wout, ("blk", "ulysses"), scatter_dimension=1, tiled=True),
        lax.psum_scatter(grad_gain_one, ("blk", "ulysses"), scatter_dimension=0, tiled=True),
        lax.psum_scatter(grad_gain_two, ("blk", "ulysses"), scatter_dimension=0, tiled=True),
    )
    return (
        layer_output,
        input_grad,
        shard_one,
        shard_qkv,
        shard_attn,
        shard_two,
        shard_in,
        shard_out,
    )


AXES = ("blk", "ulysses")
BF = jnp.bfloat16
F32 = jnp.float32
HEADS = 12
SHARE = 3
BLOCK = 256
LANES = 128
TILE = 384
BY_COLUMN = (((1,), (1,)), ((), ()))
BY_ROW = (((0,), (0,)), ((), ()))


def swap(value, axis, bit):
    size = lax.axis_size(axis)
    return lax.ppermute(value, axis, [(i, i ^ bit) for i in range(size)])


def my_bit(axis, bit):
    return (lax.axis_index(axis) // bit) % 2


def join(mine, other, side, axis):
    first = jnp.stack([mine, other], axis=axis)
    second = jnp.stack([other, mine], axis=axis)
    return jnp.where(side == 0, first, second)


def gather_sequence(tokens, also):
    sequences, rows, width = tokens.shape
    z2, z1, x = my_bit("blk", 4), my_bit("blk", 2), my_bit("blk", 1)
    y = my_bit("ulysses", 2)
    keep = lax.dynamic_index_in_dim(tokens, z2, 0, keepdims=False)
    give = lax.dynamic_index_in_dim(tokens, 1 - z2, 0, keepdims=False)
    near = join(keep, swap(keep, "blk", 2), z1, 0)
    far = join(swap(give, "blk", 4), swap(give, "blk", 6), z1, 0)
    wide = join(near, far, z2, 0).reshape(2, 2, 2, rows // 2, width)
    part_a, part_b = wide[:, :, 0], wide[:, :, 1]
    from_a, from_b = swap(part_a, "blk", 1), swap(part_b, "ulysses", 2)
    part_a = join(part_a, from_a, x, 2)
    part_b = join(part_b, from_b, y, 2)
    from_a, from_b = swap(part_a, "ulysses", 2), swap(part_b, "blk", 1)
    part_a = join(part_a, from_a, y, 3)
    part_b = join(part_b, from_b, x, 2)
    wide = jnp.stack([part_a, part_b], axis=4).reshape(16 * rows, width)
    wide, also = lax.optimization_barrier((wide, also))
    return wide, swap(wide, "ulysses", 1), also


def halve(keep, got, axis, bit, dim):
    total = (keep.astype(F32) + got.astype(F32)).astype(BF)
    side = my_bit(axis, bit)
    keep = lax.dynamic_index_in_dim(total, side, dim, keepdims=False)
    give = lax.dynamic_index_in_dim(total, 1 - side, dim, keepdims=False)
    return keep, give


def turned_tables(rows):
    lane = jnp.arange(LANES, dtype=jnp.int32) % (HEAD // 2)
    frequency = THETA ** (-(lane.astype(F32) * 2.0) / HEAD)
    row = jnp.arange(rows, dtype=jnp.int32)
    half = rows // 2
    position = row % half // 64 * 128 + row // half * 64 + row % 64
    angles = position.astype(F32)[:, None] * frequency[None, :]
    return jnp.cos(angles), jnp.sin(angles)


def exchange(value):
    return lax.all_to_all(value, AXES, split_axis=0, concat_axis=0, tiled=True)


def owner_slot(sequence, head):
    return sequence * 16 + head // SHARE * (SHARE + 1) + head % SHARE


def turn(values):
    lane = lax.broadcasted_iota(jnp.int32, values.shape, 1) % HEAD
    return jnp.where(
        lane < HEAD // 2,
        -pltpu.roll(values, LANES - HEAD // 2, 1),
        pltpu.roll(values, HEAD // 2, 1),
    )


def side_by_side(left, right):
    return jnp.concatenate([left, right], axis=1)


def smem():
    return pl.BlockSpec(memory_space=pltpu.SMEM)


def project_kernel(
    core, mine, other, gain, weight, cosine, sine, hidden, queries, key_rows, value_rows
):
    def one(tokens, slot):
        normed, inverse = normalize(tokens[...].astype(F32))
        low = (normed * gain[...]).astype(BF)
        hidden[slot] = low
        qkv = jnp.dot(low, weight[:, : 3 * HEAD], preferred_element_type=F32).astype(BF)
        both = qkv[:, :LANES].astype(F32)
        both = (both * cosine[slot] + turn(both) * sine[slot]).astype(BF)
        queries[slot] = both[:, :HEAD] * BF(HEAD**-0.5)
        key_rows[slot] = both[:, HEAD:]
        value_rows[slot] = qkv[:, LANES:]

    one(mine, core[0])
    one(other, 1 - core[0])


def project(core, mine, other, gain, weight, cosine, sine):
    length, width = mine.shape
    by_row = pl.BlockSpec((BLOCK, width), lambda i: (i, 0))
    by_pair = lambda columns: pl.BlockSpec((2, BLOCK, columns), lambda i: (0, i, 0))
    whole = lambda shape: pl.BlockSpec(shape, lambda i: (0, 0))
    return pl.pallas_call(
        project_kernel,
        grid=(length // BLOCK,),
        in_specs=[
            smem(),
            by_row,
            by_row,
            whole((1, width)),
            whole(weight.shape),
            by_pair(LANES),
            by_pair(LANES),
        ],
        out_specs=[by_pair(width), by_pair(HEAD), by_pair(HEAD), by_pair(HEAD)],
        out_shape=[jax.ShapeDtypeStruct((2, length, width), BF)]
        + [jax.ShapeDtypeStruct((2, length, HEAD), BF)] * 3,
        name="project",
    )(core, mine, other, gain, weight, cosine, sine)


def attend_kernel(queries, key_rows, value_rows, weights, attn32, total, send):
    scores = lax.dot_general(
        queries[...], key_rows[...], BY_COLUMN, preferred_element_type=F32
    )
    top = jnp.max(scores, axis=-1, keepdims=True)
    expo = jnp.exp(scores - top)
    row_total = jnp.sum(expo, axis=-1, keepdims=True)
    low = expo.astype(BF)
    weights[...] = low
    mixed = jnp.dot(low, value_rows[...], preferred_element_type=F32) / row_total
    attn32[...] = mixed
    total[...] = row_total
    mixed = mixed.astype(BF)
    for i in range(BLOCK // 64):
        rows = mixed[64 * i : 64 * i + 64]
        send[i, 0] = side_by_side(rows[:32], rows[32:])


def attend(queries, key_rows, value_rows):
    length = queries.shape[0]
    by_row = lambda columns: pl.BlockSpec((BLOCK, columns), lambda i: (i, 0))
    whole = pl.BlockSpec((length, HEAD), lambda i: (0, 0))
    steps = length // BLOCK
    return pl.pallas_call(
        attend_kernel,
        grid=(steps,),
        in_specs=[by_row(HEAD), whole, whole],
        out_specs=[
            by_row(length),
            by_row(HEAD),
            by_row(1),
            pl.BlockSpec(
                (BLOCK // 64, 1, 32, LANES), lambda i: (i % (steps // 2), i // (steps // 2), 0, 0)
            ),
        ],
        out_shape=[
            jax.ShapeDtypeStruct((length, length), BF),
            jax.ShapeDtypeStruct((length, HEAD), F32),
            jax.ShapeDtypeStruct((length, 1), F32),
            jax.ShapeDtypeStruct((length // 128, 2, 32, LANES), BF),
        ],
        cost_estimate=pl.CostEstimate(
            flops=4 * length * length * HEAD * 4,
            bytes_accessed=2 * length * length,
            transcendentals=length * length,
        ),
        name="attend",
    )(queries, key_rows, value_rows)


def middle_kernel(
    got, tokens, late, gain, grad_out, layer_output, send, acts, grad_middle
):
    width = tokens.shape[1]
    hidden_units = (late.shape[1] - width) // 3
    cut = 2 * hidden_units
    attn, hidden = acts.at[:, :width], acts.at[:, width : 2 * width]
    acts[:, 2 * width : 3 * width] = grad_out[...]
    grad_joint = acts.at[:, 3 * width : 3 * width + cut]
    activation = acts.at[:, 3 * width + cut : 3 * width + cut + hidden_units]
    branch = acts.at[:, 3 * width + cut + hidden_units :]
    for s in range(2):
        for h in range(0, HEADS, 2):
            left, right = got[owner_slot(s, h)], got[owner_slot(s, h + 1)]
            columns = slice(h * HEAD, h * HEAD + LANES)
            attn[64 * s : 64 * s + 32, columns] = side_by_side(left[:, :HEAD], right[:, :HEAD])
            attn[64 * s + 32 : 64 * s + 64, columns] = side_by_side(
                left[:, HEAD:], right[:, HEAD:]
            )
    attn_weight = late[:, cut : cut + width]
    middle = tokens[...].astype(F32) + jnp.dot(
        attn[...], attn_weight, preferred_element_type=F32
    )
    normed, inverse = normalize(middle)
    low = (normed * gain[...]).astype(BF)
    hidden[...] = low
    first = jnp.dot(low, late[:, :hidden_units], preferred_element_type=F32)
    gate = jnp.dot(low, late[:, hidden_units:cut], preferred_element_type=F32)
    cumulative = 0.5 * (1.0 + lax.erf(first * (0.5**0.5)))
    bent = first * cumulative
    active = (bent * gate).astype(BF)
    activation[...] = active
    out_weight = late[:, cut + width :]
    layer_output[...] = (
        middle + lax.dot_general(active, out_weight, BY_COLUMN, preferred_element_type=F32)
    ).astype(BF)
    grad_act = jnp.dot(grad_out[...], out_weight, preferred_element_type=F32)
    density = jnp.exp(-0.5 * first * first) * 0.3989422804014327
    grad_joint[:, :hidden_units] = (grad_act * gate * (cumulative + first * density)).astype(BF)
    grad_joint[:, hidden_units:] = (grad_act * bent).astype(BF)
    grad_hidden = lax.dot_general(
        grad_joint[...], late[:, :cut], BY_COLUMN, preferred_element_type=F32
    )
    total = grad_out[...].astype(F32) + norm_back(grad_hidden * gain[...], normed, inverse)
    grad_middle[...] = total
    branch_low = total.astype(BF)
    branch[...] = branch_low
    grad_cat = lax.dot_general(
        branch_low, attn_weight, BY_COLUMN, preferred_element_type=F32
    ).astype(BF)
    for s in range(2):
        for h in range(HEADS):
            rows = grad_cat[64 * s : 64 * s + 64, h * HEAD : (h + 1) * HEAD]
            block = side_by_side(rows[:32], rows[32:])
            send[owner_slot(s, h)] = block
            if h % SHARE == SHARE - 1:
                send[owner_slot(s, h) + 1] = block


def middle_part(got, tokens, late, gain, grad_out):
    rows, width = tokens.shape
    hidden_units = (late.shape[1] - width) // 3
    shapes = [
        ((rows, width), BF),
        (got.shape, BF),
        ((rows, 4 * width + 3 * hidden_units), BF),
        ((rows, width), F32),
    ]
    return pl.pallas_call(
        middle_kernel,
        out_shape=[jax.ShapeDtypeStruct(shape, kind) for shape, kind in shapes],
        name="middle_part",
    )(got, tokens, late, gain, grad_out)


def weight_grads_kernel(
    place, hidden, attn, grad_out, right, hidden_too, attn_too, grad_out_too, right_too,
    keep_a, give_a, keep_b, give_b, total, *, in_tiles, attn_tiles
):
    tile = pl.program_id(0)
    x, y, core = place[0], place[1], place[2]

    def multiply(left, left_too):
        product = lax.dot_general(
            left[...], right[...], BY_ROW, preferred_element_type=F32
        ) + lax.dot_general(left_too[...], right_too[...], BY_ROW, preferred_element_type=F32)
        total[...] = product.reshape(total.shape)

    def write_b():
        keep_b[...] = total[:, :, y, core].astype(BF)
        give_b[...] = total[:, :, 1 - y, core].astype(BF)

    @pl.when(tile < in_tiles)
    def _():
        multiply(hidden, hidden_too)
        keep_a[...] = total[:, x, :, core].astype(BF)
        give_a[...] = total[:, 1 - x, :, core].astype(BF)

    @pl.when((tile >= in_tiles) & (tile < in_tiles + attn_tiles))
    def _():
        multiply(attn, attn_too)
        write_b()

    @pl.when(tile >= in_tiles + attn_tiles)
    def _():
        multiply(grad_out, grad_out_too)
        write_b()


def weight_grads(place, acts, acts_too, width, hidden_units, rows_here):
    rows = acts.shape[0]
    in_tiles, attn_tiles = 2 * hidden_units // TILE, width // TILE
    out_tiles = hidden_units // TILE
    first = 3 * width // TILE
    last = first + in_tiles + out_tiles
    whole = lambda i: pl.BlockSpec((rows, width), lambda t: (0, i))

    def source(t):
        rest = t - in_tiles - attn_tiles
        late = jnp.where(rest < 0, last + t - in_tiles, first + in_tiles + rest)
        return 0, jnp.where(t < in_tiles, first + t, late)

    sides = [whole(1), whole(0), whole(2), pl.BlockSpec((rows, TILE), source)]
    zs = width // (8 * rows_here)
    block = (zs, 2, rows_here, TILE)
    out_a = pl.BlockSpec(block, lambda t: (0, 0, 0, jnp.minimum(t, in_tiles - 1)))
    out_b = pl.BlockSpec(block, lambda t: (0, 0, 0, jnp.maximum(t - in_tiles, 0)))
    shape = lambda tiles: jax.ShapeDtypeStruct((zs, 2, rows_here, tiles * TILE), BF)
    tiles = in_tiles + attn_tiles + out_tiles
    return pl.pallas_call(
        functools.partial(weight_grads_kernel, in_tiles=in_tiles, attn_tiles=attn_tiles),
        grid=(tiles,),
        in_specs=[smem()] + sides + sides,
        out_specs=[out_a, out_a, out_b, out_b],
        out_shape=[shape(in_tiles)] * 2 + [shape(attn_tiles + out_tiles)] * 2,
        scratch_shapes=[pltpu.VMEM((zs, 2, 2, 2, rows_here, TILE), F32)],
        cost_estimate=pl.CostEstimate(
            flops=4 * rows * width * tiles * TILE,
            bytes_accessed=4 * acts.size + 2 * width * tiles * TILE,
            transcendentals=0,
        ),
        name="weight_grads",
    )(place, *[acts] * 4, *[acts_too] * 4)


def attend_back_kernel(
    got, attn32, total, weights, queries, key_rows, value_rows, cosine, sine, send, grad_both,
    grad_low, grad_query, grad_key, grad_value
):
    step = pl.program_id(0)

    @pl.when(step == 0)
    def _():
        grad_key[...] = jnp.zeros_like(grad_key)
        grad_value[...] = jnp.zeros_like(grad_value)

    pieces = []
    for i in range(BLOCK // 64):
        block = got[i, 0]
        pieces += [block[:, :HEAD], block[:, HEAD:]]
    grad = jnp.concatenate(pieces, axis=0)
    wide = grad.astype(F32)
    dots = jnp.sum(wide * attn32[...], axis=-1, keepdims=True)
    grad_probs = lax.dot_general(
        grad, value_rows[...], BY_COLUMN, preferred_element_type=F32
    )
    inverse = 1.0 / total[...]
    low = weights[...]
    grad_scores = ((low.astype(F32) * inverse) * (grad_probs - dots)).astype(BF)
    grad_query[pl.ds(step * BLOCK, BLOCK), :] = HEAD**-0.5 * jnp.dot(
        grad_scores, key_rows[...], preferred_element_type=F32
    )
    grad_value[...] += lax.dot_general(
        low, (wide * inverse).astype(BF), BY_ROW, preferred_element_type=F32
    )
    grad_key[...] += lax.dot_general(
        grad_scores, queries[...], BY_ROW, preferred_element_type=F32
    )

    @pl.when(step == pl.num_programs(0) - 1)
    def _():
        length = grad_key.shape[0]
        both = side_by_side(grad_query[...], grad_key[...])
        both = (both * cosine[...] - turn(both) * sine[...]).astype(BF)
        grad_both[...] = both
        low = grad_value[...].astype(BF)
        grad_low[...] = low
        for i in range(length // 64):
            core, pair = i // (length // 128), i % (length // 128)
            rows = low[64 * i : 64 * i + 64]
            send[pair, core, :64] = both[64 * i : 64 * i + 64]
            send[pair, core, 64:] = side_by_side(rows[:32], rows[32:])


def attend_back(got, attn32, total, weights, queries, key_rows, value_rows, cosine, sine):
    length = queries.shape[0]
    steps = length // BLOCK
    by_row = lambda columns: pl.BlockSpec((BLOCK, columns), lambda i: (i, 0))
    whole = lambda *shape: pl.BlockSpec(shape, lambda i: (0,) * len(shape))
    send = (length // 128, 2, 96, LANES)
    return pl.pallas_call(
        attend_back_kernel,
        grid=(steps,),
        in_specs=[
            pl.BlockSpec(
                (BLOCK // 64, 1, 32, LANES), lambda i: (i % (steps // 2), i // (steps // 2), 0, 0)
            ),
            by_row(HEAD),
            by_row(1),
            by_row(length),
            by_row(HEAD),
            whole(length, HEAD),
            whole(length, HEAD),
            whole(length, LANES),
            whole(length, LANES),
        ],
        out_specs=[whole(*send), whole(length, LANES), whole(length, HEAD)],
        out_shape=[
            jax.ShapeDtypeStruct(send, BF),
            jax.ShapeDtypeStruct((length, LANES), BF),
            jax.ShapeDtypeStruct((length, HEAD), BF),
        ],
        scratch_shapes=[pltpu.VMEM((length, HEAD), F32)] * 3,
        cost_estimate=pl.CostEstimate(
            flops=14 * length * length * HEAD * 4,
            bytes_accessed=2 * length * length,
            transcendentals=0,
        ),
        name="attend_back",
    )(got, attn32, total, weights, queries, key_rows, value_rows, cosine, sine)


def head_grads_kernel(hidden, both, low, result, total):
    step = pl.program_id(0)

    @pl.when(step == 0)
    def _():
        total[...] = jnp.zeros_like(total)

    total[:, :LANES] += lax.dot_general(
        hidden[...], both[...], BY_ROW, preferred_element_type=F32
    )
    total[:, LANES:] += lax.dot_general(
        hidden[...], low[...], BY_ROW, preferred_element_type=F32
    )

    @pl.when(step == pl.num_programs(0) - 1)
    def _():
        result[...] = total[...].astype(BF)


def head_grads(hidden, both, low):
    length, width = hidden.shape
    by_row = lambda columns: pl.BlockSpec((2 * BLOCK, columns), lambda i: (i, 0))
    return pl.pallas_call(
        head_grads_kernel,
        grid=(length // (2 * BLOCK),),
        in_specs=[by_row(width), by_row(LANES), by_row(HEAD)],
        out_specs=pl.BlockSpec((width, 3 * HEAD), lambda i: (0, 0)),
        out_shape=jax.ShapeDtypeStruct((width, 3 * HEAD), BF),
        scratch_shapes=[pltpu.VMEM((width, 3 * HEAD), F32)],
        cost_estimate=pl.CostEstimate(
            flops=6 * HEAD * length * width,
            bytes_accessed=2 * length * (width + 3 * HEAD),
            transcendentals=0,
        ),
        name="head_grads",
    )(hidden, both, low)


def last_kernel(got, weight, tokens, gain, grad_middle, result, grads):
    width = tokens.shape[1]
    for s in range(2):
        for h in range(0, HEADS, 2):
            left, right = got[owner_slot(s, h)], got[owner_slot(s, h + 1)]
            top, end = slice(64 * s, 64 * s + 64), slice(64 * s + 64, 64 * s + 128)
            place = lambda j: slice(j * width + h * HEAD, j * width + h * HEAD + LANES)
            grads[top, place(0)] = side_by_side(left[:64, :HEAD], right[:64, :HEAD])
            grads[top, place(1)] = side_by_side(left[:64, HEAD:], right[:64, HEAD:])
            grads[64 * s : 64 * s + 32, place(2)] = side_by_side(
                left[64:, :HEAD], right[64:, :HEAD]
            )
            grads[64 * s + 32 : 64 * s + 64, place(2)] = side_by_side(
                left[64:, HEAD:], right[64:, HEAD:]
            )
    grad_hidden = lax.dot_general(
        grads[...], weight[...], BY_COLUMN, preferred_element_type=F32
    )
    normed, inverse = normalize(tokens[...].astype(F32))
    result[...] = (
        grad_middle[...] + norm_back(grad_hidden * gain[...], normed, inverse)
    ).astype(BF)


def last_part(got, weight, tokens, gain, grad_middle):
    return pl.pallas_call(
        last_kernel,
        out_shape=jax.ShapeDtypeStruct(tokens.shape, BF),
        scratch_shapes=[pltpu.VMEM((tokens.shape[0], weight.shape[1]), BF)],
        name="last_part",
    )(got, weight, tokens, gain, grad_middle)


def collect_kernel(got, weight, gain, result, gain_grad):
    width = result.shape[1] // 3
    for h in range(0, HEADS, 2):
        left = got[owner_slot(0, h)].astype(F32) + got[owner_slot(1, h)].astype(F32)
        right = got[owner_slot(0, h + 1)].astype(F32) + got[owner_slot(1, h + 1)].astype(F32)
        for j in range(3):
            columns = slice(j * HEAD, (j + 1) * HEAD)
            place = slice(j * width + h * HEAD, j * width + h * HEAD + LANES)
            result[:, place] = side_by_side(left[:, columns], right[:, columns])
    product = result[...] * weight[...].astype(F32)
    gain_grad[...] = jnp.sum(product, axis=1, keepdims=True) / gain[...]


def collect(got, weight, gain):
    rows, columns = weight.shape
    return pl.pallas_call(
        collect_kernel,
        out_shape=[
            jax.ShapeDtypeStruct((rows, columns), F32),
            jax.ShapeDtypeStruct((rows, 1), F32),
        ],
        name="collect",
    )(got, weight, gain)


def owner_body(
    tokens, attn_gain, qkv_weight, attn_out_weight, mlp_gain, in_weight, out_weight, cotangent
):
    sequences, per_device, model_width = tokens.shape
    hidden_units = out_weight.shape[0]
    rows_here = qkv_weight.shape[0]
    rows = sequences * per_device
    length = per_device * 32
    core = my_bit("ulysses", 1).astype(jnp.int32).reshape(1)
    place = jnp.stack([my_bit("blk", 1), my_bit("ulysses", 2), my_bit("ulysses", 1)])
    place = place.astype(jnp.int32)
    late = jnp.concatenate([in_weight, attn_out_weight, jnp.transpose(out_weight)], axis=1)
    late_full = lax.all_gather(late, AXES, axis=0, tiled=True)
    by_head = qkv_weight.reshape(rows_here, 3, HEADS, HEAD).transpose(2, 0, 1, 3)
    by_head = by_head.reshape(HEADS, rows_here, 3 * HEAD)
    gains = jnp.stack([attn_gain, mlp_gain], axis=1)
    gains = jnp.broadcast_to(jnp.pad(gains, ((0, 0), (0, HEAD - 2))), (HEADS, rows_here, HEAD))
    packed = jnp.concatenate([by_head, gains], axis=2)
    packed = packed.reshape(HEADS // SHARE, SHARE, rows_here, 4 * HEAD)
    packed = jnp.concatenate([packed, packed[:, -1:]], axis=1)
    packed = jnp.broadcast_to(packed[None], (2,) + packed.shape)
    mixed = exchange(packed.reshape(32, rows_here, 4 * HEAD))
    mine, other, (mixed, cosine, sine) = gather_sequence(tokens, (mixed, *turned_tables(length)))
    weight_here = mixed.reshape(model_width, 4 * HEAD)
    gain_one = weight_here[:, 3 * HEAD].reshape(1, model_width).astype(F32)
    gain_two = weight_here[:, 3 * HEAD + 1].reshape(1, model_width).astype(F32)
    hidden_one, queries, key_rows, value_rows = project(
        core,
        mine,
        other,
        gain_one,
        weight_here,
        cosine.reshape(2, length // 2, LANES),
        sine.reshape(2, length // 2, LANES),
    )
    queries, key_rows, value_rows = (
        value.reshape(length, HEAD) for value in (queries, key_rows, value_rows)
    )
    weights_low, attn32, row_total, send = attend(queries, key_rows, value_rows)
    got = exchange(send.reshape(32, 32, LANES))
    flat_tokens = tokens.reshape(rows, model_width)
    grad_out = cotangent.reshape(rows, model_width)
    layer_output, send, acts, grad_middle = middle_part(
        got, flat_tokens, late_full, gain_two, grad_out
    )
    got = exchange(send)
    acts_too = swap(acts, "ulysses", 1)
    parts = weight_grads(place, acts, acts_too, model_width, hidden_units, rows_here)
    got, parts = lax.optimization_barrier((got, parts))
    keep_a, give_a, keep_b, give_b = (
        part.reshape(2, 2, *part.shape[1:]) for part in parts
    )
    came_a, came_b = swap(give_a, "blk", 1), swap(give_b, "ulysses", 2)
    send, grad_both, grad_low = attend_back(
        got.reshape(length // 128, 2, 32, LANES),
        attn32,
        row_total,
        weights_low,
        queries,
        key_rows,
        value_rows,
        cosine,
        sine,
    )
    qkv_full = lax.all_gather(qkv_weight, AXES, axis=0, tiled=True)
    send, came_a, came_b = lax.optimization_barrier((send, came_a, came_b))
    got = exchange(send.reshape(32, 96, LANES))
    keep_a, give_a = halve(keep_a, came_a, "ulysses", 2, 2)
    keep_b, give_b = halve(keep_b, came_b, "blk", 1, 2)
    came_a, came_b = swap(give_a, "ulysses", 2), swap(give_b, "blk", 1)
    head_grad = head_grads(hidden_one.reshape(length, model_width), grad_both, grad_low)
    got, head_grad, came_a, came_b, qkv_full = lax.optimization_barrier(
        (got, head_grad, came_a, came_b, qkv_full)
    )
    got_grads = exchange(head_grad.reshape(32, rows_here, 3 * HEAD))
    total = [
        (keep.astype(F32) + came.astype(F32)).astype(BF).reshape(4, rows_here, -1)
        for keep, came in ((keep_a, came_a), (keep_b, came_b))
    ]
    z = lax.axis_index("blk") // 2

    def rows_of(owner):
        return jnp.concatenate(
            [lax.dynamic_index_in_dim(part, owner, 0, keepdims=False) for part in total], axis=1
        )

    shards = rows_of(z).astype(F32)
    for step in (2, 3, 1):
        shards = shards + swap(rows_of(z ^ step), "blk", 2 * step).astype(F32)
    input_grad = last_part(got, qkv_full, flat_tokens, gain_one, grad_middle)
    input_grad = input_grad.reshape(sequences, per_device, model_width)
    shard_qkv, shard_one = collect(
        got_grads, qkv_weight, attn_gain.astype(F32).reshape(rows_here, 1)
    )
    shard_in = shards[:, : 2 * hidden_units]
    shard_attn = shards[:, 2 * hidden_units : 2 * hidden_units + model_width]
    shard_out = jnp.transpose(shards[:, 2 * hidden_units + model_width :])
    shard_two = jnp.sum(shard_in * in_weight.astype(F32), axis=1) / mlp_gain.astype(F32)
    return (
        layer_output.reshape(sequences, per_device, model_width),
        input_grad,
        shard_one.reshape(rows_here),
        shard_qkv,
        shard_attn,
        shard_two,
        shard_in,
        shard_out,
    )


def solution(mesh):
    placed = (
        P(None, ("blk", "ulysses"), None),
        P(("blk", "ulysses")),
        P(("blk", "ulysses"), None),
        P(("blk", "ulysses"), None),
        P(("blk", "ulysses")),
        P(("blk", "ulysses"), None),
        P(None, ("blk", "ulysses")),
        P(None, ("blk", "ulysses"), None),
    )
    sizes = (mesh.shape["blk"], mesh.shape["ulysses"])
    return jax.shard_map(
        owner_body if sizes == (8, 4) else ring_body,
        mesh=mesh,
        in_specs=placed,
        out_specs=(
            P(None, ("blk", "ulysses"), None),
            P(None, ("blk", "ulysses"), None),
            P(("blk", "ulysses")),
            P(("blk", "ulysses"), None),
            P(("blk", "ulysses"), None),
            P(("blk", "ulysses")),
            P(("blk", "ulysses"), None),
            P(None, ("blk", "ulysses")),
        ),
        check_vma=False,
    )
```

```python
import functools

import jax
import jax.numpy as jnp
from jax import lax
from jax.experimental import pallas as pl
from jax.experimental.pallas import tpu as pltpu
from jax.sharding import PartitionSpec as P

HEAD = 64


EPSILON = 1e-05
THETA = 160000.0


def from_behind(value, axis, by):
    size = lax.axis_size(axis)
    return lax.ppermute(value, axis, [(i, (i + by) % size) for i in range(size)])


def normalize(values):
    center = values - jnp.mean(values, axis=-1, keepdims=True)
    inverse = lax.rsqrt(jnp.mean(center * center, axis=-1, keepdims=True) + EPSILON)
    return (center * inverse, inverse)


def norm_back(grad_normed, normed, inverse):
    first_mean = jnp.mean(grad_normed, axis=-1, keepdims=True)
    second_mean = jnp.mean(grad_normed * normed, axis=-1, keepdims=True)
    return inverse * (grad_normed - first_mean - normed * second_mean)


def rotation(first_row, row_count, head_width):
    half_width = head_width // 2
    frequency = THETA ** (-(jnp.arange(half_width, dtype=jnp.float32) * 2.0) / head_width)
    positions = (first_row + jnp.arange(row_count, dtype=jnp.int32)).astype(jnp.float32)
    angles = positions[:, None] * frequency[None, :]
    cosine_table = jnp.concatenate([jnp.cos(angles), jnp.cos(angles)], axis=-1)
    sine_table = jnp.concatenate([jnp.sin(angles), jnp.sin(angles)], axis=-1)
    return (cosine_table, sine_table)


def rotate(values, cosine_table, sine_table, direction):
    half_width = values.shape[-1] // 2
    turned = jnp.concatenate([-values[..., half_width:], values[..., :half_width]], axis=-1)
    return values * cosine_table[:, None, :] + direction * turned * sine_table[:, None, :]


def block_grads(
    query_part,
    key_part,
    value_part,
    grad_part,
    log_part,
    dots_part,
    top_part,
    total_part,
    score_scale,
):
    scores = (
        jnp.einsum("sqhd,skhd->shqk", query_part, key_part, preferred_element_type=jnp.float32)
        * score_scale
    )
    probs = jnp.exp(scores - log_part[..., None])
    grad_probs = jnp.einsum(
        "sqhd,skhd->shqk", grad_part, value_part, preferred_element_type=jnp.float32
    )
    grad_scores = (probs * (grad_probs - dots_part[..., None])).astype(jnp.bfloat16)
    weights_low = jnp.exp(scores - top_part[..., None]).astype(jnp.bfloat16)
    grad_scaled = grad_part.astype(jnp.float32) / jnp.transpose(total_part, (0, 2, 1))[..., None]
    value_term = jnp.einsum("shqk,sqhd->skhd", weights_low.astype(jnp.float32), grad_scaled)
    return (value_term, grad_scores)


def ring_body(
    tokens, attn_gain, qkv_weight, attn_out_weight, mlp_gain, in_weight, out_weight, cotangent
):
    sequences, per_device, model_width = tokens.shape
    groups = lax.axis_size("ulysses")
    cycle_size = lax.axis_size("blk")
    group_width = model_width // groups
    heads_here = group_width // HEAD
    group_rows = per_device * groups
    score_scale = HEAD ** (-0.5)
    qkv_full, attn_full, in_full, out_full, gain_one, gain_two = (
        lax.all_gather(qkv_weight, ("blk", "ulysses"), axis=0, tiled=True),
        lax.all_gather(attn_out_weight, ("blk", "ulysses"), axis=0, tiled=True),
        lax.all_gather(in_weight, ("blk", "ulysses"), axis=0, tiled=True),
        lax.all_gather(out_weight, ("blk", "ulysses"), axis=1, tiled=True),
        lax.all_gather(attn_gain, ("blk", "ulysses"), axis=0, tiled=True),
        lax.all_gather(mlp_gain, ("blk", "ulysses"), axis=0, tiled=True),
    )
    gain_one = gain_one.astype(jnp.float32)
    gain_two = gain_two.astype(jnp.float32)
    hidden_units = out_full.shape[0]
    inputs_wide = tokens.astype(jnp.float32).reshape(sequences * per_device, model_width)
    normed_one, inverse_one = normalize(inputs_wide)
    hidden_one = (normed_one * gain_one).astype(jnp.bfloat16)
    qkv = jnp.dot(hidden_one, qkv_full, preferred_element_type=jnp.float32).astype(jnp.bfloat16)
    packed = qkv.reshape(sequences, per_device, 3, groups, group_width)
    headwise = lax.all_to_all(packed, "ulysses", split_axis=3, concat_axis=1, tiled=True)
    headwise = headwise.reshape(sequences, group_rows, 3, heads_here, HEAD)
    cosine_table, sine_table = rotation(lax.axis_index("blk") * group_rows, group_rows, HEAD)
    queries = rotate(headwise[:, :, 0].astype(jnp.float32), cosine_table, sine_table, 1.0).astype(
        jnp.bfloat16
    )
    key_rows = rotate(headwise[:, :, 1].astype(jnp.float32), cosine_table, sine_table, 1.0).astype(
        jnp.bfloat16
    )
    value_rows = headwise[:, :, 2]
    start_top = jnp.full((sequences, heads_here, group_rows), -1e30, jnp.float32)
    zeros_rows = jnp.zeros((sequences, group_rows, heads_here, HEAD), jnp.float32)
    key_piece = lax.all_gather(key_rows, "blk", axis=1, tiled=True)
    value_piece = lax.all_gather(value_rows, "blk", axis=1, tiled=True)
    scores = (
        jnp.einsum("sqhd,skhd->shqk", queries, key_piece, preferred_element_type=jnp.float32)
        * score_scale
    )
    new_top = jnp.maximum(start_top, jnp.max(scores, axis=-1))
    weights = jnp.exp(scores - new_top[..., None])
    attend_row_total = jnp.sum(weights, axis=-1)
    update = jnp.einsum(
        "shqk,skhd->sqhd",
        weights.astype(jnp.bfloat16),
        value_piece,
        preferred_element_type=jnp.float32,
    )
    weighted = update
    row_top, row_total, weighted = (new_top, attend_row_total, weighted)
    log_total = row_top + jnp.log(row_total)
    attn_wide = weighted / jnp.transpose(row_total, (0, 2, 1))[..., None]
    attn_low = attn_wide.astype(jnp.bfloat16).reshape(sequences, group_rows, 1, group_width)
    token_rows = lax.all_to_all(attn_low, "ulysses", split_axis=1, concat_axis=2, tiled=True)
    attn_cat = token_rows.reshape(sequences * per_device, model_width)
    middle = inputs_wide + jnp.dot(attn_cat, attn_full, preferred_element_type=jnp.float32)
    normed_two, inverse_two = normalize(middle)
    hidden_two = (normed_two * gain_two).astype(jnp.bfloat16)
    joint = jnp.dot(hidden_two, in_full, preferred_element_type=jnp.float32)

    def geglu(joint_pre):
        return (
            jax.nn.gelu(joint_pre[:, :hidden_units], approximate=False)
            * joint_pre[:, hidden_units:]
        )

    act_wide, geglu_back = jax.vjp(geglu, joint)
    activation = act_wide.astype(jnp.bfloat16)
    result = middle + jnp.dot(activation, out_full, preferred_element_type=jnp.float32)
    layer_output = result.astype(jnp.bfloat16).reshape(sequences, per_device, model_width)
    grad_out = cotangent.reshape(sequences * per_device, model_width)
    grad_wout = jnp.einsum("tf,td->fd", activation, grad_out, preferred_element_type=jnp.float32)
    grad_act = jnp.einsum("td,fd->tf", grad_out, out_full, preferred_element_type=jnp.float32)
    grad_joint = geglu_back(grad_act)[0].astype(jnp.bfloat16)
    grad_win = jnp.einsum("tc,tf->cf", hidden_two, grad_joint, preferred_element_type=jnp.float32)
    grad_hidden_two = jnp.einsum(
        "tf,cf->tc", grad_joint, in_full, preferred_element_type=jnp.float32
    )
    grad_gain_two = jnp.sum(grad_hidden_two * normed_two, axis=0)
    grad_middle = grad_out.astype(jnp.float32) + norm_back(
        grad_hidden_two * gain_two, normed_two, inverse_two
    )
    grad_branch = grad_middle.astype(jnp.bfloat16)
    grad_wattn = jnp.einsum("tc,td->cd", attn_cat, grad_branch, preferred_element_type=jnp.float32)
    grad_cat = jnp.einsum(
        "td,cd->tc", grad_branch, attn_full, preferred_element_type=jnp.float32
    ).astype(jnp.bfloat16)
    grad_heads_in = lax.all_to_all(
        grad_cat.reshape(sequences, per_device, groups, group_width),
        "ulysses",
        split_axis=2,
        concat_axis=1,
        tiled=True,
    )
    grad_attn = grad_heads_in.reshape(sequences, group_rows, heads_here, HEAD)
    row_dots = jnp.transpose(jnp.sum(grad_attn.astype(jnp.float32) * attn_wide, axis=-1), (0, 2, 1))

    def cycle_step(step_index, state_now):
        key_now, value_now, grad_key, grad_value, grad_query = state_now
        value_term, grad_scores = block_grads(
            queries,
            key_now,
            value_now,
            grad_attn,
            log_total,
            row_dots,
            row_top,
            row_total,
            score_scale,
        )
        grad_value = grad_value + value_term
        grad_key = grad_key + score_scale * jnp.einsum(
            "shqk,sqhd->skhd", grad_scores, queries, preferred_element_type=jnp.float32
        )
        grad_query = grad_query + score_scale * jnp.einsum(
            "shqk,skhd->sqhd", grad_scores, key_now, preferred_element_type=jnp.float32
        )
        key_now, value_now = from_behind((key_now, value_now), "blk", 1)
        grad_key, grad_value = (
            from_behind(grad_key.astype(jnp.bfloat16), "blk", 1).astype(grad_key.dtype),
            from_behind(grad_value.astype(jnp.bfloat16), "blk", 1).astype(grad_value.dtype),
        )
        return (key_now, value_now, grad_key, grad_value, grad_query)

    final_state = lax.fori_loop(
        0, cycle_size, cycle_step, (key_rows, value_rows, zeros_rows, zeros_rows, zeros_rows)
    )
    grad_key, grad_value, grad_query = (final_state[2], final_state[3], final_state[4])
    grad_query = rotate(grad_query, cosine_table, sine_table, -1.0)
    grad_key = rotate(grad_key, cosine_table, sine_table, -1.0)
    grad_stack = jnp.stack([grad_query, grad_key, grad_value], axis=2).astype(jnp.bfloat16)
    grad_stack = grad_stack.reshape(sequences, group_rows, 3, 1, group_width)
    grad_tokens = lax.all_to_all(grad_stack, "ulysses", split_axis=1, concat_axis=3, tiled=True)
    grad_qkv = grad_tokens.reshape(sequences * per_device, 3 * model_width)
    grad_wqkv = jnp.einsum("tc,tf->cf", hidden_one, grad_qkv, preferred_element_type=jnp.float32)
    grad_hidden_one = jnp.einsum(
        "tf,cf->tc", grad_qkv, qkv_full, preferred_element_type=jnp.float32
    )
    grad_gain_one = jnp.sum(grad_hidden_one * normed_one, axis=0)
    grad_input = grad_middle + norm_back(grad_hidden_one * gain_one, normed_one, inverse_one)
    input_grad = grad_input.astype(jnp.bfloat16).reshape(sequences, per_device, model_width)
    shard_qkv, shard_attn, shard_in, shard_out, shard_one, shard_two = (
        lax.psum_scatter(grad_wqkv, ("blk", "ulysses"), scatter_dimension=0, tiled=True),
        lax.psum_scatter(grad_wattn, ("blk", "ulysses"), scatter_dimension=0, tiled=True),
        lax.psum_scatter(grad_win, ("blk", "ulysses"), scatter_dimension=0, tiled=True),
        lax.psum_scatter(grad_wout, ("blk", "ulysses"), scatter_dimension=1, tiled=True),
        lax.psum_scatter(grad_gain_one, ("blk", "ulysses"), scatter_dimension=0, tiled=True),
        lax.psum_scatter(grad_gain_two, ("blk", "ulysses"), scatter_dimension=0, tiled=True),
    )
    return (
        layer_output,
        input_grad,
        shard_one,
        shard_qkv,
        shard_attn,
        shard_two,
        shard_in,
        shard_out,
    )


AXES = ("blk", "ulysses")
BF = jnp.bfloat16
F32 = jnp.float32
HEADS = 12
SHARE = 3
BLOCK = 256
LANES = 128
TILE = 384
SENT = 136
BY_COLUMN = (((1,), (1,)), ((), ()))
BY_ROW = (((0,), (0,)), ((), ()))


def pick(value, index):
    return lax.dynamic_index_in_dim(value, index, 0, keepdims=False)


def swap(value, axis, bit):
    size = lax.axis_size(axis)
    return lax.ppermute(value, axis, [(i, i ^ bit) for i in range(size)])


def my_bit(axis, bit):
    return (lax.axis_index(axis) // bit) % 2


def join(mine, other, side, axis):
    first = jnp.stack([mine, other], axis=axis)
    second = jnp.stack([other, mine], axis=axis)
    return jnp.where(side == 0, first, second)


def gather_sequence(tokens, also):
    sequences, rows, width = tokens.shape
    z2, z1, x = my_bit("blk", 4), my_bit("blk", 2), my_bit("blk", 1)
    y = my_bit("ulysses", 2)
    keep = lax.dynamic_index_in_dim(tokens, z2, 0, keepdims=False)
    give = lax.dynamic_index_in_dim(tokens, 1 - z2, 0, keepdims=False)
    near = join(keep, swap(keep, "blk", 2), z1, 0)
    far = join(swap(give, "blk", 4), swap(give, "blk", 6), z1, 0)
    wide = join(near, far, z2, 0).reshape(2, 2, 2, rows // 2, width)
    part_a, part_b = wide[:, :, 0], wide[:, :, 1]
    from_a, from_b = swap(part_a, "blk", 1), swap(part_b, "ulysses", 2)
    part_a = join(part_a, from_a, x, 2)
    part_b = join(part_b, from_b, y, 2)
    from_a, from_b = swap(part_a, "ulysses", 2), swap(part_b, "blk", 1)
    part_a = join(part_a, from_a, y, 3)
    part_b = join(part_b, from_b, x, 2)
    wide = jnp.stack([part_a, part_b], axis=4).reshape(16 * rows, width)
    wide, also = lax.optimization_barrier((wide, also))
    return wide, swap(wide, "ulysses", 1), also


def halve(keep, got, axis, bit, dim):
    total = (keep.astype(F32) + got.astype(F32)).astype(BF)
    side = my_bit(axis, bit)
    keep = lax.dynamic_index_in_dim(total, side, dim, keepdims=False)
    give = lax.dynamic_index_in_dim(total, 1 - side, dim, keepdims=False)
    return keep, give


def turned_tables(rows):
    lane = jnp.arange(LANES, dtype=jnp.int32) % (HEAD // 2)
    frequency = THETA ** (-(lane.astype(F32) * 2.0) / HEAD)
    row = jnp.arange(rows, dtype=jnp.int32)
    half = rows // 2
    position = row % half // 64 * 128 + row // half * 64 + row % 64
    angles = position.astype(F32)[:, None] * frequency[None, :]
    return jnp.cos(angles), jnp.sin(angles)


def exchange(value):
    return lax.all_to_all(value, AXES, split_axis=0, concat_axis=0, tiled=True)


def owner_slot(sequence, head):
    return sequence * 16 + head // SHARE * (SHARE + 1) + head % SHARE


def turn(values):
    lane = lax.broadcasted_iota(jnp.int32, values.shape, 1) % HEAD
    return jnp.where(
        lane < HEAD // 2,
        -pltpu.roll(values, LANES - HEAD // 2, 1),
        pltpu.roll(values, HEAD // 2, 1),
    )


def side_by_side(left, right):
    return jnp.concatenate([left, right], axis=1)


def smem():
    return pl.BlockSpec(memory_space=pltpu.SMEM)


def project_kernel(
    core, mine, other, gain, weight, cosine, sine, hidden, queries, key_rows, value_rows
):
    def one(tokens, slot):
        normed, inverse = normalize(tokens[...].astype(F32))
        low = (normed * gain[...]).astype(BF)
        hidden[slot] = low
        qkv = jnp.dot(low, weight[:, : 3 * HEAD], preferred_element_type=F32).astype(BF)
        both = qkv[:, :LANES].astype(F32)
        both = (both * cosine[slot] + turn(both) * sine[slot]).astype(BF)
        queries[slot] = both[:, :HEAD] * BF(HEAD**-0.5)
        key_rows[slot] = both[:, HEAD:]
        value_rows[slot] = qkv[:, LANES:]

    one(mine, core[0])
    one(other, 1 - core[0])


def project(core, mine, other, gain, weight, cosine, sine):
    length, width = mine.shape
    by_row = pl.BlockSpec((BLOCK, width), lambda i: (i, 0))
    by_pair = lambda columns: pl.BlockSpec((2, BLOCK, columns), lambda i: (0, i, 0))
    whole = lambda shape: pl.BlockSpec(shape, lambda i: (0, 0))
    return pl.pallas_call(
        project_kernel,
        grid=(length // BLOCK,),
        in_specs=[
            smem(),
            by_row,
            by_row,
            whole((1, width)),
            whole(weight.shape),
            by_pair(LANES),
            by_pair(LANES),
        ],
        out_specs=[by_pair(width), by_pair(HEAD), by_pair(HEAD), by_pair(HEAD)],
        out_shape=[jax.ShapeDtypeStruct((2, length, width), BF)]
        + [jax.ShapeDtypeStruct((2, length, HEAD), BF)] * 3,
        name="project",
    )(core, mine, other, gain, weight, cosine, sine)


def attend_kernel(queries, key_rows, value_rows, weights, attn32, total, send):
    scores = lax.dot_general(
        queries[...], key_rows[...], BY_COLUMN, preferred_element_type=F32
    )
    top = jnp.max(scores, axis=-1, keepdims=True)
    expo = jnp.exp(scores - top)
    row_total = jnp.sum(expo, axis=-1, keepdims=True)
    low = expo.astype(BF)
    weights[...] = low
    mixed = jnp.dot(low, value_rows[...], preferred_element_type=F32) / row_total
    attn32[...] = mixed
    total[...] = row_total
    mixed = mixed.astype(BF)
    for i in range(BLOCK // 64):
        rows = mixed[64 * i : 64 * i + 64]
        send[i, 0] = side_by_side(rows[:32], rows[32:])


def attend(queries, key_rows, value_rows):
    length = queries.shape[0]
    by_row = lambda columns: pl.BlockSpec((BLOCK, columns), lambda i: (i, 0))
    whole = pl.BlockSpec((length, HEAD), lambda i: (0, 0))
    steps = length // BLOCK
    return pl.pallas_call(
        attend_kernel,
        grid=(steps,),
        in_specs=[by_row(HEAD), whole, whole],
        out_specs=[
            by_row(length),
            by_row(HEAD),
            by_row(1),
            pl.BlockSpec(
                (BLOCK // 64, 1, 32, LANES), lambda i: (i % (steps // 2), i // (steps // 2), 0, 0)
            ),
        ],
        out_shape=[
            jax.ShapeDtypeStruct((length, length), BF),
            jax.ShapeDtypeStruct((length, HEAD), F32),
            jax.ShapeDtypeStruct((length, 1), F32),
            jax.ShapeDtypeStruct((length // 128, 2, 32, LANES), BF),
        ],
        cost_estimate=pl.CostEstimate(
            flops=4 * length * length * HEAD * 4,
            bytes_accessed=2 * length * length,
            transcendentals=length * length,
        ),
        name="attend",
    )(queries, key_rows, value_rows)


def middle_kernel(
    got, tokens, late, gain, grad_out, layer_output, send, acts, grad_middle
):
    width = tokens.shape[1]
    hidden_units = (late.shape[1] - width) // 3
    cut = 2 * hidden_units
    attn, hidden = acts.at[:, :width], acts.at[:, width : 2 * width]
    acts[:, 2 * width : 3 * width] = grad_out[...]
    grad_joint = acts.at[:, 3 * width : 3 * width + cut]
    activation = acts.at[:, 3 * width + cut : 3 * width + cut + hidden_units]
    branch = acts.at[:, 3 * width + cut + hidden_units :]
    for s in range(2):
        for h in range(0, HEADS, 2):
            left, right = got[owner_slot(s, h)], got[owner_slot(s, h + 1)]
            columns = slice(h * HEAD, h * HEAD + LANES)
            attn[64 * s : 64 * s + 32, columns] = side_by_side(left[:, :HEAD], right[:, :HEAD])
            attn[64 * s + 32 : 64 * s + 64, columns] = side_by_side(
                left[:, HEAD:], right[:, HEAD:]
            )
    attn_weight = late[:, cut : cut + width]
    middle = tokens[...].astype(F32) + jnp.dot(
        attn[...], attn_weight, preferred_element_type=F32
    )
    normed, inverse = normalize(middle)
    low = (normed * gain[...]).astype(BF)
    hidden[...] = low
    first = jnp.dot(low, late[:, :hidden_units], preferred_element_type=F32)
    gate = jnp.dot(low, late[:, hidden_units:cut], preferred_element_type=F32)
    cumulative = 0.5 * (1.0 + lax.erf(first * (0.5**0.5)))
    bent = first * cumulative
    active = (bent * gate).astype(BF)
    activation[...] = active
    out_weight = late[:, cut + width :]
    layer_output[...] = (
        middle + lax.dot_general(active, out_weight, BY_COLUMN, preferred_element_type=F32)
    ).astype(BF)
    grad_act = jnp.dot(grad_out[...], out_weight, preferred_element_type=F32)
    density = jnp.exp(-0.5 * first * first) * 0.3989422804014327
    grad_joint[:, :hidden_units] = (grad_act * gate * (cumulative + first * density)).astype(BF)
    grad_joint[:, hidden_units:] = (grad_act * bent).astype(BF)
    grad_hidden = lax.dot_general(
        grad_joint[...], late[:, :cut], BY_COLUMN, preferred_element_type=F32
    )
    total = grad_out[...].astype(F32) + norm_back(grad_hidden * gain[...], normed, inverse)
    grad_middle[...] = total
    branch_low = total.astype(BF)
    branch[...] = branch_low
    grad_cat = lax.dot_general(
        branch_low, attn_weight, BY_COLUMN, preferred_element_type=F32
    ).astype(BF)
    for s in range(2):
        for h in range(HEADS):
            rows = grad_cat[64 * s : 64 * s + 64, h * HEAD : (h + 1) * HEAD]
            block = side_by_side(rows[:32], rows[32:])
            send[owner_slot(s, h)] = block
            if h % SHARE == SHARE - 1:
                send[owner_slot(s, h) + 1] = block


def middle_part(got, tokens, late, gain, grad_out):
    rows, width = tokens.shape
    hidden_units = (late.shape[1] - width) // 3
    shapes = [
        ((rows, width), BF),
        (got.shape, BF),
        ((rows, 4 * width + 3 * hidden_units), BF),
        ((rows, width), F32),
    ]
    return pl.pallas_call(
        middle_kernel,
        out_shape=[jax.ShapeDtypeStruct(shape, kind) for shape, kind in shapes],
        name="middle_part",
    )(got, tokens, late, gain, grad_out)


def weight_grads_kernel(
    place, acts, acts_too, keep_a, give_a, keep_b, give_b, own_c, give_c, total, turned, *,
    width, hidden_units
):
    x, y, core, z = place[0], place[1], place[2], place[3]
    rows = acts.shape[0]
    joint = 3 * width
    active = joint + 2 * hidden_units
    branch = active + hidden_units

    def turn_rows(i):
        columns = slice(i * width, (i + 1) * width)
        turned[:, :rows] = jnp.transpose(acts[:, columns])
        turned[:, rows:] = jnp.transpose(acts_too[:, columns])

    def multiply(start):
        right = jnp.concatenate(
            [acts[:, start : start + TILE], acts_too[:, start : start + TILE]], axis=0
        )
        product = jnp.dot(turned[...], right, preferred_element_type=F32)
        total[...] = product.reshape(total.shape)

    def write_b(i):
        columns = slice(i * TILE, (i + 1) * TILE)
        keep_b[..., columns] = total[:, :, y, core].astype(BF)
        give_b[..., columns] = total[:, :, 1 - y, core].astype(BF)

    turn_rows(0)
    for i in range(width // TILE):
        columns = slice(i * TILE, (i + 1) * TILE)
        multiply(branch + i * TILE)
        own_c[..., columns] = total[z, :, :, core].astype(BF)
        for k in (1, 2, 3):
            other = z + k - 2 * ((z % 2) * (k % 2) + (z // 2) * (k // 2) * 2)
            give_c[k - 1, ..., columns] = total[other, :, :, core].astype(BF)
    turn_rows(1)
    tiles_a = keep_a.shape[-1] // TILE
    for i in range(2 * hidden_units // TILE):
        columns = slice(i * TILE, (i + 1) * TILE)
        multiply(joint + i * TILE)
        if i < tiles_a:
            keep_a[..., columns] = total[:, x, :, core].astype(BF)
            give_a[..., columns] = total[:, 1 - x, :, core].astype(BF)
        else:
            write_b(i - tiles_a)
    turn_rows(2)
    for i in range(hidden_units // TILE):
        multiply(active + i * TILE)
        write_b(2 * hidden_units // TILE - tiles_a + i)


def weight_grads(place, acts, acts_too, width, hidden_units, rows_here):
    rows = acts.shape[0]
    zs = width // (8 * rows_here)
    columns = 3 * hidden_units + width
    columns_a = 5 * (2 * hidden_units // TILE) // 6 * TILE
    columns_b = 3 * hidden_units - columns_a
    full = lambda *dims: jax.ShapeDtypeStruct(dims, BF)
    return pl.pallas_call(
        functools.partial(weight_grads_kernel, width=width, hidden_units=hidden_units),
        in_specs=[smem()] + [pl.BlockSpec(memory_space=pltpu.VMEM)] * 2,
        out_shape=[full(zs, 2, rows_here, columns_a)] * 2
        + [full(zs, 2, rows_here, columns_b)] * 2
        + [full(2, 2, rows_here, width), full(3, 2, 2, rows_here, width)],
        scratch_shapes=[
            pltpu.VMEM((zs, 2, 2, 2, rows_here, TILE), F32),
            pltpu.VMEM((width, 2 * rows), BF),
        ],
        cost_estimate=pl.CostEstimate(
            flops=4 * rows * width * columns,
            bytes_accessed=4 * acts.size + 2 * width * columns,
            transcendentals=0,
        ),
        name="weight_grads",
    )(place, acts, acts_too)


def attend_back_kernel(
    got, attn32, total, weights, queries, key_rows, value_rows, cosine, sine, hidden, send,
    grad_query, grad_key, grad_value, held, copied
):
    step = pl.program_id(0)
    copy = pltpu.make_async_copy(hidden, held, copied)

    @pl.when(step == 0)
    def _():
        copy.start()
        grad_key[...] = jnp.zeros_like(grad_key)
        grad_value[...] = jnp.zeros_like(grad_value)

    pieces = []
    for i in range(BLOCK // 64):
        block = got[i, 0]
        pieces += [block[:, :HEAD], block[:, HEAD:]]
    grad = jnp.concatenate(pieces, axis=0)
    wide = grad.astype(F32)
    dots = jnp.sum(wide * attn32[...], axis=-1, keepdims=True)
    grad_probs = lax.dot_general(
        grad, value_rows[...], BY_COLUMN, preferred_element_type=F32
    )
    inverse = 1.0 / total[...]
    low = weights[...]
    grad_scores = ((low.astype(F32) * inverse) * (grad_probs - dots)).astype(BF)
    grad_query[pl.ds(step * BLOCK, BLOCK), :] = HEAD**-0.5 * jnp.dot(
        grad_scores, key_rows[...], preferred_element_type=F32
    )
    grad_value[...] += lax.dot_general(
        low, (wide * inverse).astype(BF), BY_ROW, preferred_element_type=F32
    )
    grad_key[...] += lax.dot_general(
        grad_scores, queries[...], BY_ROW, preferred_element_type=F32
    )

    @pl.when(step == pl.num_programs(0) - 1)
    def _():
        length = grad_key.shape[0]
        both = side_by_side(grad_query[...], grad_key[...])
        both = (both * cosine[...] - turn(both) * sine[...]).astype(BF)
        low = grad_value[...].astype(BF)
        copy.wait()
        head_grad = jnp.transpose(
            lax.dot_general(
                side_by_side(both, low), held[...], BY_ROW, preferred_element_type=F32
            )
        )
        for i in range(length // 64):
            rows = head_grad[24 * i : 24 * i + 24].astype(BF)
            send[i // 2, i % 2, 96:120] = rows[:, :LANES]
            send[i // 2, i % 2, 120:136, :HEAD] = rows[:16, LANES:]
            send[i // 2, i % 2, 120:128, HEAD:] = rows[16:, LANES:]
        for i in range(length // 64):
            core, pair = i // (length // 128), i % (length // 128)
            rows = low[64 * i : 64 * i + 64]
            send[pair, core, :64] = both[64 * i : 64 * i + 64]
            send[pair, core, 64:96] = side_by_side(rows[:32], rows[32:])


def attend_back(
    got, attn32, total, weights, queries, key_rows, value_rows, cosine, sine, hidden
):
    length = queries.shape[0]
    steps = length // BLOCK
    by_row = lambda columns: pl.BlockSpec((BLOCK, columns), lambda i: (i, 0))
    whole = lambda *shape: pl.BlockSpec(shape, lambda i: (0,) * len(shape))
    send = (length // 128, 2, SENT, LANES)
    return pl.pallas_call(
        attend_back_kernel,
        grid=(steps,),
        in_specs=[
            pl.BlockSpec(
                (BLOCK // 64, 1, 32, LANES), lambda i: (i % (steps // 2), i // (steps // 2), 0, 0)
            ),
            by_row(HEAD),
            by_row(1),
            by_row(length),
            by_row(HEAD),
            whole(length, HEAD),
            whole(length, HEAD),
            whole(length, LANES),
            whole(length, LANES),
            pl.BlockSpec(memory_space=pl.ANY),
        ],
        out_specs=whole(*send),
        out_shape=jax.ShapeDtypeStruct(send, BF),
        scratch_shapes=[pltpu.VMEM((length, HEAD), F32)] * 3
        + [pltpu.VMEM(hidden.shape, BF), pltpu.SemaphoreType.DMA],
        cost_estimate=pl.CostEstimate(
            flops=14 * length * length * HEAD * 4,
            bytes_accessed=2 * length * length,
            transcendentals=0,
        ),
        name="attend_back",
    )(got, attn32, total, weights, queries, key_rows, value_rows, cosine, sine, hidden)


def last_kernel(
    got, weight, tokens, gain, grad_middle, own_weight, own_gain, result, grad_weight, gain_grad,
    grads
):
    width = tokens.shape[1]
    place = lambda j, h: slice(j * width + h * HEAD, j * width + h * HEAD + LANES)
    for s in range(2):
        for h in range(0, HEADS, 2):
            left, right = got[owner_slot(s, h)], got[owner_slot(s, h + 1)]
            top = slice(64 * s, 64 * s + 64)
            grads[top, place(0, h)] = side_by_side(left[:64, :HEAD], right[:64, :HEAD])
            grads[top, place(1, h)] = side_by_side(left[:64, HEAD:], right[:64, HEAD:])
            grads[64 * s : 64 * s + 32, place(2, h)] = side_by_side(
                left[64:96, :HEAD], right[64:96, :HEAD]
            )
            grads[64 * s + 32 : 64 * s + 64, place(2, h)] = side_by_side(
                left[64:96, HEAD:], right[64:96, HEAD:]
            )
    grad_hidden = lax.dot_general(
        grads[...], weight[...], BY_COLUMN, preferred_element_type=F32
    )
    normed, inverse = normalize(tokens[...].astype(F32))
    result[...] = (
        grad_middle[...] + norm_back(grad_hidden * gain[...], normed, inverse)
    ).astype(BF)

    def both(head, rows):
        return (
            got[owner_slot(0, head), rows].astype(F32) + got[owner_slot(1, head), rows].astype(F32)
        )

    for h in range(0, HEADS, 2):
        left, right = both(h, slice(96, 120)), both(h + 1, slice(96, 120))
        grad_weight[:, place(0, h)] = side_by_side(left[:, :HEAD], right[:, :HEAD])
        grad_weight[:, place(1, h)] = side_by_side(left[:, HEAD:], right[:, HEAD:])
        left, right = both(h, slice(120, 136)), both(h + 1, slice(120, 136))
        grad_weight[:16, place(2, h)] = side_by_side(left[:, :HEAD], right[:, :HEAD])
        grad_weight[16:, place(2, h)] = side_by_side(left[:8, HEAD:], right[:8, HEAD:])
    sums = jnp.sum(grad_weight[...] * own_weight[...].astype(F32), axis=1, keepdims=True)
    sums = jnp.transpose(jnp.broadcast_to(sums, (sums.shape[0], LANES)))[:8]
    gain_grad[...] = sums / own_gain[...]


def last_part(got, weight, tokens, gain, grad_middle, own_weight, own_gain):
    return pl.pallas_call(
        last_kernel,
        out_shape=[
            jax.ShapeDtypeStruct(tokens.shape, BF),
            jax.ShapeDtypeStruct(own_weight.shape, F32),
            jax.ShapeDtypeStruct((8, own_weight.shape[0]), F32),
        ],
        scratch_shapes=[pltpu.VMEM((tokens.shape[0], weight.shape[1]), BF)],
        name="last_part",
    )(got, weight, tokens, gain, grad_middle, own_weight, own_gain)


def owner_body(
    tokens, attn_gain, qkv_weight, attn_out_weight, mlp_gain, in_weight, out_weight, cotangent
):
    sequences, per_device, model_width = tokens.shape
    hidden_units = out_weight.shape[0]
    rows_here = qkv_weight.shape[0]
    rows = sequences * per_device
    length = per_device * 32
    core = my_bit("ulysses", 1).astype(jnp.int32).reshape(1)
    x, y = my_bit("blk", 1), my_bit("ulysses", 2)
    z = lax.axis_index("blk") // 2
    place = jnp.stack([x, y, my_bit("ulysses", 1), z]).astype(jnp.int32)
    late = jnp.concatenate([in_weight, attn_out_weight, jnp.transpose(out_weight)], axis=1)
    late_full = lax.all_gather(late, AXES, axis=0, tiled=True)
    by_head = qkv_weight.reshape(rows_here, 3, HEADS, HEAD).transpose(2, 0, 1, 3)
    by_head = by_head.reshape(HEADS, rows_here, 3 * HEAD)
    gains = jnp.stack([attn_gain, mlp_gain], axis=1)
    gains = jnp.broadcast_to(jnp.pad(gains, ((0, 0), (0, HEAD - 2))), (HEADS, rows_here, HEAD))
    packed = jnp.concatenate([by_head, gains], axis=2)
    packed = packed.reshape(HEADS // SHARE, SHARE, rows_here, 4 * HEAD)
    packed = jnp.concatenate([packed, packed[:, -1:]], axis=1)
    packed = jnp.broadcast_to(packed[None], (2,) + packed.shape)
    mixed = exchange(packed.reshape(32, rows_here, 4 * HEAD))
    mine, other, (mixed, cosine, sine) = gather_sequence(tokens, (mixed, *turned_tables(length)))
    weight_here = mixed.reshape(model_width, 4 * HEAD)
    gain_one = weight_here[:, 3 * HEAD].reshape(1, model_width).astype(F32)
    gain_two = weight_here[:, 3 * HEAD + 1].reshape(1, model_width).astype(F32)
    hidden_one, queries, key_rows, value_rows = project(
        core,
        mine,
        other,
        gain_one,
        weight_here,
        cosine.reshape(2, length // 2, LANES),
        sine.reshape(2, length // 2, LANES),
    )
    queries, key_rows, value_rows = (
        value.reshape(length, HEAD) for value in (queries, key_rows, value_rows)
    )
    weights_low, attn32, row_total, send = attend(queries, key_rows, value_rows)
    got = exchange(send.reshape(32, 32, LANES))
    flat_tokens = tokens.reshape(rows, model_width)
    grad_out = cotangent.reshape(rows, model_width)
    layer_output, send, acts, grad_middle = middle_part(
        got, flat_tokens, late_full, gain_two, grad_out
    )
    got = exchange(send)
    acts_too = swap(acts, "ulysses", 1)
    parts = weight_grads(place, acts, acts_too, model_width, hidden_units, rows_here)
    got, parts = lax.optimization_barrier((got, parts))
    *parts, own_c, give_c = parts
    keep_a, give_a, keep_b, give_b = (
        part.reshape(2, 2, *part.shape[1:]) for part in parts
    )
    came_a, came_b = swap(give_a, "blk", 1), swap(give_b, "ulysses", 2)
    came_c = [swap(give_c[k - 1], "blk", 2 * k) for k in (1, 2, 3)]
    send = attend_back(
        got.reshape(length // 128, 2, 32, LANES),
        attn32,
        row_total,
        weights_low,
        queries,
        key_rows,
        value_rows,
        cosine,
        sine,
        hidden_one.reshape(length, model_width),
    )
    qkv_full = lax.all_gather(qkv_weight, AXES, axis=0, tiled=True)
    send, came_a, came_b, came_c = lax.optimization_barrier((send, came_a, came_b, came_c))
    got = exchange(send.reshape(32, SENT, LANES))
    keep_a, give_a = halve(keep_a, came_a, "ulysses", 2, 2)
    keep_b, give_b = halve(keep_b, came_b, "blk", 1, 2)
    came_a, came_b = swap(give_a, "ulysses", 2), swap(give_b, "blk", 1)
    total_c = own_c.astype(F32)
    for part in came_c:
        total_c = total_c + part.astype(F32)
    total_c = total_c.astype(BF).reshape(4, rows_here, model_width)
    side = x * 2 + y
    shard_attn = [pick(total_c, side)]
    shard_attn.append(swap(pick(total_c, side ^ 2), "blk", 1))
    shard_attn.append(swap(pick(total_c, side ^ 1), "ulysses", 2))
    shard_attn.append(swap(pick(total_c, side ^ 3), AXES, 6))
    came_a, came_b, qkv_full = lax.optimization_barrier((came_a, came_b, qkv_full))
    total = [
        (keep.astype(F32) + came.astype(F32)).astype(BF).reshape(4, rows_here, -1)
        for keep, came in ((keep_a, came_a), (keep_b, came_b))
    ]

    def rows_of(owner):
        return jnp.concatenate([pick(part, owner) for part in total], axis=1)

    shards = [rows_of(z)] + [swap(rows_of(z ^ k), "blk", 2 * k) for k in (2, 3, 1)]
    last = last_part(
        got,
        qkv_full,
        flat_tokens,
        gain_one,
        grad_middle,
        qkv_weight,
        attn_gain.astype(F32).reshape(1, rows_here),
    )
    (input_grad, shard_qkv, shard_one), shards, shard_attn = lax.optimization_barrier(
        (last, shards, shard_attn)
    )
    input_grad = input_grad.reshape(sequences, per_device, model_width)
    shard_attn = sum(part.astype(F32) for part in shard_attn)
    shards = sum(part.astype(F32) for part in shards)
    shard_in = shards[:, : 2 * hidden_units]
    shard_out = jnp.transpose(shards[:, 2 * hidden_units :])
    shard_two = jnp.sum(shard_in * in_weight.astype(F32), axis=1) / mlp_gain.astype(F32)
    return (
        layer_output.reshape(sequences, per_device, model_width),
        input_grad,
        shard_one[0],
        shard_qkv,
        shard_attn,
        shard_two,
        shard_in,
        shard_out,
    )


def solution(mesh):
    placed = (
        P(None, ("blk", "ulysses"), None),
        P(("blk", "ulysses")),
        P(("blk", "ulysses"), None),
        P(("blk", "ulysses"), None),
        P(("blk", "ulysses")),
        P(("blk", "ulysses"), None),
        P(None, ("blk", "ulysses")),
        P(None, ("blk", "ulysses"), None),
    )
    sizes = (mesh.shape["blk"], mesh.shape["ulysses"])
    return jax.shard_map(
        owner_body if sizes == (8, 4) else ring_body,
        mesh=mesh,
        in_specs=placed,
        out_specs=(
            P(None, ("blk", "ulysses"), None),
            P(None, ("blk", "ulysses"), None),
            P(("blk", "ulysses")),
            P(("blk", "ulysses"), None),
            P(("blk", "ulysses"), None),
            P(("blk", "ulysses")),
            P(("blk", "ulysses"), None),
            P(None, ("blk", "ulysses")),
        ),
        check_vma=False,
    )
```

```python
import functools

import jax
import jax.numpy as jnp
from jax import lax
from jax.experimental import pallas as pl
from jax.experimental.pallas import tpu as pltpu
from jax.sharding import PartitionSpec as P

HEAD = 64


EPSILON = 1e-05
THETA = 160000.0


def from_behind(value, axis, by):
    size = lax.axis_size(axis)
    return lax.ppermute(value, axis, [(i, (i + by) % size) for i in range(size)])


def normalize(values):
    center = values - jnp.mean(values, axis=-1, keepdims=True)
    inverse = lax.rsqrt(jnp.mean(center * center, axis=-1, keepdims=True) + EPSILON)
    return (center * inverse, inverse)


def norm_back(grad_normed, normed, inverse):
    first_mean = jnp.mean(grad_normed, axis=-1, keepdims=True)
    second_mean = jnp.mean(grad_normed * normed, axis=-1, keepdims=True)
    return inverse * (grad_normed - first_mean - normed * second_mean)


def rotation(first_row, row_count, head_width):
    half_width = head_width // 2
    frequency = THETA ** (-(jnp.arange(half_width, dtype=jnp.float32) * 2.0) / head_width)
    positions = (first_row + jnp.arange(row_count, dtype=jnp.int32)).astype(jnp.float32)
    angles = positions[:, None] * frequency[None, :]
    cosine_table = jnp.concatenate([jnp.cos(angles), jnp.cos(angles)], axis=-1)
    sine_table = jnp.concatenate([jnp.sin(angles), jnp.sin(angles)], axis=-1)
    return (cosine_table, sine_table)


def rotate(values, cosine_table, sine_table, direction):
    half_width = values.shape[-1] // 2
    turned = jnp.concatenate([-values[..., half_width:], values[..., :half_width]], axis=-1)
    return values * cosine_table[:, None, :] + direction * turned * sine_table[:, None, :]


def block_grads(
    query_part,
    key_part,
    value_part,
    grad_part,
    log_part,
    dots_part,
    top_part,
    total_part,
    score_scale,
):
    scores = (
        jnp.einsum("sqhd,skhd->shqk", query_part, key_part, preferred_element_type=jnp.float32)
        * score_scale
    )
    probs = jnp.exp(scores - log_part[..., None])
    grad_probs = jnp.einsum(
        "sqhd,skhd->shqk", grad_part, value_part, preferred_element_type=jnp.float32
    )
    grad_scores = (probs * (grad_probs - dots_part[..., None])).astype(jnp.bfloat16)
    weights_low = jnp.exp(scores - top_part[..., None]).astype(jnp.bfloat16)
    grad_scaled = grad_part.astype(jnp.float32) / jnp.transpose(total_part, (0, 2, 1))[..., None]
    value_term = jnp.einsum("shqk,sqhd->skhd", weights_low.astype(jnp.float32), grad_scaled)
    return (value_term, grad_scores)


def ring_body(
    tokens, attn_gain, qkv_weight, attn_out_weight, mlp_gain, in_weight, out_weight, cotangent
):
    sequences, per_device, model_width = tokens.shape
    groups = lax.axis_size("ulysses")
    cycle_size = lax.axis_size("blk")
    group_width = model_width // groups
    heads_here = group_width // HEAD
    group_rows = per_device * groups
    score_scale = HEAD ** (-0.5)
    qkv_full, attn_full, in_full, out_full, gain_one, gain_two = (
        lax.all_gather(qkv_weight, ("blk", "ulysses"), axis=0, tiled=True),
        lax.all_gather(attn_out_weight, ("blk", "ulysses"), axis=0, tiled=True),
        lax.all_gather(in_weight, ("blk", "ulysses"), axis=0, tiled=True),
        lax.all_gather(out_weight, ("blk", "ulysses"), axis=1, tiled=True),
        lax.all_gather(attn_gain, ("blk", "ulysses"), axis=0, tiled=True),
        lax.all_gather(mlp_gain, ("blk", "ulysses"), axis=0, tiled=True),
    )
    gain_one = gain_one.astype(jnp.float32)
    gain_two = gain_two.astype(jnp.float32)
    hidden_units = out_full.shape[0]
    inputs_wide = tokens.astype(jnp.float32).reshape(sequences * per_device, model_width)
    normed_one, inverse_one = normalize(inputs_wide)
    hidden_one = (normed_one * gain_one).astype(jnp.bfloat16)
    qkv = jnp.dot(hidden_one, qkv_full, preferred_element_type=jnp.float32).astype(jnp.bfloat16)
    packed = qkv.reshape(sequences, per_device, 3, groups, group_width)
    headwise = lax.all_to_all(packed, "ulysses", split_axis=3, concat_axis=1, tiled=True)
    headwise = headwise.reshape(sequences, group_rows, 3, heads_here, HEAD)
    cosine_table, sine_table = rotation(lax.axis_index("blk") * group_rows, group_rows, HEAD)
    queries = rotate(headwise[:, :, 0].astype(jnp.float32), cosine_table, sine_table, 1.0).astype(
        jnp.bfloat16
    )
    key_rows = rotate(headwise[:, :, 1].astype(jnp.float32), cosine_table, sine_table, 1.0).astype(
        jnp.bfloat16
    )
    value_rows = headwise[:, :, 2]
    start_top = jnp.full((sequences, heads_here, group_rows), -1e30, jnp.float32)
    zeros_rows = jnp.zeros((sequences, group_rows, heads_here, HEAD), jnp.float32)
    key_piece = lax.all_gather(key_rows, "blk", axis=1, tiled=True)
    value_piece = lax.all_gather(value_rows, "blk", axis=1, tiled=True)
    scores = (
        jnp.einsum("sqhd,skhd->shqk", queries, key_piece, preferred_element_type=jnp.float32)
        * score_scale
    )
    new_top = jnp.maximum(start_top, jnp.max(scores, axis=-1))
    weights = jnp.exp(scores - new_top[..., None])
    attend_row_total = jnp.sum(weights, axis=-1)
    update = jnp.einsum(
        "shqk,skhd->sqhd",
        weights.astype(jnp.bfloat16),
        value_piece,
        preferred_element_type=jnp.float32,
    )
    weighted = update
    row_top, row_total, weighted = (new_top, attend_row_total, weighted)
    log_total = row_top + jnp.log(row_total)
    attn_wide = weighted / jnp.transpose(row_total, (0, 2, 1))[..., None]
    attn_low = attn_wide.astype(jnp.bfloat16).reshape(sequences, group_rows, 1, group_width)
    token_rows = lax.all_to_all(attn_low, "ulysses", split_axis=1, concat_axis=2, tiled=True)
    attn_cat = token_rows.reshape(sequences * per_device, model_width)
    middle = inputs_wide + jnp.dot(attn_cat, attn_full, preferred_element_type=jnp.float32)
    normed_two, inverse_two = normalize(middle)
    hidden_two = (normed_two * gain_two).astype(jnp.bfloat16)
    joint = jnp.dot(hidden_two, in_full, preferred_element_type=jnp.float32)

    def geglu(joint_pre):
        return (
            jax.nn.gelu(joint_pre[:, :hidden_units], approximate=False)
            * joint_pre[:, hidden_units:]
        )

    act_wide, geglu_back = jax.vjp(geglu, joint)
    activation = act_wide.astype(jnp.bfloat16)
    result = middle + jnp.dot(activation, out_full, preferred_element_type=jnp.float32)
    layer_output = result.astype(jnp.bfloat16).reshape(sequences, per_device, model_width)
    grad_out = cotangent.reshape(sequences * per_device, model_width)
    grad_wout = jnp.einsum("tf,td->fd", activation, grad_out, preferred_element_type=jnp.float32)
    grad_act = jnp.einsum("td,fd->tf", grad_out, out_full, preferred_element_type=jnp.float32)
    grad_joint = geglu_back(grad_act)[0].astype(jnp.bfloat16)
    grad_win = jnp.einsum("tc,tf->cf", hidden_two, grad_joint, preferred_element_type=jnp.float32)
    grad_hidden_two = jnp.einsum(
        "tf,cf->tc", grad_joint, in_full, preferred_element_type=jnp.float32
    )
    grad_gain_two = jnp.sum(grad_hidden_two * normed_two, axis=0)
    grad_middle = grad_out.astype(jnp.float32) + norm_back(
        grad_hidden_two * gain_two, normed_two, inverse_two
    )
    grad_branch = grad_middle.astype(jnp.bfloat16)
    grad_wattn = jnp.einsum("tc,td->cd", attn_cat, grad_branch, preferred_element_type=jnp.float32)
    grad_cat = jnp.einsum(
        "td,cd->tc", grad_branch, attn_full, preferred_element_type=jnp.float32
    ).astype(jnp.bfloat16)
    grad_heads_in = lax.all_to_all(
        grad_cat.reshape(sequences, per_device, groups, group_width),
        "ulysses",
        split_axis=2,
        concat_axis=1,
        tiled=True,
    )
    grad_attn = grad_heads_in.reshape(sequences, group_rows, heads_here, HEAD)
    row_dots = jnp.transpose(jnp.sum(grad_attn.astype(jnp.float32) * attn_wide, axis=-1), (0, 2, 1))

    def cycle_step(step_index, state_now):
        key_now, value_now, grad_key, grad_value, grad_query = state_now
        value_term, grad_scores = block_grads(
            queries,
            key_now,
            value_now,
            grad_attn,
            log_total,
            row_dots,
            row_top,
            row_total,
            score_scale,
        )
        grad_value = grad_value + value_term
        grad_key = grad_key + score_scale * jnp.einsum(
            "shqk,sqhd->skhd", grad_scores, queries, preferred_element_type=jnp.float32
        )
        grad_query = grad_query + score_scale * jnp.einsum(
            "shqk,skhd->sqhd", grad_scores, key_now, preferred_element_type=jnp.float32
        )
        key_now, value_now = from_behind((key_now, value_now), "blk", 1)
        grad_key, grad_value = (
            from_behind(grad_key.astype(jnp.bfloat16), "blk", 1).astype(grad_key.dtype),
            from_behind(grad_value.astype(jnp.bfloat16), "blk", 1).astype(grad_value.dtype),
        )
        return (key_now, value_now, grad_key, grad_value, grad_query)

    final_state = lax.fori_loop(
        0, cycle_size, cycle_step, (key_rows, value_rows, zeros_rows, zeros_rows, zeros_rows)
    )
    grad_key, grad_value, grad_query = (final_state[2], final_state[3], final_state[4])
    grad_query = rotate(grad_query, cosine_table, sine_table, -1.0)
    grad_key = rotate(grad_key, cosine_table, sine_table, -1.0)
    grad_stack = jnp.stack([grad_query, grad_key, grad_value], axis=2).astype(jnp.bfloat16)
    grad_stack = grad_stack.reshape(sequences, group_rows, 3, 1, group_width)
    grad_tokens = lax.all_to_all(grad_stack, "ulysses", split_axis=1, concat_axis=3, tiled=True)
    grad_qkv = grad_tokens.reshape(sequences * per_device, 3 * model_width)
    grad_wqkv = jnp.einsum("tc,tf->cf", hidden_one, grad_qkv, preferred_element_type=jnp.float32)
    grad_hidden_one = jnp.einsum(
        "tf,cf->tc", grad_qkv, qkv_full, preferred_element_type=jnp.float32
    )
    grad_gain_one = jnp.sum(grad_hidden_one * normed_one, axis=0)
    grad_input = grad_middle + norm_back(grad_hidden_one * gain_one, normed_one, inverse_one)
    input_grad = grad_input.astype(jnp.bfloat16).reshape(sequences, per_device, model_width)
    shard_qkv, shard_attn, shard_in, shard_out, shard_one, shard_two = (
        lax.psum_scatter(grad_wqkv, ("blk", "ulysses"), scatter_dimension=0, tiled=True),
        lax.psum_scatter(grad_wattn, ("blk", "ulysses"), scatter_dimension=0, tiled=True),
        lax.psum_scatter(grad_win, ("blk", "ulysses"), scatter_dimension=0, tiled=True),
        lax.psum_scatter(grad_wout, ("blk", "ulysses"), scatter_dimension=1, tiled=True),
        lax.psum_scatter(grad_gain_one, ("blk", "ulysses"), scatter_dimension=0, tiled=True),
        lax.psum_scatter(grad_gain_two, ("blk", "ulysses"), scatter_dimension=0, tiled=True),
    )
    return (
        layer_output,
        input_grad,
        shard_one,
        shard_qkv,
        shard_attn,
        shard_two,
        shard_in,
        shard_out,
    )


AXES = ("blk", "ulysses")
BF = jnp.bfloat16
F32 = jnp.float32
HEADS = 12
SHARE = 3
BLOCK = 256
LANES = 128
TILE = 384
SENT = 136
BY_COLUMN = (((1,), (1,)), ((), ()))
BY_ROW = (((0,), (0,)), ((), ()))


def swap(value, axis, bit):
    size = lax.axis_size(axis)
    return lax.ppermute(value, axis, [(i, i ^ bit) for i in range(size)])


def my_bit(axis, bit):
    return (lax.axis_index(axis) // bit) % 2


def join(mine, other, side, axis):
    first = jnp.stack([mine, other], axis=axis)
    second = jnp.stack([other, mine], axis=axis)
    return jnp.where(side == 0, first, second)


def gather_sequence(tokens, also):
    sequences, rows, width = tokens.shape
    z2, z1, x = my_bit("blk", 4), my_bit("blk", 2), my_bit("blk", 1)
    y = my_bit("ulysses", 2)
    keep = lax.dynamic_index_in_dim(tokens, z2, 0, keepdims=False)
    give = lax.dynamic_index_in_dim(tokens, 1 - z2, 0, keepdims=False)
    near = join(keep, swap(keep, "blk", 2), z1, 0)
    far = join(swap(give, "blk", 4), swap(give, "blk", 6), z1, 0)
    wide = join(near, far, z2, 0).reshape(2, 2, 2, rows // 2, width)
    part_a, part_b = wide[:, :, 0], wide[:, :, 1]
    from_a, from_b = swap(part_a, "blk", 1), swap(part_b, "ulysses", 2)
    part_a = join(part_a, from_a, x, 2)
    part_b = join(part_b, from_b, y, 2)
    from_a, from_b = swap(part_a, "ulysses", 2), swap(part_b, "blk", 1)
    part_a = join(part_a, from_a, y, 3)
    part_b = join(part_b, from_b, x, 2)
    wide = jnp.stack([part_a, part_b], axis=4).reshape(16 * rows, width)
    wide, also = lax.optimization_barrier((wide, also))
    return wide, swap(wide, "ulysses", 1), also


def halve(keep, got, axis, bit, dim):
    total = (keep.astype(F32) + got.astype(F32)).astype(BF)
    side = my_bit(axis, bit)
    keep = lax.dynamic_index_in_dim(total, side, dim, keepdims=False)
    give = lax.dynamic_index_in_dim(total, 1 - side, dim, keepdims=False)
    return keep, give


def turned_tables(rows):
    lane = jnp.arange(LANES, dtype=jnp.int32) % (HEAD // 2)
    frequency = THETA ** (-(lane.astype(F32) * 2.0) / HEAD)
    row = jnp.arange(rows, dtype=jnp.int32)
    half = rows // 2
    position = row % half // 64 * 128 + row // half * 64 + row % 64
    angles = position.astype(F32)[:, None] * frequency[None, :]
    return jnp.cos(angles), jnp.sin(angles)


def exchange(value):
    return lax.all_to_all(value, AXES, split_axis=0, concat_axis=0, tiled=True)


def owner_slot(sequence, head):
    return sequence * 16 + head // SHARE * (SHARE + 1) + head % SHARE


def turn(values):
    lane = lax.broadcasted_iota(jnp.int32, values.shape, 1) % HEAD
    return jnp.where(
        lane < HEAD // 2,
        -pltpu.roll(values, LANES - HEAD // 2, 1),
        pltpu.roll(values, HEAD // 2, 1),
    )


def side_by_side(left, right):
    return jnp.concatenate([left, right], axis=1)


def smem():
    return pl.BlockSpec(memory_space=pltpu.SMEM)


def project_kernel(
    core, mine, other, gain, weight, cosine, sine, hidden, queries, key_rows, value_rows
):
    def one(tokens, slot):
        normed, inverse = normalize(tokens[...].astype(F32))
        low = (normed * gain[...]).astype(BF)
        hidden[slot] = low
        qkv = jnp.dot(low, weight[:, : 3 * HEAD], preferred_element_type=F32).astype(BF)
        both = qkv[:, :LANES].astype(F32)
        both = (both * cosine[slot] + turn(both) * sine[slot]).astype(BF)
        queries[slot] = both[:, :HEAD] * BF(HEAD**-0.5)
        key_rows[slot] = both[:, HEAD:]
        value_rows[slot] = qkv[:, LANES:]

    one(mine, core[0])
    one(other, 1 - core[0])


def project(core, mine, other, gain, weight, cosine, sine):
    length, width = mine.shape
    by_row = pl.BlockSpec((BLOCK, width), lambda i: (i, 0))
    by_pair = lambda columns: pl.BlockSpec((2, BLOCK, columns), lambda i: (0, i, 0))
    whole = lambda shape: pl.BlockSpec(shape, lambda i: (0, 0))
    return pl.pallas_call(
        project_kernel,
        grid=(length // BLOCK,),
        in_specs=[
            smem(),
            by_row,
            by_row,
            whole((1, width)),
            whole(weight.shape),
            by_pair(LANES),
            by_pair(LANES),
        ],
        out_specs=[by_pair(width), by_pair(HEAD), by_pair(HEAD), by_pair(HEAD)],
        out_shape=[jax.ShapeDtypeStruct((2, length, width), BF)]
        + [jax.ShapeDtypeStruct((2, length, HEAD), BF)] * 3,
        name="project",
    )(core, mine, other, gain, weight, cosine, sine)


def attend_kernel(queries, key_rows, value_rows, weights, attn32, total, send):
    scores = lax.dot_general(
        queries[...], key_rows[...], BY_COLUMN, preferred_element_type=F32
    )
    top = jnp.max(scores, axis=-1, keepdims=True)
    expo = jnp.exp(scores - top)
    row_total = jnp.sum(expo, axis=-1, keepdims=True)
    low = expo.astype(BF)
    weights[...] = low
    mixed = jnp.dot(low, value_rows[...], preferred_element_type=F32) / row_total
    attn32[...] = mixed
    total[...] = row_total
    mixed = mixed.astype(BF)
    for i in range(BLOCK // 64):
        rows = mixed[64 * i : 64 * i + 64]
        send[i, 0] = side_by_side(rows[:32], rows[32:])


def attend(queries, key_rows, value_rows):
    length = queries.shape[0]
    by_row = lambda columns: pl.BlockSpec((BLOCK, columns), lambda i: (i, 0))
    whole = pl.BlockSpec((length, HEAD), lambda i: (0, 0))
    steps = length // BLOCK
    return pl.pallas_call(
        attend_kernel,
        grid=(steps,),
        in_specs=[by_row(HEAD), whole, whole],
        out_specs=[
            by_row(length),
            by_row(HEAD),
            by_row(1),
            pl.BlockSpec(
                (BLOCK // 64, 1, 32, LANES), lambda i: (i % (steps // 2), i // (steps // 2), 0, 0)
            ),
        ],
        out_shape=[
            jax.ShapeDtypeStruct((length, length), BF),
            jax.ShapeDtypeStruct((length, HEAD), F32),
            jax.ShapeDtypeStruct((length, 1), F32),
            jax.ShapeDtypeStruct((length // 128, 2, 32, LANES), BF),
        ],
        cost_estimate=pl.CostEstimate(
            flops=4 * length * length * HEAD * 4,
            bytes_accessed=2 * length * length,
            transcendentals=length * length,
        ),
        name="attend",
    )(queries, key_rows, value_rows)


def middle_kernel(
    got, tokens, late, gain, grad_out, layer_output, send, acts, grad_middle
):
    width = tokens.shape[1]
    hidden_units = (late.shape[1] - width) // 3
    cut = 2 * hidden_units
    attn, hidden = acts.at[:, :width], acts.at[:, width : 2 * width]
    acts[:, 2 * width : 3 * width] = grad_out[...]
    grad_joint = acts.at[:, 3 * width : 3 * width + cut]
    activation = acts.at[:, 3 * width + cut : 3 * width + cut + hidden_units]
    branch = acts.at[:, 3 * width + cut + hidden_units :]
    for s in range(2):
        for h in range(0, HEADS, 2):
            left, right = got[owner_slot(s, h)], got[owner_slot(s, h + 1)]
            columns = slice(h * HEAD, h * HEAD + LANES)
            attn[64 * s : 64 * s + 32, columns] = side_by_side(left[:, :HEAD], right[:, :HEAD])
            attn[64 * s + 32 : 64 * s + 64, columns] = side_by_side(
                left[:, HEAD:], right[:, HEAD:]
            )
    attn_weight = late[:, cut : cut + width]
    middle = tokens[...].astype(F32) + jnp.dot(
        attn[...], attn_weight, preferred_element_type=F32
    )
    normed, inverse = normalize(middle)
    low = (normed * gain[...]).astype(BF)
    hidden[...] = low
    first = jnp.dot(low, late[:, :hidden_units], preferred_element_type=F32)
    gate = jnp.dot(low, late[:, hidden_units:cut], preferred_element_type=F32)
    cumulative = 0.5 * (1.0 + lax.erf(first * (0.5**0.5)))
    bent = first * cumulative
    active = (bent * gate).astype(BF)
    activation[...] = active
    out_weight = late[:, cut + width :]
    layer_output[...] = (
        middle + lax.dot_general(active, out_weight, BY_COLUMN, preferred_element_type=F32)
    ).astype(BF)
    grad_act = jnp.dot(grad_out[...], out_weight, preferred_element_type=F32)
    density = jnp.exp(-0.5 * first * first) * 0.3989422804014327
    grad_joint[:, :hidden_units] = (grad_act * gate * (cumulative + first * density)).astype(BF)
    grad_joint[:, hidden_units:] = (grad_act * bent).astype(BF)
    grad_hidden = lax.dot_general(
        grad_joint[...], late[:, :cut], BY_COLUMN, preferred_element_type=F32
    )
    total = grad_out[...].astype(F32) + norm_back(grad_hidden * gain[...], normed, inverse)
    grad_middle[...] = total
    branch_low = total.astype(BF)
    branch[...] = branch_low
    grad_cat = lax.dot_general(
        branch_low, attn_weight, BY_COLUMN, preferred_element_type=F32
    ).astype(BF)
    for s in range(2):
        for h in range(HEADS):
            rows = grad_cat[64 * s : 64 * s + 64, h * HEAD : (h + 1) * HEAD]
            block = side_by_side(rows[:32], rows[32:])
            send[owner_slot(s, h)] = block
            if h % SHARE == SHARE - 1:
                send[owner_slot(s, h) + 1] = block


def middle_part(got, tokens, late, gain, grad_out):
    rows, width = tokens.shape
    hidden_units = (late.shape[1] - width) // 3
    shapes = [
        ((rows, width), BF),
        (got.shape, BF),
        ((rows, 4 * width + 3 * hidden_units), BF),
        ((rows, width), F32),
    ]
    return pl.pallas_call(
        middle_kernel,
        out_shape=[jax.ShapeDtypeStruct(shape, kind) for shape, kind in shapes],
        name="middle_part",
    )(got, tokens, late, gain, grad_out)


def weight_grads_kernel(
    place, acts, acts_too, keep_a, give_a, keep_b, give_b, total, turned, *, width, hidden_units
):
    x, y, core = place[0], place[1], place[2]
    rows = acts.shape[0]
    cut = 3 * width + 2 * hidden_units

    def turn_rows(i):
        columns = slice(i * width, (i + 1) * width)
        turned[:, :rows] = jnp.transpose(acts[:, columns])
        turned[:, rows:] = jnp.transpose(acts_too[:, columns])

    def multiply(start, count):
        right = jnp.concatenate(
            [acts[:, start : start + count], acts_too[:, start : start + count]], axis=0
        )
        product = jnp.dot(turned[...], right, preferred_element_type=F32)
        total[..., :count] = product.reshape(*total.shape[:-1], count)

    turn_rows(1)
    for i in range(2 * hidden_units // TILE):
        columns = slice(i * TILE, (i + 1) * TILE)
        multiply(3 * width + i * TILE, TILE)
        keep_a[..., columns] = total[:, x, :, core].astype(BF)
        give_a[..., columns] = total[:, 1 - x, :, core].astype(BF)
    turn_rows(0)
    for i in range((width + hidden_units) // TILE):
        columns = slice(i * TILE, (i + 1) * TILE)
        if i == width // TILE:
            turn_rows(2)
        if i < width // TILE:
            multiply(cut + hidden_units + i * TILE, TILE)
        else:
            multiply(cut - width + i * TILE, TILE)
        keep_b[..., columns] = total[:, :, y, core].astype(BF)
        give_b[..., columns] = total[:, :, 1 - y, core].astype(BF)


def weight_grads(place, acts, acts_too, width, hidden_units, rows_here):
    rows = acts.shape[0]
    zs = width // (8 * rows_here)
    shape = lambda columns: jax.ShapeDtypeStruct((zs, 2, rows_here, columns), BF)
    columns = 3 * hidden_units + width
    return pl.pallas_call(
        functools.partial(weight_grads_kernel, width=width, hidden_units=hidden_units),
        in_specs=[smem()] + [pl.BlockSpec(memory_space=pltpu.VMEM)] * 2,
        out_shape=[shape(2 * hidden_units)] * 2 + [shape(width + hidden_units)] * 2,
        scratch_shapes=[
            pltpu.VMEM((zs, 2, 2, 2, rows_here, TILE), F32),
            pltpu.VMEM((width, 2 * rows), BF),
        ],
        cost_estimate=pl.CostEstimate(
            flops=4 * rows * width * columns,
            bytes_accessed=4 * acts.size + 2 * width * columns,
            transcendentals=0,
        ),
        name="weight_grads",
    )(place, acts, acts_too)


def attend_back_kernel(
    got, attn32, total, weights, queries, key_rows, value_rows, cosine, sine, hidden, send,
    grad_query, grad_key, grad_value, held, copied
):
    step = pl.program_id(0)
    copy = pltpu.make_async_copy(hidden, held, copied)

    @pl.when(step == 0)
    def _():
        copy.start()
        grad_key[...] = jnp.zeros_like(grad_key)
        grad_value[...] = jnp.zeros_like(grad_value)

    pieces = []
    for i in range(BLOCK // 64):
        block = got[i, 0]
        pieces += [block[:, :HEAD], block[:, HEAD:]]
    grad = jnp.concatenate(pieces, axis=0)
    wide = grad.astype(F32)
    dots = jnp.sum(wide * attn32[...], axis=-1, keepdims=True)
    grad_probs = lax.dot_general(
        grad, value_rows[...], BY_COLUMN, preferred_element_type=F32
    )
    inverse = 1.0 / total[...]
    low = weights[...]
    grad_scores = ((low.astype(F32) * inverse) * (grad_probs - dots)).astype(BF)
    grad_query[pl.ds(step * BLOCK, BLOCK), :] = HEAD**-0.5 * jnp.dot(
        grad_scores, key_rows[...], preferred_element_type=F32
    )
    grad_value[...] += lax.dot_general(
        (wide * inverse).astype(BF), low, BY_ROW, preferred_element_type=F32
    )
    grad_key[...] += lax.dot_general(
        queries[...], grad_scores, BY_ROW, preferred_element_type=F32
    )

    @pl.when(step == pl.num_programs(0) - 1)
    def _():
        length = grad_query.shape[0]
        both = side_by_side(grad_query[...], jnp.transpose(grad_key[...]))
        both = (both * cosine[...] - turn(both) * sine[...]).astype(BF)
        low = jnp.transpose(grad_value[...]).astype(BF)
        copy.wait()
        head_grad = jnp.transpose(
            lax.dot_general(
                side_by_side(both, low), held[...], BY_ROW, preferred_element_type=F32
            )
        )
        for i in range(length // 64):
            rows = head_grad[24 * i : 24 * i + 24].astype(BF)
            send[i // 2, i % 2, 96:120] = rows[:, :LANES]
            send[i // 2, i % 2, 120:136, :HEAD] = rows[:16, LANES:]
            send[i // 2, i % 2, 120:128, HEAD:] = rows[16:, LANES:]
        for i in range(length // 64):
            core, pair = i // (length // 128), i % (length // 128)
            rows = low[64 * i : 64 * i + 64]
            send[pair, core, :64] = both[64 * i : 64 * i + 64]
            send[pair, core, 64:96] = side_by_side(rows[:32], rows[32:])


def attend_back(
    got, attn32, total, weights, queries, key_rows, value_rows, cosine, sine, hidden
):
    length = queries.shape[0]
    steps = length // BLOCK
    by_row = lambda columns: pl.BlockSpec((BLOCK, columns), lambda i: (i, 0))
    whole = lambda *shape: pl.BlockSpec(shape, lambda i: (0,) * len(shape))
    send = (length // 128, 2, SENT, LANES)
    return pl.pallas_call(
        attend_back_kernel,
        grid=(steps,),
        in_specs=[
            pl.BlockSpec(
                (BLOCK // 64, 1, 32, LANES), lambda i: (i % (steps // 2), i // (steps // 2), 0, 0)
            ),
            by_row(HEAD),
            by_row(1),
            by_row(length),
            by_row(HEAD),
            whole(length, HEAD),
            whole(length, HEAD),
            whole(length, LANES),
            whole(length, LANES),
            pl.BlockSpec(memory_space=pl.ANY),
        ],
        out_specs=whole(*send),
        out_shape=jax.ShapeDtypeStruct(send, BF),
        scratch_shapes=[pltpu.VMEM((length, HEAD), F32)]
        + [pltpu.VMEM((HEAD, length), F32)] * 2
        + [pltpu.VMEM(hidden.shape, BF), pltpu.SemaphoreType.DMA],
        cost_estimate=pl.CostEstimate(
            flops=14 * length * length * HEAD * 4,
            bytes_accessed=2 * length * length,
            transcendentals=0,
        ),
        name="attend_back",
    )(got, attn32, total, weights, queries, key_rows, value_rows, cosine, sine, hidden)


def last_kernel(
    got, weight, tokens, gain, grad_middle, own_weight, own_gain, result, grad_weight, gain_grad,
    grads
):
    width = tokens.shape[1]
    place = lambda j, h: slice(j * width + h * HEAD, j * width + h * HEAD + LANES)
    for s in range(2):
        for h in range(0, HEADS, 2):
            left, right = got[owner_slot(s, h)], got[owner_slot(s, h + 1)]
            top = slice(64 * s, 64 * s + 64)
            grads[top, place(0, h)] = side_by_side(left[:64, :HEAD], right[:64, :HEAD])
            grads[top, place(1, h)] = side_by_side(left[:64, HEAD:], right[:64, HEAD:])
            grads[64 * s : 64 * s + 32, place(2, h)] = side_by_side(
                left[64:96, :HEAD], right[64:96, :HEAD]
            )
            grads[64 * s + 32 : 64 * s + 64, place(2, h)] = side_by_side(
                left[64:96, HEAD:], right[64:96, HEAD:]
            )
    grad_hidden = lax.dot_general(
        grads[...], weight[...], BY_COLUMN, preferred_element_type=F32
    )
    normed, inverse = normalize(tokens[...].astype(F32))
    result[...] = (
        grad_middle[...] + norm_back(grad_hidden * gain[...], normed, inverse)
    ).astype(BF)

    def both(head, rows):
        return (
            got[owner_slot(0, head), rows].astype(F32) + got[owner_slot(1, head), rows].astype(F32)
        )

    for h in range(0, HEADS, 2):
        left, right = both(h, slice(96, 120)), both(h + 1, slice(96, 120))
        grad_weight[:, place(0, h)] = side_by_side(left[:, :HEAD], right[:, :HEAD])
        grad_weight[:, place(1, h)] = side_by_side(left[:, HEAD:], right[:, HEAD:])
        left, right = both(h, slice(120, 136)), both(h + 1, slice(120, 136))
        grad_weight[:16, place(2, h)] = side_by_side(left[:, :HEAD], right[:, :HEAD])
        grad_weight[16:, place(2, h)] = side_by_side(left[:8, HEAD:], right[:8, HEAD:])
    sums = jnp.sum(grad_weight[...] * own_weight[...].astype(F32), axis=1, keepdims=True)
    sums = jnp.transpose(jnp.broadcast_to(sums, (sums.shape[0], LANES)))[:8]
    gain_grad[...] = (sums / own_gain[...])[0]


def last_part(got, weight, tokens, gain, grad_middle, own_weight, own_gain):
    return pl.pallas_call(
        last_kernel,
        out_shape=[
            jax.ShapeDtypeStruct(tokens.shape, BF),
            jax.ShapeDtypeStruct(own_weight.shape, F32),
            jax.ShapeDtypeStruct((own_weight.shape[0],), F32),
        ],
        scratch_shapes=[pltpu.VMEM((tokens.shape[0], weight.shape[1]), BF)],
        name="last_part",
    )(got, weight, tokens, gain, grad_middle, own_weight, own_gain)


def owner_body(
    tokens, attn_gain, qkv_weight, attn_out_weight, mlp_gain, in_weight, out_weight, cotangent
):
    sequences, per_device, model_width = tokens.shape
    hidden_units = out_weight.shape[0]
    rows_here = qkv_weight.shape[0]
    rows = sequences * per_device
    length = per_device * 32
    core = my_bit("ulysses", 1).astype(jnp.int32).reshape(1)
    place = jnp.stack([my_bit("blk", 1), my_bit("ulysses", 2), my_bit("ulysses", 1)])
    place = place.astype(jnp.int32)
    late = jnp.concatenate([in_weight, attn_out_weight, jnp.transpose(out_weight)], axis=1)
    late_full = lax.all_gather(late, AXES, axis=0, tiled=True)
    by_head = qkv_weight.reshape(rows_here, 3, HEADS, HEAD).transpose(2, 0, 1, 3)
    by_head = by_head.reshape(HEADS, rows_here, 3 * HEAD)
    gains = jnp.stack([attn_gain, mlp_gain], axis=1)
    gains = jnp.broadcast_to(jnp.pad(gains, ((0, 0), (0, HEAD - 2))), (HEADS, rows_here, HEAD))
    packed = jnp.concatenate([by_head, gains], axis=2)
    packed = packed.reshape(HEADS // SHARE, SHARE, rows_here, 4 * HEAD)
    packed = jnp.concatenate([packed, packed[:, -1:]], axis=1)
    packed = jnp.broadcast_to(packed[None], (2,) + packed.shape)
    mixed = exchange(packed.reshape(32, rows_here, 4 * HEAD))
    mine, other, (mixed, cosine, sine) = gather_sequence(tokens, (mixed, *turned_tables(length)))
    weight_here = mixed.reshape(model_width, 4 * HEAD)
    gain_one = weight_here[:, 3 * HEAD].reshape(1, model_width).astype(F32)
    gain_two = weight_here[:, 3 * HEAD + 1].reshape(1, model_width).astype(F32)
    hidden_one, queries, key_rows, value_rows = project(
        core,
        mine,
        other,
        gain_one,
        weight_here,
        cosine.reshape(2, length // 2, LANES),
        sine.reshape(2, length // 2, LANES),
    )
    queries, key_rows, value_rows = (
        value.reshape(length, HEAD) for value in (queries, key_rows, value_rows)
    )
    weights_low, attn32, row_total, send = attend(queries, key_rows, value_rows)
    got = exchange(send.reshape(32, 32, LANES))
    flat_tokens = tokens.reshape(rows, model_width)
    grad_out = cotangent.reshape(rows, model_width)
    layer_output, send, acts, grad_middle = middle_part(
        got, flat_tokens, late_full, gain_two, grad_out
    )
    got = exchange(send)
    acts_too = swap(acts, "ulysses", 1)
    parts = weight_grads(place, acts, acts_too, model_width, hidden_units, rows_here)
    got, parts = lax.optimization_barrier((got, parts))
    keep_a, give_a, keep_b, give_b = (
        part.reshape(2, 2, *part.shape[1:]) for part in parts
    )
    came_a, came_b = swap(give_a, "blk", 1), swap(give_b, "ulysses", 2)
    send = attend_back(
        got.reshape(length // 128, 2, 32, LANES),
        attn32,
        row_total,
        weights_low,
        queries,
        key_rows,
        value_rows,
        cosine,
        sine,
        hidden_one.reshape(length, model_width),
    )
    qkv_full = lax.all_gather(qkv_weight, AXES, axis=0, tiled=True)
    send, came_a, came_b = lax.optimization_barrier((send, came_a, came_b))
    got = exchange(send.reshape(32, SENT, LANES))
    keep_a, give_a = halve(keep_a, came_a, "ulysses", 2, 2)
    keep_b, give_b = halve(keep_b, came_b, "blk", 1, 2)
    came_a, came_b = swap(give_a, "ulysses", 2), swap(give_b, "blk", 1)
    z = lax.axis_index("blk") // 2

    def spread(keep, came):
        total = (keep.astype(F32) + came.astype(F32)).astype(BF).reshape(4, rows_here, -1)
        row = lambda owner: lax.dynamic_index_in_dim(total, owner, 0, keepdims=False)
        return [row(z)] + [swap(row(z ^ k), "blk", 2 * k) for k in (2, 3, 1)]

    parts_a = spread(keep_a, came_a)
    came_b, qkv_full = lax.optimization_barrier((came_b, qkv_full))
    parts_b = spread(keep_b, came_b)
    last = last_part(
        got,
        qkv_full,
        flat_tokens,
        gain_one,
        grad_middle,
        qkv_weight,
        attn_gain.astype(F32).reshape(1, rows_here),
    )
    (input_grad, shard_qkv, shard_one), parts_a, parts_b = lax.optimization_barrier(
        (last, parts_a, parts_b)
    )
    input_grad = input_grad.reshape(sequences, per_device, model_width)
    shard_in = sum(part.astype(F32) for part in parts_a)
    shards = sum(part.astype(F32) for part in parts_b)
    shard_attn = shards[:, :model_width]
    shard_out = jnp.transpose(shards[:, model_width:])
    shard_two = jnp.sum(shard_in * in_weight.astype(F32), axis=1) / mlp_gain.astype(F32)
    return (
        layer_output.reshape(sequences, per_device, model_width),
        input_grad,
        shard_one,
        shard_qkv,
        shard_attn,
        shard_two,
        shard_in,
        shard_out,
    )


def solution(mesh):
    placed = (
        P(None, ("blk", "ulysses"), None),
        P(("blk", "ulysses")),
        P(("blk", "ulysses"), None),
        P(("blk", "ulysses"), None),
        P(("blk", "ulysses")),
        P(("blk", "ulysses"), None),
        P(None, ("blk", "ulysses")),
        P(None, ("blk", "ulysses"), None),
    )
    sizes = (mesh.shape["blk"], mesh.shape["ulysses"])
    return jax.shard_map(
        owner_body if sizes == (8, 4) else ring_body,
        mesh=mesh,
        in_specs=placed,
        out_specs=(
            P(None, ("blk", "ulysses"), None),
            P(None, ("blk", "ulysses"), None),
            P(("blk", "ulysses")),
            P(("blk", "ulysses"), None),
            P(("blk", "ulysses"), None),
            P(("blk", "ulysses")),
            P(("blk", "ulysses"), None),
            P(None, ("blk", "ulysses")),
        ),
        check_vma=False,
    )
```

```python
import functools

import jax
import jax.numpy as jnp
from jax import lax
from jax.experimental import pallas as pl
from jax.experimental.pallas import tpu as pltpu
from jax.sharding import PartitionSpec as P

HEAD = 64


EPSILON = 1e-05
THETA = 160000.0


def from_behind(value, axis, by):
    size = lax.axis_size(axis)
    return lax.ppermute(value, axis, [(i, (i + by) % size) for i in range(size)])


def normalize(values):
    center = values - jnp.mean(values, axis=-1, keepdims=True)
    inverse = lax.rsqrt(jnp.mean(center * center, axis=-1, keepdims=True) + EPSILON)
    return (center * inverse, inverse)


def norm_back(grad_normed, normed, inverse):
    first_mean = jnp.mean(grad_normed, axis=-1, keepdims=True)
    second_mean = jnp.mean(grad_normed * normed, axis=-1, keepdims=True)
    return inverse * (grad_normed - first_mean - normed * second_mean)


def rotation(first_row, row_count, head_width):
    half_width = head_width // 2
    frequency = THETA ** (-(jnp.arange(half_width, dtype=jnp.float32) * 2.0) / head_width)
    positions = (first_row + jnp.arange(row_count, dtype=jnp.int32)).astype(jnp.float32)
    angles = positions[:, None] * frequency[None, :]
    cosine_table = jnp.concatenate([jnp.cos(angles), jnp.cos(angles)], axis=-1)
    sine_table = jnp.concatenate([jnp.sin(angles), jnp.sin(angles)], axis=-1)
    return (cosine_table, sine_table)


def rotate(values, cosine_table, sine_table, direction):
    half_width = values.shape[-1] // 2
    turned = jnp.concatenate([-values[..., half_width:], values[..., :half_width]], axis=-1)
    return values * cosine_table[:, None, :] + direction * turned * sine_table[:, None, :]


def block_grads(
    query_part,
    key_part,
    value_part,
    grad_part,
    log_part,
    dots_part,
    top_part,
    total_part,
    score_scale,
):
    scores = (
        jnp.einsum("sqhd,skhd->shqk", query_part, key_part, preferred_element_type=jnp.float32)
        * score_scale
    )
    probs = jnp.exp(scores - log_part[..., None])
    grad_probs = jnp.einsum(
        "sqhd,skhd->shqk", grad_part, value_part, preferred_element_type=jnp.float32
    )
    grad_scores = (probs * (grad_probs - dots_part[..., None])).astype(jnp.bfloat16)
    weights_low = jnp.exp(scores - top_part[..., None]).astype(jnp.bfloat16)
    grad_scaled = grad_part.astype(jnp.float32) / jnp.transpose(total_part, (0, 2, 1))[..., None]
    value_term = jnp.einsum("shqk,sqhd->skhd", weights_low.astype(jnp.float32), grad_scaled)
    return (value_term, grad_scores)


def ring_body(
    tokens, attn_gain, qkv_weight, attn_out_weight, mlp_gain, in_weight, out_weight, cotangent
):
    sequences, per_device, model_width = tokens.shape
    groups = lax.axis_size("ulysses")
    cycle_size = lax.axis_size("blk")
    group_width = model_width // groups
    heads_here = group_width // HEAD
    group_rows = per_device * groups
    score_scale = HEAD ** (-0.5)
    qkv_full, attn_full, in_full, out_full, gain_one, gain_two = (
        lax.all_gather(qkv_weight, ("blk", "ulysses"), axis=0, tiled=True),
        lax.all_gather(attn_out_weight, ("blk", "ulysses"), axis=0, tiled=True),
        lax.all_gather(in_weight, ("blk", "ulysses"), axis=0, tiled=True),
        lax.all_gather(out_weight, ("blk", "ulysses"), axis=1, tiled=True),
        lax.all_gather(attn_gain, ("blk", "ulysses"), axis=0, tiled=True),
        lax.all_gather(mlp_gain, ("blk", "ulysses"), axis=0, tiled=True),
    )
    gain_one = gain_one.astype(jnp.float32)
    gain_two = gain_two.astype(jnp.float32)
    hidden_units = out_full.shape[0]
    inputs_wide = tokens.astype(jnp.float32).reshape(sequences * per_device, model_width)
    normed_one, inverse_one = normalize(inputs_wide)
    hidden_one = (normed_one * gain_one).astype(jnp.bfloat16)
    qkv = jnp.dot(hidden_one, qkv_full, preferred_element_type=jnp.float32).astype(jnp.bfloat16)
    packed = qkv.reshape(sequences, per_device, 3, groups, group_width)
    headwise = lax.all_to_all(packed, "ulysses", split_axis=3, concat_axis=1, tiled=True)
    headwise = headwise.reshape(sequences, group_rows, 3, heads_here, HEAD)
    cosine_table, sine_table = rotation(lax.axis_index("blk") * group_rows, group_rows, HEAD)
    queries = rotate(headwise[:, :, 0].astype(jnp.float32), cosine_table, sine_table, 1.0).astype(
        jnp.bfloat16
    )
    key_rows = rotate(headwise[:, :, 1].astype(jnp.float32), cosine_table, sine_table, 1.0).astype(
        jnp.bfloat16
    )
    value_rows = headwise[:, :, 2]
    start_top = jnp.full((sequences, heads_here, group_rows), -1e30, jnp.float32)
    zeros_rows = jnp.zeros((sequences, group_rows, heads_here, HEAD), jnp.float32)
    key_piece = lax.all_gather(key_rows, "blk", axis=1, tiled=True)
    value_piece = lax.all_gather(value_rows, "blk", axis=1, tiled=True)
    scores = (
        jnp.einsum("sqhd,skhd->shqk", queries, key_piece, preferred_element_type=jnp.float32)
        * score_scale
    )
    new_top = jnp.maximum(start_top, jnp.max(scores, axis=-1))
    weights = jnp.exp(scores - new_top[..., None])
    attend_row_total = jnp.sum(weights, axis=-1)
    update = jnp.einsum(
        "shqk,skhd->sqhd",
        weights.astype(jnp.bfloat16),
        value_piece,
        preferred_element_type=jnp.float32,
    )
    weighted = update
    row_top, row_total, weighted = (new_top, attend_row_total, weighted)
    log_total = row_top + jnp.log(row_total)
    attn_wide = weighted / jnp.transpose(row_total, (0, 2, 1))[..., None]
    attn_low = attn_wide.astype(jnp.bfloat16).reshape(sequences, group_rows, 1, group_width)
    token_rows = lax.all_to_all(attn_low, "ulysses", split_axis=1, concat_axis=2, tiled=True)
    attn_cat = token_rows.reshape(sequences * per_device, model_width)
    middle = inputs_wide + jnp.dot(attn_cat, attn_full, preferred_element_type=jnp.float32)
    normed_two, inverse_two = normalize(middle)
    hidden_two = (normed_two * gain_two).astype(jnp.bfloat16)
    joint = jnp.dot(hidden_two, in_full, preferred_element_type=jnp.float32)

    def geglu(joint_pre):
        return (
            jax.nn.gelu(joint_pre[:, :hidden_units], approximate=False)
            * joint_pre[:, hidden_units:]
        )

    act_wide, geglu_back = jax.vjp(geglu, joint)
    activation = act_wide.astype(jnp.bfloat16)
    result = middle + jnp.dot(activation, out_full, preferred_element_type=jnp.float32)
    layer_output = result.astype(jnp.bfloat16).reshape(sequences, per_device, model_width)
    grad_out = cotangent.reshape(sequences * per_device, model_width)
    grad_wout = jnp.einsum("tf,td->fd", activation, grad_out, preferred_element_type=jnp.float32)
    grad_act = jnp.einsum("td,fd->tf", grad_out, out_full, preferred_element_type=jnp.float32)
    grad_joint = geglu_back(grad_act)[0].astype(jnp.bfloat16)
    grad_win = jnp.einsum("tc,tf->cf", hidden_two, grad_joint, preferred_element_type=jnp.float32)
    grad_hidden_two = jnp.einsum(
        "tf,cf->tc", grad_joint, in_full, preferred_element_type=jnp.float32
    )
    grad_gain_two = jnp.sum(grad_hidden_two * normed_two, axis=0)
    grad_middle = grad_out.astype(jnp.float32) + norm_back(
        grad_hidden_two * gain_two, normed_two, inverse_two
    )
    grad_branch = grad_middle.astype(jnp.bfloat16)
    grad_wattn = jnp.einsum("tc,td->cd", attn_cat, grad_branch, preferred_element_type=jnp.float32)
    grad_cat = jnp.einsum(
        "td,cd->tc", grad_branch, attn_full, preferred_element_type=jnp.float32
    ).astype(jnp.bfloat16)
    grad_heads_in = lax.all_to_all(
        grad_cat.reshape(sequences, per_device, groups, group_width),
        "ulysses",
        split_axis=2,
        concat_axis=1,
        tiled=True,
    )
    grad_attn = grad_heads_in.reshape(sequences, group_rows, heads_here, HEAD)
    row_dots = jnp.transpose(jnp.sum(grad_attn.astype(jnp.float32) * attn_wide, axis=-1), (0, 2, 1))

    def cycle_step(step_index, state_now):
        key_now, value_now, grad_key, grad_value, grad_query = state_now
        value_term, grad_scores = block_grads(
            queries,
            key_now,
            value_now,
            grad_attn,
            log_total,
            row_dots,
            row_top,
            row_total,
            score_scale,
        )
        grad_value = grad_value + value_term
        grad_key = grad_key + score_scale * jnp.einsum(
            "shqk,sqhd->skhd", grad_scores, queries, preferred_element_type=jnp.float32
        )
        grad_query = grad_query + score_scale * jnp.einsum(
            "shqk,skhd->sqhd", grad_scores, key_now, preferred_element_type=jnp.float32
        )
        key_now, value_now = from_behind((key_now, value_now), "blk", 1)
        grad_key, grad_value = (
            from_behind(grad_key.astype(jnp.bfloat16), "blk", 1).astype(grad_key.dtype),
            from_behind(grad_value.astype(jnp.bfloat16), "blk", 1).astype(grad_value.dtype),
        )
        return (key_now, value_now, grad_key, grad_value, grad_query)

    final_state = lax.fori_loop(
        0, cycle_size, cycle_step, (key_rows, value_rows, zeros_rows, zeros_rows, zeros_rows)
    )
    grad_key, grad_value, grad_query = (final_state[2], final_state[3], final_state[4])
    grad_query = rotate(grad_query, cosine_table, sine_table, -1.0)
    grad_key = rotate(grad_key, cosine_table, sine_table, -1.0)
    grad_stack = jnp.stack([grad_query, grad_key, grad_value], axis=2).astype(jnp.bfloat16)
    grad_stack = grad_stack.reshape(sequences, group_rows, 3, 1, group_width)
    grad_tokens = lax.all_to_all(grad_stack, "ulysses", split_axis=1, concat_axis=3, tiled=True)
    grad_qkv = grad_tokens.reshape(sequences * per_device, 3 * model_width)
    grad_wqkv = jnp.einsum("tc,tf->cf", hidden_one, grad_qkv, preferred_element_type=jnp.float32)
    grad_hidden_one = jnp.einsum(
        "tf,cf->tc", grad_qkv, qkv_full, preferred_element_type=jnp.float32
    )
    grad_gain_one = jnp.sum(grad_hidden_one * normed_one, axis=0)
    grad_input = grad_middle + norm_back(grad_hidden_one * gain_one, normed_one, inverse_one)
    input_grad = grad_input.astype(jnp.bfloat16).reshape(sequences, per_device, model_width)
    shard_qkv, shard_attn, shard_in, shard_out, shard_one, shard_two = (
        lax.psum_scatter(grad_wqkv, ("blk", "ulysses"), scatter_dimension=0, tiled=True),
        lax.psum_scatter(grad_wattn, ("blk", "ulysses"), scatter_dimension=0, tiled=True),
        lax.psum_scatter(grad_win, ("blk", "ulysses"), scatter_dimension=0, tiled=True),
        lax.psum_scatter(grad_wout, ("blk", "ulysses"), scatter_dimension=1, tiled=True),
        lax.psum_scatter(grad_gain_one, ("blk", "ulysses"), scatter_dimension=0, tiled=True),
        lax.psum_scatter(grad_gain_two, ("blk", "ulysses"), scatter_dimension=0, tiled=True),
    )
    return (
        layer_output,
        input_grad,
        shard_one,
        shard_qkv,
        shard_attn,
        shard_two,
        shard_in,
        shard_out,
    )


AXES = ("blk", "ulysses")
BF = jnp.bfloat16
F32 = jnp.float32
HEADS = 12
SHARE = 3
BLOCK = 256
LANES = 128
TILE = 384
SENT = 136
BY_COLUMN = (((1,), (1,)), ((), ()))
BY_ROW = (((0,), (0,)), ((), ()))


def swap(value, axis, bit):
    size = lax.axis_size(axis)
    return lax.ppermute(value, axis, [(i, i ^ bit) for i in range(size)])


def my_bit(axis, bit):
    return (lax.axis_index(axis) // bit) % 2


def join(mine, other, side, axis):
    first = jnp.stack([mine, other], axis=axis)
    second = jnp.stack([other, mine], axis=axis)
    return jnp.where(side == 0, first, second)


def gather_sequence(tokens, also):
    sequences, rows, width = tokens.shape
    z2, z1, x = my_bit("blk", 4), my_bit("blk", 2), my_bit("blk", 1)
    y = my_bit("ulysses", 2)
    keep = lax.dynamic_index_in_dim(tokens, z2, 0, keepdims=False)
    give = lax.dynamic_index_in_dim(tokens, 1 - z2, 0, keepdims=False)
    near = join(keep, swap(keep, "blk", 2), z1, 0)
    far = join(swap(give, "blk", 4), swap(give, "blk", 6), z1, 0)
    wide = join(near, far, z2, 0).reshape(2, 2, 2, rows // 2, width)
    part_a, part_b = wide[:, :, 0], wide[:, :, 1]
    from_a, from_b = swap(part_a, "blk", 1), swap(part_b, "ulysses", 2)
    part_a = join(part_a, from_a, x, 2)
    part_b = join(part_b, from_b, y, 2)
    from_a, from_b = swap(part_a, "ulysses", 2), swap(part_b, "blk", 1)
    part_a = join(part_a, from_a, y, 3)
    part_b = join(part_b, from_b, x, 2)
    wide = jnp.stack([part_a, part_b], axis=4).reshape(16 * rows, width)
    wide, also = lax.optimization_barrier((wide, also))
    return wide, swap(wide, "ulysses", 1), also


def halve(keep, got, axis, bit, dim):
    total = (keep.astype(F32) + got.astype(F32)).astype(BF)
    side = my_bit(axis, bit)
    keep = lax.dynamic_index_in_dim(total, side, dim, keepdims=False)
    give = lax.dynamic_index_in_dim(total, 1 - side, dim, keepdims=False)
    return keep, give


def turned_tables(rows):
    lane = jnp.arange(LANES, dtype=jnp.int32) % (HEAD // 2)
    frequency = THETA ** (-(lane.astype(F32) * 2.0) / HEAD)
    row = jnp.arange(rows, dtype=jnp.int32)
    half = rows // 2
    position = row % half // 64 * 128 + row // half * 64 + row % 64
    angles = position.astype(F32)[:, None] * frequency[None, :]
    return jnp.cos(angles), jnp.sin(angles)


def exchange(value):
    return lax.all_to_all(value, AXES, split_axis=0, concat_axis=0, tiled=True)


def owner_slot(sequence, head):
    return sequence * 16 + head // SHARE * (SHARE + 1) + head % SHARE


def turn(values):
    lane = lax.broadcasted_iota(jnp.int32, values.shape, 1) % HEAD
    return jnp.where(
        lane < HEAD // 2,
        -pltpu.roll(values, LANES - HEAD // 2, 1),
        pltpu.roll(values, HEAD // 2, 1),
    )


def side_by_side(left, right):
    return jnp.concatenate([left, right], axis=1)


def smem():
    return pl.BlockSpec(memory_space=pltpu.SMEM)


def project_kernel(
    core, mine, other, gain, weight, cosine, sine, hidden, queries, key_rows, value_rows
):
    def one(tokens, slot):
        normed, inverse = normalize(tokens[...].astype(F32))
        low = (normed * gain[...]).astype(BF)
        hidden[slot] = low
        qkv = jnp.dot(low, weight[:, : 3 * HEAD], preferred_element_type=F32).astype(BF)
        both = qkv[:, :LANES].astype(F32)
        both = (both * cosine[slot] + turn(both) * sine[slot]).astype(BF)
        queries[slot] = both[:, :HEAD] * BF(HEAD**-0.5)
        key_rows[slot] = both[:, HEAD:]
        value_rows[slot] = qkv[:, LANES:]

    one(mine, core[0])
    one(other, 1 - core[0])


def project(core, mine, other, gain, weight, cosine, sine):
    length, width = mine.shape
    by_row = pl.BlockSpec((BLOCK, width), lambda i: (i, 0))
    by_pair = lambda columns: pl.BlockSpec((2, BLOCK, columns), lambda i: (0, i, 0))
    whole = lambda shape: pl.BlockSpec(shape, lambda i: (0, 0))
    return pl.pallas_call(
        project_kernel,
        grid=(length // BLOCK,),
        in_specs=[
            smem(),
            by_row,
            by_row,
            whole((1, width)),
            whole(weight.shape),
            by_pair(LANES),
            by_pair(LANES),
        ],
        out_specs=[by_pair(width), by_pair(HEAD), by_pair(HEAD), by_pair(HEAD)],
        out_shape=[jax.ShapeDtypeStruct((2, length, width), BF)]
        + [jax.ShapeDtypeStruct((2, length, HEAD), BF)] * 3,
        name="project",
    )(core, mine, other, gain, weight, cosine, sine)


def attend_kernel(queries, key_rows, value_rows, weights, attn32, total, send):
    scores = lax.dot_general(
        queries[...], key_rows[...], BY_COLUMN, preferred_element_type=F32
    )
    top = jnp.max(scores, axis=-1, keepdims=True)
    expo = jnp.exp(scores - top)
    row_total = jnp.sum(expo, axis=-1, keepdims=True)
    low = expo.astype(BF)
    weights[...] = low
    mixed = jnp.dot(low, value_rows[...], preferred_element_type=F32) / row_total
    attn32[...] = mixed
    total[...] = row_total
    mixed = mixed.astype(BF)
    for i in range(BLOCK // 64):
        rows = mixed[64 * i : 64 * i + 64]
        send[i, 0] = side_by_side(rows[:32], rows[32:])


def attend(queries, key_rows, value_rows):
    length = queries.shape[0]
    by_row = lambda columns: pl.BlockSpec((BLOCK, columns), lambda i: (i, 0))
    whole = pl.BlockSpec((length, HEAD), lambda i: (0, 0))
    steps = length // BLOCK
    return pl.pallas_call(
        attend_kernel,
        grid=(steps,),
        in_specs=[by_row(HEAD), whole, whole],
        out_specs=[
            by_row(length),
            by_row(HEAD),
            by_row(1),
            pl.BlockSpec(
                (BLOCK // 64, 1, 32, LANES), lambda i: (i % (steps // 2), i // (steps // 2), 0, 0)
            ),
        ],
        out_shape=[
            jax.ShapeDtypeStruct((length, length), BF),
            jax.ShapeDtypeStruct((length, HEAD), F32),
            jax.ShapeDtypeStruct((length, 1), F32),
            jax.ShapeDtypeStruct((length // 128, 2, 32, LANES), BF),
        ],
        cost_estimate=pl.CostEstimate(
            flops=4 * length * length * HEAD * 4,
            bytes_accessed=2 * length * length,
            transcendentals=length * length,
        ),
        name="attend",
    )(queries, key_rows, value_rows)


def middle_kernel(
    got, tokens, late, gain, grad_out, layer_output, send, acts, grad_middle
):
    width = tokens.shape[1]
    hidden_units = (late.shape[1] - width) // 3
    cut = 2 * hidden_units
    attn, hidden = acts.at[:, :width], acts.at[:, width : 2 * width]
    acts[:, 2 * width : 3 * width] = grad_out[...]
    grad_joint = acts.at[:, 3 * width : 3 * width + cut]
    activation = acts.at[:, 3 * width + cut : 3 * width + cut + hidden_units]
    branch = acts.at[:, 3 * width + cut + hidden_units :]
    for s in range(2):
        for h in range(0, HEADS, 2):
            left, right = got[owner_slot(s, h)], got[owner_slot(s, h + 1)]
            columns = slice(h * HEAD, h * HEAD + LANES)
            attn[64 * s : 64 * s + 32, columns] = side_by_side(left[:, :HEAD], right[:, :HEAD])
            attn[64 * s + 32 : 64 * s + 64, columns] = side_by_side(
                left[:, HEAD:], right[:, HEAD:]
            )
    attn_weight = late[:, cut : cut + width]
    middle = tokens[...].astype(F32) + jnp.dot(
        attn[...], attn_weight, preferred_element_type=F32
    )
    normed, inverse = normalize(middle)
    low = (normed * gain[...]).astype(BF)
    hidden[...] = low
    first = jnp.dot(low, late[:, :hidden_units], preferred_element_type=F32)
    gate = jnp.dot(low, late[:, hidden_units:cut], preferred_element_type=F32)
    cumulative = 0.5 * (1.0 + lax.erf(first * (0.5**0.5)))
    bent = first * cumulative
    active = (bent * gate).astype(BF)
    activation[...] = active
    out_weight = late[:, cut + width :]
    layer_output[...] = (
        middle + lax.dot_general(active, out_weight, BY_COLUMN, preferred_element_type=F32)
    ).astype(BF)
    grad_act = jnp.dot(grad_out[...], out_weight, preferred_element_type=F32)
    density = jnp.exp(-0.5 * first * first) * 0.3989422804014327
    grad_joint[:, :hidden_units] = (grad_act * gate * (cumulative + first * density)).astype(BF)
    grad_joint[:, hidden_units:] = (grad_act * bent).astype(BF)
    grad_hidden = lax.dot_general(
        grad_joint[...], late[:, :cut], BY_COLUMN, preferred_element_type=F32
    )
    total = grad_out[...].astype(F32) + norm_back(grad_hidden * gain[...], normed, inverse)
    grad_middle[...] = total
    branch_low = total.astype(BF)
    branch[...] = branch_low
    grad_cat = lax.dot_general(
        branch_low, attn_weight, BY_COLUMN, preferred_element_type=F32
    ).astype(BF)
    for s in range(2):
        for h in range(HEADS):
            rows = grad_cat[64 * s : 64 * s + 64, h * HEAD : (h + 1) * HEAD]
            block = side_by_side(rows[:32], rows[32:])
            send[owner_slot(s, h)] = block
            if h % SHARE == SHARE - 1:
                send[owner_slot(s, h) + 1] = block


def middle_part(got, tokens, late, gain, grad_out):
    rows, width = tokens.shape
    hidden_units = (late.shape[1] - width) // 3
    shapes = [
        ((rows, width), BF),
        (got.shape, BF),
        ((rows, 4 * width + 3 * hidden_units), BF),
        ((rows, width), F32),
    ]
    return pl.pallas_call(
        middle_kernel,
        out_shape=[jax.ShapeDtypeStruct(shape, kind) for shape, kind in shapes],
        name="middle_part",
    )(got, tokens, late, gain, grad_out)


def weight_grads_kernel(
    place, acts, acts_too, keep_a, give_a, keep_b, give_b, total, turned, *, width, hidden_units
):
    x, y, core = place[0], place[1], place[2]
    rows = acts.shape[0]
    cut = 3 * width + 2 * hidden_units

    def turn_rows(i):
        columns = slice(i * width, (i + 1) * width)
        turned[:, :rows] = jnp.transpose(acts[:, columns])
        turned[:, rows:] = jnp.transpose(acts_too[:, columns])

    def multiply(start, count):
        right = jnp.concatenate(
            [acts[:, start : start + count], acts_too[:, start : start + count]], axis=0
        )
        product = jnp.dot(turned[...], right, preferred_element_type=F32)
        total[..., :count] = product.reshape(*total.shape[:-1], count)

    turn_rows(1)
    for i in range(2 * hidden_units // TILE):
        columns = slice(i * TILE, (i + 1) * TILE)
        multiply(3 * width + i * TILE, TILE)
        keep_a[..., columns] = total[:, x, :, core].astype(BF)
        give_a[..., columns] = total[:, 1 - x, :, core].astype(BF)
    turn_rows(0)
    for i in range((width + hidden_units) // TILE):
        columns = slice(i * TILE, (i + 1) * TILE)
        if i == width // TILE:
            turn_rows(2)
        if i < width // TILE:
            multiply(cut + hidden_units + i * TILE, TILE)
        else:
            multiply(cut - width + i * TILE, TILE)
        keep_b[..., columns] = total[:, :, y, core].astype(BF)
        give_b[..., columns] = total[:, :, 1 - y, core].astype(BF)


def weight_grads(place, acts, acts_too, width, hidden_units, rows_here):
    rows = acts.shape[0]
    zs = width // (8 * rows_here)
    shape = lambda columns: jax.ShapeDtypeStruct((zs, 2, rows_here, columns), BF)
    columns = 3 * hidden_units + width
    return pl.pallas_call(
        functools.partial(weight_grads_kernel, width=width, hidden_units=hidden_units),
        in_specs=[smem()] + [pl.BlockSpec(memory_space=pltpu.VMEM)] * 2,
        out_shape=[shape(2 * hidden_units)] * 2 + [shape(width + hidden_units)] * 2,
        scratch_shapes=[
            pltpu.VMEM((zs, 2, 2, 2, rows_here, TILE), F32),
            pltpu.VMEM((width, 2 * rows), BF),
        ],
        cost_estimate=pl.CostEstimate(
            flops=4 * rows * width * columns,
            bytes_accessed=4 * acts.size + 2 * width * columns,
            transcendentals=0,
        ),
        name="weight_grads",
    )(place, acts, acts_too)


def attend_back_kernel(
    got, attn32, total, weights, queries, key_rows, value_rows, cosine, sine, hidden, send,
    grad_query, grad_key, grad_value, held, copied
):
    step = pl.program_id(0)
    copy = pltpu.make_async_copy(hidden, held, copied)

    @pl.when(step == 0)
    def _():
        copy.start()
        grad_key[...] = jnp.zeros_like(grad_key)
        grad_value[...] = jnp.zeros_like(grad_value)

    pieces = []
    for i in range(BLOCK // 64):
        block = got[i, 0]
        pieces += [block[:, :HEAD], block[:, HEAD:]]
    grad = jnp.concatenate(pieces, axis=0)
    wide = grad.astype(F32)
    dots = jnp.sum(wide * attn32[...], axis=-1, keepdims=True)
    grad_probs = lax.dot_general(
        grad, value_rows[...], BY_COLUMN, preferred_element_type=F32
    )
    inverse = 1.0 / total[...]
    low = weights[...]
    grad_scores = ((low.astype(F32) * inverse) * (grad_probs - dots)).astype(BF)
    grad_query[pl.ds(step * BLOCK, BLOCK), :] = HEAD**-0.5 * jnp.dot(
        grad_scores, key_rows[...], preferred_element_type=F32
    )
    grad_value[...] += lax.dot_general(
        (wide * inverse).astype(BF), low, BY_ROW, preferred_element_type=F32
    )
    grad_key[...] += lax.dot_general(
        queries[...], grad_scores, BY_ROW, preferred_element_type=F32
    )

    @pl.when(step == pl.num_programs(0) - 1)
    def _():
        length = grad_query.shape[0]
        both = side_by_side(grad_query[...], jnp.transpose(grad_key[...]))
        both = (both * cosine[...] - turn(both) * sine[...]).astype(BF)
        low = jnp.transpose(grad_value[...]).astype(BF)
        copy.wait()
        head_grad = jnp.transpose(
            lax.dot_general(
                side_by_side(both, low), held[...], BY_ROW, preferred_element_type=F32
            )
        )
        for i in range(length // 64):
            rows = head_grad[24 * i : 24 * i + 24].astype(BF)
            send[i // 2, i % 2, 96:120] = rows[:, :LANES]
            send[i // 2, i % 2, 120:136, :HEAD] = rows[:16, LANES:]
            send[i // 2, i % 2, 120:128, HEAD:] = rows[16:, LANES:]
        for i in range(length // 64):
            core, pair = i // (length // 128), i % (length // 128)
            rows = low[64 * i : 64 * i + 64]
            send[pair, core, :64] = both[64 * i : 64 * i + 64]
            send[pair, core, 64:96] = side_by_side(rows[:32], rows[32:])


def attend_back(
    got, attn32, total, weights, queries, key_rows, value_rows, cosine, sine, hidden
):
    length = queries.shape[0]
    steps = length // BLOCK
    by_row = lambda columns: pl.BlockSpec((BLOCK, columns), lambda i: (i, 0))
    whole = lambda *shape: pl.BlockSpec(shape, lambda i: (0,) * len(shape))
    send = (length // 128, 2, SENT, LANES)
    return pl.pallas_call(
        attend_back_kernel,
        grid=(steps,),
        in_specs=[
            pl.BlockSpec(
                (BLOCK // 64, 1, 32, LANES), lambda i: (i % (steps // 2), i // (steps // 2), 0, 0)
            ),
            by_row(HEAD),
            by_row(1),
            by_row(length),
            by_row(HEAD),
            whole(length, HEAD),
            whole(length, HEAD),
            whole(length, LANES),
            whole(length, LANES),
            pl.BlockSpec(memory_space=pl.ANY),
        ],
        out_specs=whole(*send),
        out_shape=jax.ShapeDtypeStruct(send, BF),
        scratch_shapes=[pltpu.VMEM((length, HEAD), F32)]
        + [pltpu.VMEM((HEAD, length), F32)] * 2
        + [pltpu.VMEM(hidden.shape, BF), pltpu.SemaphoreType.DMA],
        cost_estimate=pl.CostEstimate(
            flops=14 * length * length * HEAD * 4,
            bytes_accessed=2 * length * length,
            transcendentals=0,
        ),
        name="attend_back",
    )(got, attn32, total, weights, queries, key_rows, value_rows, cosine, sine, hidden)


def last_kernel(
    got, weight, tokens, gain, grad_middle, own_weight, own_gain, result, grad_weight, gain_grad,
    grads
):
    width = tokens.shape[1]
    place = lambda j, h: slice(j * width + h * HEAD, j * width + h * HEAD + LANES)
    for s in range(2):
        for h in range(0, HEADS, 2):
            left, right = got[owner_slot(s, h)], got[owner_slot(s, h + 1)]
            top = slice(64 * s, 64 * s + 64)
            grads[top, place(0, h)] = side_by_side(left[:64, :HEAD], right[:64, :HEAD])
            grads[top, place(1, h)] = side_by_side(left[:64, HEAD:], right[:64, HEAD:])
            grads[64 * s : 64 * s + 32, place(2, h)] = side_by_side(
                left[64:96, :HEAD], right[64:96, :HEAD]
            )
            grads[64 * s + 32 : 64 * s + 64, place(2, h)] = side_by_side(
                left[64:96, HEAD:], right[64:96, HEAD:]
            )
    grad_hidden = lax.dot_general(
        grads[...], weight[...], BY_COLUMN, preferred_element_type=F32
    )
    normed, inverse = normalize(tokens[...].astype(F32))
    result[...] = (
        grad_middle[...] + norm_back(grad_hidden * gain[...], normed, inverse)
    ).astype(BF)

    def both(head, rows):
        return (
            got[owner_slot(0, head), rows].astype(F32) + got[owner_slot(1, head), rows].astype(F32)
        )

    for h in range(0, HEADS, 2):
        left, right = both(h, slice(96, 120)), both(h + 1, slice(96, 120))
        grad_weight[:, place(0, h)] = side_by_side(left[:, :HEAD], right[:, :HEAD])
        grad_weight[:, place(1, h)] = side_by_side(left[:, HEAD:], right[:, HEAD:])
        left, right = both(h, slice(120, 136)), both(h + 1, slice(120, 136))
        grad_weight[:16, place(2, h)] = side_by_side(left[:, :HEAD], right[:, :HEAD])
        grad_weight[16:, place(2, h)] = side_by_side(left[:8, HEAD:], right[:8, HEAD:])
    sums = jnp.sum(grad_weight[...] * own_weight[...].astype(F32), axis=1, keepdims=True)
    sums = jnp.transpose(jnp.broadcast_to(sums, (sums.shape[0], LANES)))[:8]
    gain_grad[...] = (sums / own_gain[...])[0]


def last_part(got, weight, tokens, gain, grad_middle, own_weight, own_gain):
    return pl.pallas_call(
        last_kernel,
        out_shape=[
            jax.ShapeDtypeStruct(tokens.shape, BF),
            jax.ShapeDtypeStruct(own_weight.shape, F32),
            jax.ShapeDtypeStruct((own_weight.shape[0],), F32),
        ],
        scratch_shapes=[pltpu.VMEM((tokens.shape[0], weight.shape[1]), BF)],
        name="last_part",
    )(got, weight, tokens, gain, grad_middle, own_weight, own_gain)


def owner_body(
    tokens, attn_gain, qkv_weight, attn_out_weight, mlp_gain, in_weight, out_weight, cotangent
):
    sequences, per_device, model_width = tokens.shape
    hidden_units = out_weight.shape[0]
    rows_here = qkv_weight.shape[0]
    rows = sequences * per_device
    length = per_device * 32
    core = my_bit("ulysses", 1).astype(jnp.int32).reshape(1)
    place = jnp.stack([my_bit("blk", 1), my_bit("ulysses", 2), my_bit("ulysses", 1)])
    place = place.astype(jnp.int32)
    late = jnp.concatenate([in_weight, attn_out_weight, jnp.transpose(out_weight)], axis=1)
    late_full = lax.all_gather(late, AXES, axis=0, tiled=True)
    by_head = qkv_weight.reshape(rows_here, 3, HEADS, HEAD).transpose(2, 0, 1, 3)
    by_head = by_head.reshape(HEADS, rows_here, 3 * HEAD)
    gains = jnp.stack([attn_gain, mlp_gain], axis=1)
    gains = jnp.broadcast_to(jnp.pad(gains, ((0, 0), (0, HEAD - 2))), (HEADS, rows_here, HEAD))
    packed = jnp.concatenate([by_head, gains], axis=2)
    packed = packed.reshape(HEADS // SHARE, SHARE, rows_here, 4 * HEAD)
    packed = jnp.concatenate([packed, packed[:, -1:]], axis=1)
    packed = jnp.broadcast_to(packed[None], (2,) + packed.shape)
    mixed = exchange(packed.reshape(32, rows_here, 4 * HEAD))
    mine, other, (mixed, cosine, sine) = gather_sequence(tokens, (mixed, *turned_tables(length)))
    weight_here = mixed.reshape(model_width, 4 * HEAD)
    gain_one = weight_here[:, 3 * HEAD].reshape(1, model_width).astype(F32)
    gain_two = weight_here[:, 3 * HEAD + 1].reshape(1, model_width).astype(F32)
    hidden_one, queries, key_rows, value_rows = project(
        core,
        mine,
        other,
        gain_one,
        weight_here,
        cosine.reshape(2, length // 2, LANES),
        sine.reshape(2, length // 2, LANES),
    )
    queries, key_rows, value_rows = (
        value.reshape(length, HEAD) for value in (queries, key_rows, value_rows)
    )
    weights_low, attn32, row_total, send = attend(queries, key_rows, value_rows)
    got = exchange(send.reshape(32, 32, LANES))
    flat_tokens = tokens.reshape(rows, model_width)
    grad_out = cotangent.reshape(rows, model_width)
    layer_output, send, acts, grad_middle = middle_part(
        got, flat_tokens, late_full, gain_two, grad_out
    )
    got = exchange(send)
    acts_too = swap(acts, "ulysses", 1)
    parts = weight_grads(place, acts, acts_too, model_width, hidden_units, rows_here)
    got, parts = lax.optimization_barrier((got, parts))
    keep_a, give_a, keep_b, give_b = (
        part.reshape(2, 2, *part.shape[1:]) for part in parts
    )
    came_a, came_b = swap(give_a, "blk", 1), swap(give_b, "ulysses", 2)
    send = attend_back(
        got.reshape(length // 128, 2, 32, LANES),
        attn32,
        row_total,
        weights_low,
        queries,
        key_rows,
        value_rows,
        cosine,
        sine,
        hidden_one.reshape(length, model_width),
    )
    qkv_full = lax.all_gather(qkv_weight, AXES, axis=0, tiled=True)
    send, came_b = lax.optimization_barrier((send, came_b))
    got = exchange(send.reshape(32, SENT, LANES))
    keep_a, give_a = halve(keep_a, came_a, "ulysses", 2, 2)
    keep_b, give_b = halve(keep_b, came_b, "blk", 1, 2)
    came_a, came_b = swap(give_a, "ulysses", 2), swap(give_b, "blk", 1)
    z = lax.axis_index("blk") // 2

    def spread(keep, came):
        total = (keep.astype(F32) + came.astype(F32)).astype(BF).reshape(4, rows_here, -1)
        row = lambda owner: lax.dynamic_index_in_dim(total, owner, 0, keepdims=False)
        return [row(z)] + [swap(row(z ^ k), "blk", 2 * k) for k in (2, 3, 1)]

    parts_a = spread(keep_a, came_a)
    came_b, qkv_full = lax.optimization_barrier((came_b, qkv_full))
    parts_b = spread(keep_b, came_b)
    last = last_part(
        got,
        qkv_full,
        flat_tokens,
        gain_one,
        grad_middle,
        qkv_weight,
        attn_gain.astype(F32).reshape(1, rows_here),
    )
    (input_grad, shard_qkv, shard_one), parts_a, parts_b = lax.optimization_barrier(
        (last, parts_a, parts_b)
    )
    input_grad = input_grad.reshape(sequences, per_device, model_width)
    shard_in = sum(part.astype(F32) for part in parts_a)
    shards = sum(part.astype(F32) for part in parts_b)
    shard_attn = shards[:, :model_width]
    shard_out = jnp.transpose(shards[:, model_width:])
    shard_two = jnp.sum(shard_in * in_weight.astype(F32), axis=1) / mlp_gain.astype(F32)
    return (
        layer_output.reshape(sequences, per_device, model_width),
        input_grad,
        shard_one,
        shard_qkv,
        shard_attn,
        shard_two,
        shard_in,
        shard_out,
    )


def solution(mesh):
    placed = (
        P(None, ("blk", "ulysses"), None),
        P(("blk", "ulysses")),
        P(("blk", "ulysses"), None),
        P(("blk", "ulysses"), None),
        P(("blk", "ulysses")),
        P(("blk", "ulysses"), None),
        P(None, ("blk", "ulysses")),
        P(None, ("blk", "ulysses"), None),
    )
    sizes = (mesh.shape["blk"], mesh.shape["ulysses"])
    return jax.shard_map(
        owner_body if sizes == (8, 4) else ring_body,
        mesh=mesh,
        in_specs=placed,
        out_specs=(
            P(None, ("blk", "ulysses"), None),
            P(None, ("blk", "ulysses"), None),
            P(("blk", "ulysses")),
            P(("blk", "ulysses"), None),
            P(("blk", "ulysses"), None),
            P(("blk", "ulysses")),
            P(("blk", "ulysses"), None),
            P(None, ("blk", "ulysses")),
        ),
        check_vma=False,
    )
```
